32 devices in a mesh: fsdp: 2 (over x), seq: 16 (over z, y, core).
Axes of the slice: x: 2, y: 2, z: 4, core: 2. Of those that a mesh axis runs over, the one named last changes fastest.
Arguments:
- tokens: bfloat16 [16384, 1152], P(('fsdp', 'seq')), may hold values from -16 to 16
- qkv_weight: bfloat16 [2, 1152, 3456], P(None, ('fsdp', 'seq')), may hold values from -0.1875 to 0.1875
- out_weight: bfloat16 [2, 1152, 1152], P(None, ('fsdp', 'seq')), may hold values from -1 to 1
- up_weight: bfloat16 [2, 1152, 4608], P(None, ('fsdp', 'seq')), may hold values from -0.1875 to 0.1875
- down_weight: bfloat16 [2, 4608, 1152], P(None, ('fsdp', 'seq')), may hold values from -0.09375 to 0.09375
- mod_weight: bfloat16 [2, 1152, 6912], P(None, ('fsdp', 'seq')), may hold values from -0.375 to 0.375
- qv_bias: bfloat16 [2, 2304], P(None, ('fsdp', 'seq')), may hold values from -3 to 3
- out_bias: bfloat16 [2, 1152], P(None, ('fsdp', 'seq')), may hold values from -3 to 3
- up_bias: bfloat16 [2, 4608], P(None, ('fsdp', 'seq')), may hold values from -3 to 3
- down_bias: bfloat16 [2, 1152], P(None, ('fsdp', 'seq')), may hold values from -3 to 3
- mod_bias: bfloat16 [2, 6912], P(None, ('fsdp', 'seq')), may hold values from -3 to 3
- row_items: int32 [16], P('seq'), may hold values from 1 to 4, as said below
- timesteps: int32 [16, 4], P('seq'), may hold values from 0 to 999
- head_mask: int32 [16, 2, 4, 16], P('seq'), may hold values 0 or 1
- channel_mask: int32 [16, 2, 4, 4608], P('seq'), may hold values 0 or 1
- token_keep: int32 [16384, 2], P(('fsdp', 'seq')), may hold values 0 or 1
- cotangent: float32 [16384, 1152], P(('fsdp', 'seq')), may hold values from -6 to 6
Outputs:
- output: bfloat16 [16384, 1152], P(('fsdp', 'seq'))
- grad_tokens: float32 [16384, 1152], P(('fsdp', 'seq'))
- grad_qkv_weight: float32 [2, 1152, 3456], P(None, ('fsdp', 'seq'))
- grad_out_weight: float32 [2, 1152, 1152], P(None, ('fsdp', 'seq'))
- grad_up_weight: float32 [2, 1152, 4608], P(None, ('fsdp', 'seq'))
- grad_down_weight: float32 [2, 4608, 1152], P(None, ('fsdp', 'seq'))
- grad_mod_weight: float32 [2, 1152, 6912], P(None, ('fsdp', 'seq'))
- grad_qv_bias: float32 [2, 2304], P(None, ('fsdp', 'seq'))
- grad_out_bias: float32 [2, 1152], P(None, ('fsdp', 'seq'))
- grad_up_bias: float32 [2, 4608], P(None, ('fsdp', 'seq'))
- grad_down_bias: float32 [2, 1152], P(None, ('fsdp', 'seq'))
- grad_mod_bias: float32 [2, 6912], P(None, ('fsdp', 'seq'))
The draws below stay inside these ranges and needn't reach their ends.
Inputs may be any that keep to these rules, and one draw needn't show every extreme that they name: `row_items`: each row holds 1 or 4 items, exactly half of the rows each. A row of one item uses only the first slot of timesteps, head_mask and channel_mask.
All inputs are finite; a program needn't handle non-finite values. No bound on the sum of `head_mask` or of `channel_mask` or of `token_keep` on one device may be relied on, other than what follows from the above.
Results may differ from the reference program's by a relative error of at most 0.018.
The reference program's roundings to bfloat16 on the way count: a program that leaves them out, or rounds other values in their place, can miss the bound.
Values may be sent and summed in bfloat16 or wider, within the bound.
No kernel may reach another device: no remote copies, remote signals or barrier semaphores. Data moves between devices by JAX's collectives and lax.ppermute only.
A program may use at most 448 MiB of HBM per device.

```python
import math
import jax
import jax.numpy as jnp
from jax import lax

D = 1152
HEADS = 16
FF = 4608
LAYERS = 2
ROW_LEN = 1024
ITEMS = 4
ROWS = 16
TOKENS = 16384


def draw_tokens(key, part):
    first_key, second_key, third_key = jax.random.split(key, 3)
    row_scale = 0.3 * jnp.exp(jax.random.uniform(second_key, (TOKENS, 1), jnp.float32, 0.0, math.log(10.0)))
    column_scale = 0.3 * jnp.exp(jax.random.uniform(third_key, (1, D), jnp.float32, 0.0, math.log(10.0)))
    values = jax.random.normal(first_key, (TOKENS, D), jnp.float32) * row_scale * column_scale
    return jnp.clip(values, -16.0, 16.0).astype(jnp.bfloat16)


def draw_row_items(key, part):
    order = jax.random.permutation(key, ROWS)
    return jnp.where(order < ROWS // 2, 1, ITEMS).astype(jnp.int32)


def touch_ends(values, rng, least, largest):
    longest = values.shape.index(max(values.shape))
    spots = []
    for shift in (0, 1):
        where = [jax.random.randint(jax.random.fold_in(rng, axis), (), 0, length) for axis, length in enumerate(values.shape)]
        where[longest] = (where[longest] + shift) % values.shape[longest]
        spots.append(tuple(where))
    return values.at[spots[0]].set(least).at[spots[1]].set(largest)


def block_scale(rng, dims, cuts, smallest, high):
    loudness = 1.0
    for dim, shards_of in cuts:
        draws = jax.random.uniform(jax.random.fold_in(jax.random.fold_in(rng, 6), dim), (shards_of,), jnp.float32, smallest / len(cuts), high / len(cuts))
        loudness = loudness * jnp.repeat(jnp.exp(draws), dims[dim] // shards_of).reshape((-1,) + (1,) * (len(dims) - 1 - dim))
    return loudness


def normal_values(own_key, dims, width, reach, shards=(), kind=jnp.bfloat16):
    array = width * jax.random.normal(own_key, dims, jnp.float32)
    if shards:
        array = array * block_scale(own_key, dims, shards, -0.22, 0.18)
    return jnp.clip(array, -reach, reach).astype(kind)


def setup_inputs(seed: int = 0) -> dict:
    keys = jax.random.split(jax.random.key(seed), 18)
    return {
        "tokens": draw_tokens(jax.random.fold_in(keys[17], 71), 0),
        "qkv_weight": normal_values(keys[1], (LAYERS, D, 3 * D), D ** -0.5, 0.1875, ((1, 32),)),
        "out_weight": normal_values(keys[2], (LAYERS, D, D), (D // 32) ** -0.5, 1.0, ((1, 32),)),
        "up_weight": normal_values(keys[3], (LAYERS, D, FF), D ** -0.5, 0.1875, ((1, 32),)),
        "down_weight": normal_values(keys[4], (LAYERS, FF, D), FF ** -0.5, 0.09375, ((1, 32),)),
        "mod_weight": normal_values(keys[5], (LAYERS, D, 6 * D), (D // 4) ** -0.5, 0.375, ((1, 32),)),
        "qv_bias": normal_values(keys[6], (LAYERS, 2 * D), 0.5, 3.0, ((1, 32),)),
        "out_bias": normal_values(keys[7], (LAYERS, D), 0.5, 3.0, ((1, 32),)),
        "up_bias": normal_values(keys[8], (LAYERS, FF), 0.5, 3.0, ((1, 32),)),
        "down_bias": normal_values(keys[9], (LAYERS, D), 0.5, 3.0, ((1, 32),)),
        "mod_bias": normal_values(keys[10], (LAYERS, 6 * D), 0.5, 3.0, ((1, 32),)),
        "row_items": draw_row_items(jax.random.fold_in(keys[17], 71), 0),
        "timesteps": touch_ends(jax.random.randint(keys[12], (ROWS, ITEMS), 0, 1000), jax.random.fold_in(keys[12], 1), 0, 999).astype(jnp.int32),
        "head_mask": touch_ends((jax.random.randint(keys[13], (ROWS, LAYERS, ITEMS, HEADS), 0, 4) < 3).astype(jnp.int32), jax.random.fold_in(keys[13], 1), 0, 1),
        "channel_mask": touch_ends((jax.random.randint(keys[14], (ROWS, LAYERS, ITEMS, FF), 0, 4) < 3).astype(jnp.int32), jax.random.fold_in(keys[14], 1), 0, 1),
        "token_keep": touch_ends((jax.random.randint(keys[15], (TOKENS, LAYERS), 0, 4) < 3).astype(jnp.int32), jax.random.fold_in(keys[15], 1), 0, 1),
        "cotangent": normal_values(keys[16], (TOKENS, D), 1.0, 6.0, ((0, 32),), jnp.float32),
    }


highest = lax.Precision.HIGHEST

@jax.custom_vjp
def low(v):
    return lax.optimization_barrier(v.astype(jnp.bfloat16)).astype(jnp.float32)

@jax.custom_vjp
def low_back(v):
    return v

def low_keep(v):
    return (low(v), None)

def low_pass(kept, grad):
    return (grad,)

def back_keep(v):
    return (v, None)

def back_low(kept, grad):
    return (low(grad),)
low.defvjp(low_keep, low_pass)
low_back.defvjp(back_keep, back_low)

def embed_steps(step_values, model_width):
    half_width = model_width // 2
    frequency = jnp.exp(-math.log(10000.0) * jnp.arange(half_width, dtype=jnp.float32) / half_width)
    angles = step_values.astype(jnp.float32)[:, None] * frequency[None, :]
    return jnp.concatenate([jnp.cos(angles), jnp.sin(angles)], axis=1)

def modulate(values, shift_part, scale_part):
    centered = values - lax.optimization_barrier(jnp.mean(values, axis=1, keepdims=True))
    spread = lax.optimization_barrier(jnp.mean(centered * centered, axis=1, keepdims=True))
    return centered * lax.rsqrt(spread + 1e-06) * (1.0 + scale_part) + shift_part

def matmul(left_side, right_side):
    return jnp.dot(left_side, right_side, precision=highest, preferred_element_type=jnp.float32)

def to_rows(flat, row_count, row_len):
    tail = flat.shape[1:]
    return jnp.swapaxes(flat.reshape((2, row_count, row_len // 2) + tail), 0, 1).reshape((row_count, row_len) + tail)

def from_rows(rowed, row_count, row_len):
    tail = rowed.shape[2:]
    return jnp.swapaxes(rowed.reshape((row_count, 2, row_len // 2) + tail), 0, 1).reshape((row_count * row_len,) + tail)

def layer_forward(layer_weights, inputs, token_item, same_item, cond_low, heads_on, channel_on, keep_col):
    qkv_weight, out_weight, up_weight, down_weight, mod_weight, qv_bias, out_bias, up_bias, down_bias, mod_bias = layer_weights
    model_width = out_weight.shape[1]
    head_count = heads_on.shape[1]
    head_size = model_width // head_count
    row_len = inputs.shape[0]
    modulation = matmul(cond_low, mod_weight) + mod_bias
    token_mod = modulation[token_item]
    shift_one, scale_one, gate_one, shift_two, scale_two, gate_two = jnp.split(token_mod, 6, axis=1)
    head_on_tok = heads_on.astype(jnp.float32)[token_item]
    channel_tok = channel_on.astype(jnp.float32)[token_item]
    keep_tok = keep_col.astype(jnp.float32)[:, None]
    low_one = low(modulate(inputs, shift_one, scale_one))
    bias_three = jnp.concatenate([qv_bias[:model_width], jnp.zeros((model_width,), jnp.float32), qv_bias[model_width:]])
    qkv_all = low(low_back(matmul(low_one, qkv_weight) + bias_three))
    query_heads = qkv_all[:, :model_width].reshape(row_len, head_count, head_size)
    key_heads = qkv_all[:, model_width:2 * model_width].reshape(row_len, head_count, head_size)
    value_heads = qkv_all[:, 2 * model_width:].reshape(row_len, head_count, head_size)
    raw = jnp.einsum('qhd,khd->hqk', query_heads, key_heads, precision=highest) * (1.0 / math.sqrt(head_size))
    scores = low_back(jnp.where(same_item[None], raw, -1e+30))
    probs = low(jax.nn.softmax(scores, axis=2))
    attended = jnp.einsum('hqk,khd->qhd', probs, value_heads, precision=highest)
    mixed = low(low_back((attended * head_on_tok[:, :, None]).reshape(row_len, model_width)))
    branch_one = low_back(matmul(mixed, out_weight) + out_bias)
    after_attn = inputs + gate_one * branch_one
    low_two = low(modulate(after_attn, shift_two, scale_two))
    hidden_pre = low_back(matmul(low_two, up_weight) + up_bias)
    hidden_low = low(jax.nn.gelu(hidden_pre, approximate=True) * channel_tok)
    branch_two = low_back(matmul(hidden_low, down_weight) + down_bias)
    return after_attn + keep_tok * gate_two * branch_two

def row_forward(weights, row_data):
    inputs, items_here, step_values, heads_on, channel_on, keep_row = row_data
    layer_count = weights[0].shape[0]
    model_width = weights[1].shape[2]
    row_len = inputs.shape[0]
    positions = jnp.arange(row_len, dtype=jnp.int32)
    token_item = positions * items_here // row_len
    same_item = token_item[:, None] == token_item[None, :]
    cond_low = low(jax.nn.silu(embed_steps(step_values, model_width)))
    current = inputs
    for layer in range(layer_count):
        layer_weights = tuple((matrix[layer] for matrix in weights))
        current = layer_forward(layer_weights, current, token_item, same_item, cond_low, heads_on[layer], channel_on[layer], keep_row[:, layer])
    return current

def reference(tokens, qkv_weight, out_weight, up_weight, down_weight, mod_weight, qv_bias, out_bias, up_bias, down_bias, mod_bias, row_items, timesteps, head_mask, channel_mask, token_keep, cotangent):
    inputs = to_rows(tokens.astype(jnp.float32), ROWS, ROW_LEN)
    weights = jax.tree.map(lambda matrix: matrix.astype(jnp.float32), (qkv_weight, out_weight, up_weight, down_weight, mod_weight, qv_bias, out_bias, up_bias, down_bias, mod_bias))
    keep_rows = to_rows(token_keep, ROWS, ROW_LEN)

    def forward(inputs_f, weights_f):

        def one_row(row_data):
            return row_forward(weights_f, row_data)
        return lax.map(jax.checkpoint(one_row), (inputs_f, row_items, timesteps, head_mask, channel_mask, keep_rows))
    result, pullback = jax.vjp(forward, inputs, weights)
    grad_inputs, grad_weights = pullback(to_rows(cotangent, ROWS, ROW_LEN))
    return (from_rows(result, ROWS, ROW_LEN).astype(jnp.bfloat16), from_rows(grad_inputs, ROWS, ROW_LEN), grad_weights[0], grad_weights[1], grad_weights[2], grad_weights[3], grad_weights[4], grad_weights[5], grad_weights[6], grad_weights[7], grad_weights[8], grad_weights[9])
```

```python
import math

import jax
import jax.numpy as jnp
from jax import lax
from jax.experimental import pallas as pl
from jax.experimental.pallas import tpu as pltpu
from jax.sharding import PartitionSpec as P

BF = jnp.bfloat16
F32 = jnp.float32
AXES = ("fsdp", "seq")


def swap_bit(block, stage):
    axis, bit = stage
    count = lax.axis_size(axis)
    return lax.ppermute(block, axis, [(low, low ^ (1 << bit)) for low in range(count)])


def stage_bit(stage):
    axis, bit = stage
    return (lax.axis_index(axis) >> bit) & 1


def contract(left, right, left_dim, right_dim):
    return lax.dot_general(
        left, right, (((left_dim,), (right_dim,)), ((), ())), preferred_element_type=F32
    )


def relative_masks(stages, mask_of):
    masks = [0]
    for stage in reversed(stages):
        masks = masks + [mask ^ mask_of(stage) for mask in masks]
    return masks


class Feed:
    def __init__(self):
        self.flights = []
        self.ticks = 0
        self.later = {}

    def start(self, flight):
        wait, parts = next(flight)
        self.flights.append((flight, self.ticks + wait - 1, parts))

    def at(self, tick, flight):
        self.later.setdefault(tick, []).append(flight)

    def tick(self, value):
        for flight in self.later.pop(self.ticks, []):
            self.start(flight)
        due = [entry for entry in self.flights if entry[1] <= self.ticks]
        flying = [entry for entry in self.flights if entry[1] > self.ticks]
        self.ticks += 1
        value, arrived = lax.optimization_barrier((value, [parts for _, _, parts in due]))
        for (flight, _, _), parts in zip(due, arrived):
            try:
                wait, sent = flight.send(parts)
                flying.append((flight, self.ticks + wait - 1, sent))
            except StopIteration:
                pass
        self.flights = flying
        return value

    def until(self, result, value):
        while not result:
            value = self.tick(value)
        return value

    def finish(self, value):
        while self.flights or self.later:
            value = self.tick(value)
        return value


def reduce_flight(away, stay, right, side, routes, cuts, rows, waits, result):
    core_stage, first_route, second_route, far_stages = routes
    first, second = cuts
    arrived = yield waits[0], swap_bit(contract(away, right, side, 0).astype(BF), core_stage)
    kept, first_sent, second_sent = keep_grad(stay, right, side, arrived, first, second)
    first_arrived, second_arrived = yield waits[1], (
        swap_bit(first_sent, first_route[0]),
        swap_bit(second_sent, second_route[0]),
    )

    def add(left, other, low, high):
        return left[low:high].astype(F32) + other[low:high].astype(F32)

    first_kept, second_kept = kept[:first], kept[first:]
    half_first, half_second = first // 2, second // 2
    first_sent = add(first_kept, first_arrived, half_first, first).astype(BF)
    second_sent = add(second_kept, second_arrived, half_second, second).astype(BF)
    first_kept = add(first_kept, first_arrived, 0, half_first).astype(BF)
    second_kept = add(second_kept, second_arrived, 0, half_second).astype(BF)
    first_arrived, second_arrived = yield waits[2], (
        swap_bit(first_sent, first_route[1]),
        swap_bit(second_sent, second_route[1]),
    )
    for index, stage in enumerate(far_stages):
        first, second = half_first, half_second
        half_first, half_second = first // 2, second // 2
        sent = jnp.concatenate(
            [
                add(first_kept, first_arrived, half_first, first),
                add(second_kept, second_arrived, half_second, second),
            ],
            axis=0,
        ).astype(BF)
        first_kept = add(first_kept, first_arrived, 0, half_first).astype(BF)
        second_kept = add(second_kept, second_arrived, 0, half_second).astype(BF)
        arrived = yield 1, swap_bit(sent, stage)
        first_arrived, second_arrived = arrived[:half_first], arrived[half_first:]
    block = jnp.concatenate(
        [
            add(first_kept, first_arrived, 0, half_first),
            add(second_kept, second_arrived, 0, half_second),
        ],
        axis=0,
    )
    result.append(block[:rows])


def wide_tile(columns):
    return next(tile for tile in (1536, 1152, 768, 512, 384, 256, 128) if columns % tile == 0)


def keep_grad(left, right, side, arrived, first, second):
    half = first + second
    tokens, columns = right.shape
    tile = wide_tile(columns)

    def kernel(left_ref, right_ref, arrived_ref, kept_ref, first_ref, second_ref, *scratch):
        if side == 0:
            turned_ref = scratch[0]

            @pl.when(pl.program_id(0) == 0)
            def _():
                turned_ref[...] = left_ref[...].astype(F32).T.astype(BF)

        else:
            turned_ref = left_ref
        total = jnp.dot(turned_ref[...], right_ref[...], preferred_element_type=F32)
        total = (total + arrived_ref[...].astype(F32)).astype(BF)
        kept_ref[...] = total[:half]
        first_ref[...] = total[half : half + first]
        second_ref[...] = total[half + first :]

    outs = [jax.ShapeDtypeStruct((count, columns), BF) for count in (half, first, second)]
    return pl.pallas_call(
        kernel,
        out_shape=outs,
        grid=(columns // tile,),
        in_specs=[
            pl.BlockSpec(left.shape, lambda j: (0, 0)),
            pl.BlockSpec((tokens, tile), lambda j: (0, j)),
            pl.BlockSpec((2 * half, tile), lambda j: (0, j)),
        ],
        out_specs=[
            pl.BlockSpec((count, tile), lambda j: (0, j)) for count in (half, first, second)
        ],
        scratch_shapes=[pltpu.VMEM((2 * half, tokens), BF)] if side == 0 else [],
        cost_estimate=cost(4 * half * tokens * columns, [left, right, arrived, *outs]),
        name="keep_grad",
    )(left, right, arrived)


def modulation_flight(block, bias, stages, result):
    for stage in stages[:-1]:
        half = block.shape[0] // 2
        arrived = yield 1, swap_bit(block[half:], stage)
        block = block[:half] + arrived
    arrived = yield 1, swap_bit(block, stages[-1])
    result.append(block + arrived + bias[None])


def gather_flight(shard, cut, routes, waits, result):
    core_stage, first_route, second_route, far_stages = routes
    waits = [1] * (len(far_stages) - 2) + list(waits)
    shard = yield 1, shard
    blocks = [shard]
    for stage in reversed(far_stages):
        sent = jnp.concatenate(blocks, axis=0) if len(blocks) > 1 else blocks[0]
        arrived = yield waits.pop(0), swap_bit(sent, stage)
        rows = shard.shape[0]
        blocks = blocks + [
            arrived[start : start + rows] for start in range(0, arrived.shape[0], rows)
        ]
    owned = [
        jnp.concatenate([block[:cut] for block in blocks], axis=0),
        jnp.concatenate([block[cut:] for block in blocks], axis=0),
    ]
    routes = (second_route, first_route)
    arrived = yield (
        waits.pop(0),
        [swap_bit(part, route[0]) for part, route in zip(owned, routes)],
    )
    pairs = [jnp.concatenate([part, more], axis=0) for part, more in zip(owned, arrived)]
    fars = yield waits.pop(0), [swap_bit(pair, route[1]) for pair, route in zip(pairs, routes)]
    others = yield (
        waits.pop(0),
        [[swap_bit(pair, core_stage), swap_bit(far, core_stage)] for pair, far in zip(pairs, fars)],
    )
    for pair, far, other in zip(pairs, fars, others):
        result.append((pair, far, other[0], other[1]))


def take_chunks(left, places, chunk_rows):
    far_count = places.shape[0] - 3
    columns = left.shape[1]
    part_rows = chunk_rows // 2

    def take(places_ref, in_ref, stay_ref, away_ref):
        x_here, y_here, core_here = places_ref[0], places_ref[1], places_ref[2]
        for half in range(2):
            for one in range(2):
                for two in range(2):
                    x_place = jnp.bitwise_xor(x_here, two if half else one)
                    y_place = jnp.bitwise_xor(y_here, one if half else two)
                    stay_ref[two, half, one, 0] = in_ref[x_place, 0, y_place, core_here, half]
                    away_ref[two, half, one, 0] = in_ref[x_place, 0, y_place, 1 - core_here, half]

    shape = (2, 2, 2, far_count, part_rows, columns)
    out_spec = pl.BlockSpec(
        (2, 2, 2, 1, part_rows, columns), lambda i, places: (0, 0, 0, i, 0, 0)
    )
    parts = pl.pallas_call(
        take,
        out_shape=[jax.ShapeDtypeStruct(shape, left.dtype)] * 2,
        grid_spec=pltpu.PrefetchScalarGridSpec(
            num_scalar_prefetch=1,
            grid=(far_count,),
            in_specs=[
                pl.BlockSpec(
                    (2, 1, 2, 2, 2, part_rows, columns),
                    lambda i, places: (0, places[3 + i], 0, 0, 0, 0, 0),
                )
            ],
            out_specs=[out_spec, out_spec],
        ),
        cost_estimate=pl.CostEstimate(
            flops=0, bytes_accessed=4 * left.size, transcendentals=0
        ),
        name="take_chunks",
    )(places, left.reshape(2, far_count, 2, 2, 2, part_rows, columns))
    return [part.reshape(left.shape[0] // 2, columns) for part in parts]


def place_chunks(first, second, places, out_shape):
    far_count = places.shape[0] - 3
    columns = out_shape[1]
    rows = first[0].shape[0] // (2 * far_count)
    pieces = [piece.reshape(2, far_count, rows, columns) for piece in (*first, *second)]

    def place(places_ref, *refs):
        out_ref = refs[-1]
        x_here, y_here, core_here = places_ref[0], places_ref[1], places_ref[2]
        for half in range(2):
            for core in range(2):
                for two in range(2):
                    ref = refs[4 * half + 2 * core + two]
                    for one in range(2):
                        x_place = jnp.bitwise_xor(x_here, two if half else one)
                        y_place = jnp.bitwise_xor(y_here, one if half else two)
                        core_place = jnp.bitwise_xor(core_here, core)
                        out_ref[x_place, 0, y_place, core_place, half] = ref[one, 0]

    in_spec = pl.BlockSpec((2, 1, rows, columns), lambda i, places: (0, i, 0, 0))
    view = (2, far_count, 2, 2, 2, rows, columns)
    return pl.pallas_call(
        place,
        out_shape=jax.ShapeDtypeStruct(view, BF),
        grid_spec=pltpu.PrefetchScalarGridSpec(
            num_scalar_prefetch=1,
            grid=(far_count,),
            in_specs=[in_spec] * 8,
            out_specs=pl.BlockSpec(
                (2, 1, 2, 2, 2, rows, columns), lambda i, places: (0, places[3 + i], 0, 0, 0, 0, 0)
            ),
        ),
        cost_estimate=pl.CostEstimate(
            flops=0, bytes_accessed=4 * out_shape[0] * columns, transcendentals=0
        ),
        name="place_chunks",
    )(places, *pieces).reshape(out_shape)


class Tiles:
    def __init__(self, parts, tile, start, count):
        first, second = parts
        self.pieces = [piece for pair in zip(first, second) for piece in pair]
        self.tile, self.start, self.count = tile, start, count
        self.rows = sum(piece.shape[0] for piece in self.pieces)

    def operands(self):
        return list(self.pieces)

    def specs(self):
        return [
            pl.BlockSpec((piece.shape[0], self.tile), lambda j: (0, self.start + j))
            for piece in self.pieces
        ]

    def weight(self, refs):
        return jnp.concatenate([ref[...] for ref in refs[:8]], axis=0)

    def columns(self):
        return self.count * self.tile


def cost(flops, arrays, transcendentals=0):
    return pl.CostEstimate(
        flops=int(flops),
        bytes_accessed=int(sum(array.size * array.dtype.itemsize for array in arrays)),
        transcendentals=int(transcendentals),
    )


def project(left, tiles, bias, out_dtype, name):
    rows = left.shape[0]
    operands = tiles.operands()

    def kernel(left_ref, bias_ref, *refs):
        out_ref = refs[-1]

        total = jnp.dot(left_ref[...], tiles.weight(refs), preferred_element_type=F32)
        out_ref[...] = (total + bias_ref[...]).astype(out_dtype)

    out = jax.ShapeDtypeStruct((rows, tiles.columns()), out_dtype)
    return pl.pallas_call(
        kernel,
        out_shape=out,
        grid=(tiles.count,),
        in_specs=[
            pl.BlockSpec(left.shape, lambda j: (0, 0)),
            pl.BlockSpec((1, tiles.tile), lambda j: (0, j)),
            *tiles.specs(),
        ],
        out_specs=pl.BlockSpec((rows, tiles.tile), lambda j: (0, j)),
        cost_estimate=cost(2 * rows * left.shape[1] * tiles.columns(), [left, out, *operands]),
        name=name,
    )(left, bias.reshape(1, -1), *operands)


def gelu_parts(value):
    inner = math.sqrt(2.0 / math.pi) * (value + 0.044715 * (value * value * value))
    return jnp.tanh(inner)


def project_up(left, tiles, bias, channel_on):
    rows = left.shape[0]
    groups = channel_on.shape[0]
    operands = tiles.operands()

    def kernel(left_ref, bias_ref, channel_ref, *refs):
        pre_ref, turned_ref = refs[-2:]

        pre = jnp.dot(left_ref[...], tiles.weight(refs), preferred_element_type=F32)
        pre = pre + bias_ref[...]
        pre_ref[...] = pre
        hidden = 0.5 * pre * (1.0 + gelu_parts(pre))
        span = rows // groups
        for group in range(groups):
            part = hidden[group * span : (group + 1) * span] * channel_ref[group : group + 1]
            turned_ref[:, group * span : (group + 1) * span] = part.T.astype(BF)

    pre = jax.ShapeDtypeStruct((rows, tiles.columns()), F32)
    turned = jax.ShapeDtypeStruct((tiles.columns(), rows), BF)
    return pl.pallas_call(
        kernel,
        out_shape=[pre, turned],
        grid=(tiles.count,),
        in_specs=[
            pl.BlockSpec(left.shape, lambda j: (0, 0)),
            pl.BlockSpec((1, tiles.tile), lambda j: (0, j)),
            pl.BlockSpec((groups, tiles.tile), lambda j: (0, j)),
            *tiles.specs(),
        ],
        out_specs=[
            pl.BlockSpec((rows, tiles.tile), lambda j: (0, j)),
            pl.BlockSpec((tiles.tile, rows), lambda j: (j, 0)),
        ],
        cost_estimate=cost(
            2 * rows * left.shape[1] * tiles.columns(), [left, pre, turned, *operands], pre.size
        ),
        name="project_up",
    )(left, bias.reshape(1, -1), channel_on, *operands)


def project_back(right, tiles, order, parts, name):
    rows = right.shape[0]
    operands = tiles.operands()
    width = order.shape[1]

    def kernel(right_ref, order_ref, *refs):
        out_ref, total_ref = refs[-2:]
        index = pl.program_id(0)

        @pl.when(index == 0)
        def _():
            total_ref[...] = jnp.zeros_like(total_ref)

        total_ref[...] += contract(right_ref[...], tiles.weight(refs), 1, 1)

        @pl.when(index == tiles.count - 1)
        def _():
            rest = total_ref[...]
            out = None
            for part in range(parts):
                high = rest.astype(BF)
                placed = jnp.dot(high, order_ref[...], preferred_element_type=F32)
                out = placed if out is None else out + placed
                if part < parts - 1:
                    rest = rest - high.astype(F32)
            out_ref[...] = out

    out = jax.ShapeDtypeStruct((rows, width), F32)
    return pl.pallas_call(
        kernel,
        out_shape=out,
        grid=(tiles.count,),
        in_specs=[
            pl.BlockSpec((rows, tiles.tile), lambda j: (0, j)),
            pl.BlockSpec(order.shape, lambda j: (0, 0)),
            *tiles.specs(),
        ],
        out_specs=pl.BlockSpec(out.shape, lambda j: (0, 0)),
        scratch_shapes=[pltpu.VMEM((rows, tiles.rows), F32)],
        cost_estimate=cost(
            2 * rows * tiles.rows * (tiles.columns() + parts * width), [right, out, order, *operands]
        ),
        name=name,
    )(right, order, *operands)


def hidden_back(down_grad, full_down, pre, channel_on, tile):
    rows, width = down_grad.shape
    groups = channel_on.shape[0]
    columns = pre.shape[1]

    def kernel(grad_ref, weight_ref, pre_ref, channel_ref, out_ref, sum_ref):
        value = pre_ref[...]
        tanh = gelu_parts(value)
        slope = 0.5 * (1.0 + tanh) + 0.5 * value * (1.0 - tanh * tanh) * math.sqrt(
            2.0 / math.pi
        ) * (1.0 + 3.0 * 0.044715 * value * value)
        grad = contract(grad_ref[...], weight_ref[...], 1, 1) * slope
        span = rows // groups
        total = None
        for group in range(groups):
            part = (
                grad[group * span : (group + 1) * span] * channel_ref[group : group + 1]
            ).astype(BF)
            out_ref[group * span : (group + 1) * span] = part
            along = jnp.sum(part.astype(F32), axis=0, keepdims=True)
            total = along if total is None else total + along
        sum_ref[...] = total

    out = jax.ShapeDtypeStruct((rows, columns), BF)
    sums = jax.ShapeDtypeStruct((1, columns), F32)
    return pl.pallas_call(
        kernel,
        out_shape=[out, sums],
        grid=(columns // tile,),
        in_specs=[
            pl.BlockSpec(down_grad.shape, lambda j: (0, 0)),
            pl.BlockSpec((tile, width), lambda j: (j, 0)),
            pl.BlockSpec((rows, tile), lambda j: (0, j)),
            pl.BlockSpec((groups, tile), lambda j: (0, j)),
        ],
        out_specs=[
            pl.BlockSpec((rows, tile), lambda j: (0, j)),
            pl.BlockSpec((1, tile), lambda j: (0, j)),
        ],
        cost_estimate=cost(
            2 * rows * width * columns, [down_grad, full_down, pre, out], rows * columns
        ),
        name="hidden_back",
    )(down_grad, full_down, pre, channel_on)


def head_window(head, head_size, width):
    start = jnp.minimum(head * head_size // 128, width // 128 - 2) * 128
    lane = lax.broadcasted_iota(jnp.int32, (1, 256), 1) + start
    inside = (lane >= head * head_size) & (lane < (head + 1) * head_size)
    return pl.multiple_of(start, 128), inside


def attend(qkv, other, head_on, block_mask, head_count):
    rows = qkv.shape[0]
    width = qkv.shape[1] // 3
    head_size = width // head_count
    groups = head_on.shape[0]
    span = rows // groups
    factor = 1.0 / math.sqrt(head_size) / math.log(2.0)

    def kernel(qkv_ref, other_ref, head_ref, mask_ref, mixed_ref, total_ref):
        head = pl.program_id(0)
        start, inside = head_window(head, head_size, width)
        window = pl.ds(start, 256)
        key_window = pl.ds(start + width, 256)
        value_window = pl.ds(start + 2 * width, 256)
        keys = (qkv_ref[:, key_window], other_ref[:, window])
        values = (qkv_ref[:, value_window], other_ref[:, key_window])
        for group in range(groups):
            at = pl.ds(group * span, span)
            query = qkv_ref[at, window]
            query = jnp.where(inside, query, jnp.zeros_like(query))
            scores = [
                contract(query, key, 1, 1) * factor
                + mask_ref[group : group + 1, side * rows : (side + 1) * rows]
                for side, key in enumerate(keys)
            ]
            largest = jnp.maximum(
                jnp.max(scores[0], axis=1, keepdims=True), jnp.max(scores[1], axis=1, keepdims=True)
            )
            powers = [jnp.exp2(score - largest) for score in scores]
            total = jnp.sum(powers[0], axis=1, keepdims=True) + jnp.sum(
                powers[1], axis=1, keepdims=True
            )
            inverse = 1.0 / total
            out = None
            for power, value in zip(powers, values):
                part = jnp.dot((power * inverse).astype(BF), value, preferred_element_type=F32)
                out = part if out is None else out + part
            out = (out * head_ref[group : group + 1, window]).astype(BF)
            mixed_ref[at, window] = jnp.where(inside, out, mixed_ref[at, window])
            lane = lax.broadcasted_iota(jnp.int32, (1, 128), 1)
            total_ref[at, :] = jnp.where(
                lane == head, largest + jnp.log2(total), total_ref[at, :]
            )

    mixed = jax.ShapeDtypeStruct((rows, width), BF)
    totals = jax.ShapeDtypeStruct((rows, 128), F32)
    return pl.pallas_call(
        kernel,
        out_shape=[mixed, totals],
        grid=(head_count,),
        in_specs=[
            pl.BlockSpec(array.shape, lambda h: (0, 0)) for array in (qkv, other, head_on, block_mask)
        ],
        out_specs=[pl.BlockSpec(array.shape, lambda h: (0, 0)) for array in (mixed, totals)],
        cost_estimate=cost(
            4 * head_count * rows * 2 * rows * 256, [qkv, other, mixed], head_count * rows * 2 * rows
        ),
        name="attend",
    )(qkv, other, head_on, block_mask)


def attend_back(qkv, other, grad_mixed, totals, block_mask, head_count):
    rows = qkv.shape[0]
    width = qkv.shape[1] // 3
    head_size = width // head_count
    blocks = block_mask.shape[0]
    span = 2 * rows // blocks
    scale = 1.0 / math.sqrt(head_size)
    factor = scale / math.log(2.0)

    def kernel(qkv_ref, other_ref, grad_ref, totals_ref, mask_ref, query_out, own_out, other_out):
        head = pl.program_id(0)
        start, inside = head_window(head, head_size, width)
        window = pl.ds(start, 256)
        key_window = pl.ds(start + width, 256)
        value_window = pl.ds(start + 2 * width, 256)
        query = qkv_ref[:, window]
        query = jnp.where(inside, query, jnp.zeros_like(query))
        grad = grad_ref[:, window]
        grad = jnp.where(inside, grad, jnp.zeros_like(grad))
        total = totals_ref[pl.ds(head, 1), :]
        kept = []
        along = None
        for block in range(blocks):
            own = block < blocks // 2
            at = pl.ds((block if own else block - blocks // 2) * span, span)
            key = qkv_ref[at, key_window] if own else other_ref[at, window]
            value = qkv_ref[at, value_window] if own else other_ref[at, key_window]
            scores = contract(key, query, 1, 1)
            probs = jnp.exp2(scores * factor + (mask_ref[block : block + 1, :] - total))
            grad_probs = contract(value, grad, 1, 1)
            part = jnp.sum(probs * grad_probs, axis=0, keepdims=True)
            along = part if along is None else along + part
            kept.append((own, at, key, probs, grad_probs))
        query_grad = None
        for own, at, key, probs, grad_probs in kept:
            grad_scores = (probs * (grad_probs - along)).astype(BF)
            key_part = jnp.dot(grad_scores, query, preferred_element_type=F32) * scale
            value_part = jnp.dot(probs.astype(BF), grad, preferred_element_type=F32)
            out_ref = own_out if own else other_out
            out_ref[at, window] = jnp.where(
                inside, key_part.astype(out_ref.dtype), out_ref[at, window]
            )
            out_ref[at, key_window] = jnp.where(
                inside, value_part.astype(out_ref.dtype), out_ref[at, key_window]
            )
            part = contract(grad_scores, key, 0, 0)
            query_grad = part if query_grad is None else query_grad + part
        query_out[:, window] = jnp.where(
            inside, (query_grad * scale).astype(BF), query_out[:, window]
        )

    outs = [
        jax.ShapeDtypeStruct((rows, width), BF),
        jax.ShapeDtypeStruct((rows, 2 * width), F32),
        jax.ShapeDtypeStruct((rows, 2 * width), BF),
    ]
    operands = (qkv, other, grad_mixed, totals, block_mask)
    return pl.pallas_call(
        kernel,
        out_shape=outs,
        grid=(head_count,),
        in_specs=[pl.BlockSpec(array.shape, lambda h: (0, 0)) for array in operands],
        out_specs=[pl.BlockSpec(array.shape, lambda h: (0, 0)) for array in outs],
        cost_estimate=cost(
            10 * head_count * rows * 2 * rows * 256, [*operands, *outs], head_count * rows * 2 * rows
        ),
        name="attend_back",
    )(*operands)


def cond_columns(steps, first, count, model_width):
    half_width = model_width // 2
    index = first + jnp.arange(count, dtype=jnp.int32)
    is_sine = index >= half_width
    place = jnp.where(is_sine, index - half_width, index).astype(F32)
    frequency = jnp.exp(-math.log(10000.0) * place / half_width)
    angles = steps.astype(F32)[:, None] * frequency[None, :]
    values = jnp.where(is_sine[None, :], jnp.sin(angles), jnp.cos(angles))
    return jax.nn.silu(values).astype(BF)


def normalize(values):
    centered = values - jnp.mean(values, axis=-1, keepdims=True)
    spread = jnp.mean(centered * centered, axis=-1, keepdims=True)
    inverse = lax.rsqrt(spread + 1e-06)
    return centered * inverse, inverse


def normalize_back(grad_normed, normed, inverse):
    along = jnp.mean(grad_normed * normed, axis=-1, keepdims=True)
    level = jnp.mean(grad_normed, axis=-1, keepdims=True)
    return inverse * (grad_normed - level - normed * along)


def body(
    tokens,
    qkv_weight,
    out_weight,
    up_weight,
    down_weight,
    mod_weight,
    qv_bias,
    out_bias,
    up_bias,
    down_bias,
    mod_bias,
    row_items,
    timesteps,
    head_mask,
    channel_mask,
    token_keep,
    cotangent,
):
    layer_count = qkv_weight.shape[0]
    width = out_weight.shape[2]
    hidden_width = up_weight.shape[2]
    head_count = head_mask.shape[3]
    head_size = width // head_count
    item_count = timesteps.shape[1]
    local_rows = tokens.shape[0]
    row_len = 2 * local_rows
    group_rows = row_len // item_count
    group_count = local_rows // group_rows
    scale_factor = 1.0 / math.sqrt(head_size)
    seq_count = lax.axis_size("seq")
    seq_bits = seq_count.bit_length() - 1
    device_count = 2 * seq_count
    half_index = lax.axis_index("fsdp")
    seq_index = lax.axis_index("seq")
    flat_index = half_index * seq_count + seq_index
    shard_rows = mod_weight.shape[1]
    items_here = row_items[0]
    far_stages = [("seq", bit) for bit in range(2, seq_bits)]
    core_stage = ("seq", 0)

    padded_rows = -(-shard_rows // 8) * 8
    row_cut = (padded_rows + 8) // 16 * 8
    x_stage, y_stage = ("fsdp", 0), ("seq", 1)
    routes = (core_stage, (y_stage, x_stage), (x_stage, y_stage), far_stages)
    far_count = 1 << len(far_stages)

    def flat_mask(stage):
        return seq_count if stage[0] == "fsdp" else 1 << stage[1]

    chunk_masks, chunk_places = [], []
    for core_mask in (0, 1):
        for two in range(2):
            for part, route in enumerate(routes[1:3]):
                part_rows = padded_rows - row_cut if part else row_cut
                first_mask = flat_mask(route[0]) if two else 0
                for mask in relative_masks([route[1], *far_stages], flat_mask):
                    chunk_masks += [core_mask ^ first_mask ^ mask] * part_rows
                    chunk_places += list(range(row_cut * part, row_cut * part + part_rows))
    chunk_masks = jnp.array(chunk_masks, jnp.int32)
    chunk_places = jnp.array(chunk_places, jnp.int32)
    source = jnp.where(
        chunk_places < shard_rows, (flat_index ^ chunk_masks) * shard_rows + chunk_places, -1
    )
    order = (source[:, None] == jnp.arange(width, dtype=jnp.int32)[None, :]).astype(BF)

    def ordered(left):
        return contract(left, order, 1, 1).astype(BF)

    feed = Feed()
    place_table = jnp.stack(
        [half_index, (seq_index >> 1) & 1, seq_index & 1]
        + [
            (seq_index >> 2) ^ (mask >> 2)
            for mask in relative_masks(far_stages, lambda stage: 1 << stage[1])
        ]
    ).astype(jnp.int32)

    def scatter_ordered(left, right, waits, result):
        half = left.shape[1] // 2
        cuts = (2 * far_count * row_cut, 2 * far_count * (padded_rows - row_cut))
        feed.start(
            reduce_flight(
                left[:, half:], left[:, :half], right, 0, routes, cuts, shard_rows, waits, result
            )
        )

    def scatter_chunks(turned, right, waits, result):
        rows = turned.shape[0] // device_count
        stay, away = take_chunks(turned, place_table, rows)
        cuts = (far_count * rows, far_count * rows)
        feed.start(reduce_flight(away, stay, right, 1, routes, cuts, rows, waits, result))

    gathered = []

    def unit_ticks(unit):
        early = ((0, 1, 2, 3, 5, 6), (1, 3, 4, 6, 8, 9), (4, 6, 7, 8, 11, 12))
        late = ((7, 8, 10, 11, 13, 14), (8, 10, 11, 13, 16, 17), (11, 13, 15, 16, 19, 20))
        if unit < 3:
            return early[unit]
        return tuple(tick + 8 * (unit // 3 - 1) for tick in late[unit % 3])

    def padded(shard):
        return jnp.pad(shard, ((0, padded_rows - shard_rows), (0, 0)))

    for layer in range(layer_count):
        up_out = jnp.concatenate([up_weight[layer], out_weight[layer]], axis=1)
        for index, (shard, cut) in enumerate(
            (
                (padded(qkv_weight[layer]), row_cut),
                (padded(up_out), row_cut),
                (down_weight[layer], down_weight.shape[1] // 2),
            )
        ):
            result = []
            gathered.append(result)
            start, *due = unit_ticks(3 * layer + index)
            waits = [after - before for before, after in zip([start] + due, due)]
            feed.at(start, gather_flight(shard, cut, routes, waits, result))

    def qkv_tiles(layer):
        return Tiles(gathered[3 * layer], width, 0, 3)

    def pair_tiles(layer):
        return Tiles(gathered[3 * layer], width, 1, 2)

    def up_tiles(layer):
        tile = wide_tile(hidden_width) // 2
        return Tiles(gathered[3 * layer + 1], tile, 0, hidden_width // tile)

    def out_tiles(layer):
        return Tiles(gathered[3 * layer + 1], width, hidden_width // width, 1)

    biases = (qv_bias, out_bias, up_bias, down_bias, mod_bias)
    steps_high = (timesteps // 32).astype(BF)
    steps_low = (timesteps % 32).astype(BF)
    small = jnp.concatenate(
        [bias.reshape(-1) for bias in biases] + [steps_high.reshape(-1), steps_low.reshape(-1)]
    )
    small = feed.tick(small[None])
    small_stages = [("seq", bit) for bit in reversed(range(seq_bits))] + [x_stage]
    for index, stage in enumerate(small_stages):
        small = jnp.concatenate([small, swap_bit(small, stage)], axis=0)
        if index == 1:
            small = feed.tick(small)
    small_masks = jnp.array(relative_masks(list(reversed(small_stages)), flat_mask), jnp.int32)
    put_back = (flat_index ^ small_masks)[None, :] == jnp.arange(device_count)[:, None]
    every_small = jnp.dot(put_back.astype(BF), small, preferred_element_type=F32)
    full_biases = []
    offset = 0
    for bias in biases:
        columns = bias.shape[1]
        full_biases.append(
            [
                every_small[:, offset + layer * columns : offset + (layer + 1) * columns]
                .reshape(-1)
                for layer in range(layer_count)
            ]
        )
        offset += layer_count * columns
    step_parts = every_small[:seq_count, offset:]
    every_step = step_parts[:, :item_count] * 32.0 + step_parts[:, item_count:]

    cond_every = cond_columns(every_step.reshape(-1), flat_index * shard_rows, shard_rows, width)
    seq_masks = jnp.array(
        relative_masks([("seq", bit) for bit in range(seq_bits)], lambda stage: 1 << stage[1]),
        jnp.int32,
    )
    pick_row = (seq_index ^ seq_masks)[:, None] == jnp.arange(seq_count)[None, :]
    cond_relative = (
        jnp.sum(
            jnp.where(
                pick_row[:, :, None, None],
                cond_every.astype(F32).reshape(1, seq_count, item_count, shard_rows),
                0.0,
            ),
            axis=1,
        )
        .astype(BF)
        .reshape(seq_count * item_count, shard_rows)
    )

    mod_stages = [("seq", bit) for bit in range(seq_bits)] + [("fsdp", 0)]
    modulations = [[] for _ in range(layer_count)]

    def modulation_part(layer):
        return jnp.dot(cond_relative, mod_weight[layer], preferred_element_type=F32)

    block = feed.tick(modulation_part(0))
    for index, stage in enumerate(mod_stages[:-1]):
        half = block.shape[0] // 2
        block = block[:half] + swap_bit(block[half:], stage)
        if index == 1:
            block = feed.tick(block)
    block = block + swap_bit(block, mod_stages[-1]) + full_biases[4][0][None]
    modulations[0].append(feed.tick(block))
    for layer in range(1, layer_count):
        feed.start(
            modulation_flight(
                modulation_part(layer), full_biases[4][layer], mod_stages, modulations[layer]
            )
        )

    group_item = (
        (half_index * local_rows + jnp.arange(group_count, dtype=jnp.int32) * group_rows)
        * items_here
        // row_len
    )
    other_item = (
        ((1 - half_index) * local_rows + jnp.arange(group_count, dtype=jnp.int32) * group_rows)
        * items_here
        // row_len
    )
    group_is = group_item[:, None] == jnp.arange(item_count, dtype=jnp.int32)[None, :]

    def of_groups(table):
        return jnp.sum(
            jnp.where(group_is[:, :, None], table.astype(F32)[None], 0.0), axis=1, keepdims=False
        )[:, None, :]

    block_item = jnp.concatenate([group_item, other_item])
    block_mask = jnp.where(group_item[:, None] == block_item[None, :], 0.0, -1e30).astype(F32)
    query_mask = jnp.repeat(block_mask, group_rows, axis=1)
    key_mask = jnp.repeat(block_mask.T, group_rows, axis=1)

    def grouped(values):
        return values.reshape(group_count, group_rows, values.shape[-1])

    def ungrouped(values):
        return values.reshape(local_rows, values.shape[-1])

    current = grouped(tokens.astype(F32))
    saved_layers = []
    full_downs = []
    for layer in range(layer_count):
        pair_bias, out_b, up_b, down_b = (full_biases[index][layer] for index in range(4))
        current = feed.until(modulations[layer], current)
        (modulation,) = modulations[layer]
        shift_one, scale_one, gate_one, shift_two, scale_two, gate_two = jnp.split(
            of_groups(modulation), 6, axis=2
        )
        head_on = jnp.repeat(of_groups(head_mask[0, layer]), head_size, axis=2)[:, 0]
        channel_on = of_groups(channel_mask[0, layer])[:, 0]
        keep_tok = grouped(token_keep[:, layer].astype(F32)[:, None])
        normed_one, inverse_one = normalize(current)
        low_one = ungrouped((normed_one * (1.0 + scale_one) + shift_one).astype(BF))
        other_one = swap_bit(low_one, x_stage)
        bias_three = jnp.concatenate(
            [pair_bias[:width], jnp.zeros((width,), F32), pair_bias[width:]]
        )
        low_one = feed.tick(low_one)
        low_one = feed.tick(ordered(low_one))
        low_one = feed.until(gathered[3 * layer], low_one)
        qkv_low = project(low_one, qkv_tiles(layer), bias_three, BF, "project_qkv")
        other_low = project(
            ordered(other_one), pair_tiles(layer), bias_three[width:], BF, "project_pair"
        )
        other_low = feed.tick(other_low)
        mixed_low, totals = attend(qkv_low, other_low, head_on, query_mask, head_count)
        totals = totals[:, :head_count].T
        mixed_low = feed.tick(mixed_low)
        mixed_low = feed.tick(ordered(mixed_low))
        mixed_low = feed.until(gathered[3 * layer + 1], mixed_low)
        branch_one = grouped(project(mixed_low, out_tiles(layer), out_b, F32, "project_out"))
        after_attn = current + gate_one * branch_one
        normed_two, inverse_two = normalize(after_attn)
        low_two = ungrouped((normed_two * (1.0 + scale_two) + shift_two).astype(BF))
        low_two = feed.tick(ordered(low_two))
        hidden_pre, hidden_turned = project_up(low_two, up_tiles(layer), up_b, channel_on)
        hidden_turned = feed.tick(hidden_turned)
        hidden_turned = feed.tick(hidden_turned)
        hidden_turned = feed.until(gathered[3 * layer + 2], hidden_turned)
        full_down = place_chunks(*gathered[3 * layer + 2], place_table, (hidden_width, width))
        full_downs.append(full_down)
        branch_two = grouped(contract(hidden_turned, full_down, 0, 0) + down_b)
        saved_layers.append(
            dict(
                inputs=current,
                scale_one=scale_one,
                gate_one=gate_one,
                scale_two=scale_two,
                gate_two=gate_two,
                head_on=head_on,
                channel_on=channel_on,
                keep_tok=keep_tok,
                low_one=low_one,
                qkv_low=qkv_low,
                other_low=other_low,
                totals=totals,
                mixed_low=mixed_low,
                branch_one=branch_one,
                after_attn=after_attn,
                low_two=low_two,
                hidden_pre=hidden_pre,
                hidden_turned=hidden_turned,
                branch_two=branch_two,
            )
        )
        current = after_attn + keep_tok * gate_two * branch_two
    output = ungrouped(current).astype(BF)
    output = feed.finish(output)

    cond_rows = jnp.concatenate(
        [
            cond_every.reshape(seq_count, item_count, shard_rows),
            jnp.zeros((seq_count, 8 - item_count, shard_rows), BF),
        ],
        axis=1,
    ).reshape(seq_count * 8, shard_rows)
    cond_twice = jnp.concatenate([cond_rows, cond_rows], axis=0)
    grad_current = grouped(cotangent)
    layer_totals = [None] * layer_count
    for layer in reversed(range(layer_count)):
        saved = saved_layers[layer]
        kept_grad = grad_current * saved["keep_tok"]
        down_grad = ungrouped((kept_grad * saved["gate_two"]).astype(BF))
        grad_gate_two = jnp.sum(kept_grad * saved["branch_two"], axis=1)
        grad_down_bias = jnp.sum(down_grad.astype(F32), axis=0)
        down_rows, up_rows, out_rows, qkv_rows = [], [], [], []
        scatter_chunks(saved["hidden_turned"], down_grad, (1, 2, 2), down_rows)
        up_grad, grad_up_bias = hidden_back(
            down_grad, full_downs[layer], saved["hidden_pre"], saved["channel_on"], wide_tile(hidden_width) // 2
        )
        grad_up_bias = grad_up_bias[0]
        up_grad = feed.tick(up_grad)
        scatter_ordered(saved["low_two"], up_grad, (1, 2, 2), up_rows)
        grad_h2 = grouped(project_back(up_grad, up_tiles(layer), order, 2, "back_up"))
        grad_h2 = feed.tick(grad_h2)
        normed_two, inverse_two = normalize(saved["after_attn"])
        grad_shift_two = jnp.sum(grad_h2, axis=1)
        grad_scale_two = jnp.sum(grad_h2 * normed_two, axis=1)
        grad_after = grad_current + normalize_back(
            grad_h2 * (1.0 + saved["scale_two"]), normed_two, inverse_two
        )
        out_grad = ungrouped((grad_after * saved["gate_one"]).astype(BF))
        grad_gate_one = jnp.sum(grad_after * saved["branch_one"], axis=1)
        grad_out_bias = jnp.sum(out_grad.astype(F32), axis=0)
        out_grad = feed.tick(out_grad)
        scatter_ordered(saved["mixed_low"], out_grad, (1, 1, 1), out_rows)
        grad_mixed = ungrouped(
            (
                grouped(project_back(out_grad, out_tiles(layer), order, 1, "back_out"))
                * saved["head_on"][:, None]
            ).astype(BF)
        )
        grad_mixed = feed.tick(grad_mixed)
        grad_query, own_pair, other_pair = attend_back(
            saved["qkv_low"], saved["other_low"], grad_mixed, saved["totals"], key_mask, head_count
        )
        other_pair = feed.tick(other_pair)
        back_pair = swap_bit(other_pair, x_stage)
        grad_qkv = jnp.concatenate(
            [grad_query, (own_pair + back_pair.astype(F32)).astype(BF)], axis=1
        )
        grad_qkv = feed.tick(grad_qkv)
        grad_qkv_bias = jnp.sum(grad_qkv.astype(F32), axis=0)
        scatter_ordered(saved["low_one"], grad_qkv, (1, 2, 2), qkv_rows)
        grad_h1 = grouped(project_back(grad_qkv, qkv_tiles(layer), order, 2, "back_qkv"))
        grad_h1 = feed.tick(grad_h1)
        normed_one, inverse_one = normalize(saved["inputs"])
        grad_shift_one = jnp.sum(grad_h1, axis=1)
        grad_scale_one = jnp.sum(grad_h1 * normed_one, axis=1)
        grad_inputs = grad_after + normalize_back(
            grad_h1 * (1.0 + saved["scale_one"]), normed_one, inverse_one
        )
        grad_groups = jnp.concatenate(
            [
                grad_shift_one,
                grad_scale_one,
                grad_gate_one,
                grad_shift_two,
                grad_scale_two,
                grad_gate_two,
            ],
            axis=1,
        )
        grad_slots = jnp.sum(jnp.where(group_is[:, :, None], grad_groups[:, None, :], 0.0), axis=0)
        mod_width = grad_slots.shape[1]
        bias_row = jnp.concatenate(
            [
                grad_qkv_bias[:width],
                grad_qkv_bias[2 * width :],
                grad_out_bias,
                grad_up_bias,
                grad_down_bias,
            ]
        )
        spare = jnp.zeros(((8 - item_count) * mod_width - bias_row.shape[0],), F32)
        packet = jnp.concatenate(
            [grad_slots, jnp.concatenate([bias_row, spare]).reshape(8 - item_count, mod_width)],
            axis=0,
        ).astype(BF)
        every_packet = lax.all_gather(packet, AXES, axis=0, tiled=True)
        grad_mod_weight = contract(cond_twice, every_packet, 0, 0)
        packet_sum = jnp.sum(
            every_packet.astype(F32).reshape(device_count, 8, mod_width), axis=0
        )
        mod_cols = mod_bias.shape[1]
        grad_mod_bias = lax.dynamic_slice_in_dim(
            jnp.sum(packet_sum[:item_count], axis=0), flat_index * mod_cols, mod_cols, 0
        )
        bias_sum = packet_sum[item_count:].reshape(-1)
        parts = []
        start = 0
        for bias in (qv_bias, out_bias, up_bias, down_bias):
            columns = bias.shape[1]
            parts.append(
                lax.dynamic_slice_in_dim(bias_sum, start + flat_index * columns, columns, 0)
            )
            start += device_count * columns
        grad_current = grad_inputs
        layer_totals[layer] = (
            qkv_rows,
            out_rows,
            up_rows,
            down_rows,
            grad_mod_weight,
            *parts,
            grad_mod_bias,
        )
    grad_current = feed.finish(grad_current)
    layer_totals = [
        [part[0] if isinstance(part, list) else part for part in totals] for totals in layer_totals
    ]
    stacked = tuple(
        jnp.stack([layer_totals[layer][index] for layer in range(layer_count)])
        for index in range(10)
    )
    return (output, ungrouped(grad_current), *stacked)


def solution(mesh):
    rows = P(AXES, None)
    matrix = P(None, AXES, None)
    vector = P(None, AXES)
    return jax.shard_map(
        body,
        mesh=mesh,
        in_specs=(
            rows,
            matrix,
            matrix,
            matrix,
            matrix,
            matrix,
            vector,
            vector,
            vector,
            vector,
            vector,
            P("seq"),
            P("seq", None),
            P("seq", None, None, None),
            P("seq", None, None, None),
            rows,
            rows,
        ),
        out_specs=(
            rows,
            rows,
            matrix,
            matrix,
            matrix,
            matrix,
            matrix,
            vector,
            vector,
            vector,
            vector,
            vector,
        ),
        check_vma=False,
    )
```

```python
import math

import jax
import jax.numpy as jnp
from jax import lax
from jax.experimental import pallas as pl
from jax.experimental.pallas import tpu as pltpu
from jax.sharding import PartitionSpec as P

BF = jnp.bfloat16
F32 = jnp.float32
AXES = ("fsdp", "seq")


def swap_bit(block, stage):
    axis, bit = stage
    count = lax.axis_size(axis)
    return lax.ppermute(block, axis, [(low, low ^ (1 << bit)) for low in range(count)])


def stage_bit(stage):
    axis, bit = stage
    return (lax.axis_index(axis) >> bit) & 1


def contract(left, right, left_dim, right_dim):
    return lax.dot_general(
        left, right, (((left_dim,), (right_dim,)), ((), ())), preferred_element_type=F32
    )


def relative_masks(stages, mask_of):
    masks = [0]
    for stage in reversed(stages):
        masks = masks + [mask ^ mask_of(stage) for mask in masks]
    return masks


class Feed:
    def __init__(self):
        self.flights = []
        self.ticks = 0
        self.later = {}

    def start(self, flight):
        wait, parts = next(flight)
        self.flights.append((flight, self.ticks + wait - 1, parts))

    def at(self, tick, flight):
        self.later.setdefault(tick, []).append(flight)

    def tick(self, value):
        for flight in self.later.pop(self.ticks, []):
            self.start(flight)
        due = [entry for entry in self.flights if entry[1] <= self.ticks]
        flying = [entry for entry in self.flights if entry[1] > self.ticks]
        self.ticks += 1
        value, arrived = lax.optimization_barrier((value, [parts for _, _, parts in due]))
        for (flight, _, _), parts in zip(due, arrived):
            try:
                wait, sent = flight.send(parts)
                flying.append((flight, self.ticks + wait - 1, sent))
            except StopIteration:
                pass
        self.flights = flying
        return value

    def until(self, result, value):
        while not result:
            value = self.tick(value)
        return value

    def finish(self, value):
        while self.flights or self.later:
            value = self.tick(value)
        return value


def reduce_flight(grads, routes, cuts, rows, waits, result):
    core_stage, first_route, second_route, far_stages = routes
    first, second = cuts
    waits = list(waits) + [1] * 8
    arrived = yield waits[0], swap_bit(grads.away(), core_stage)
    parts = grads.stay(arrived, first, second)
    if waits[1]:
        parts = yield waits[1], parts
    kept, first_sent, second_sent = parts
    first_arrived, second_arrived = yield waits[2], (
        swap_bit(first_sent, first_route[0]),
        swap_bit(second_sent, second_route[0]),
    )

    def add(left, other, low, high):
        return left[low:high].astype(F32) + other[low:high].astype(F32)

    first_kept, second_kept = kept[:first], kept[first:]
    half_first, half_second = first // 2, second // 2
    first_sent = add(first_kept, first_arrived, half_first, first).astype(BF)
    second_sent = add(second_kept, second_arrived, half_second, second).astype(BF)
    first_kept = add(first_kept, first_arrived, 0, half_first).astype(BF)
    second_kept = add(second_kept, second_arrived, 0, half_second).astype(BF)
    first_arrived, second_arrived = yield waits[3], (
        swap_bit(first_sent, first_route[1]),
        swap_bit(second_sent, second_route[1]),
    )
    for index, stage in enumerate(far_stages):
        first, second = half_first, half_second
        half_first, half_second = first // 2, second // 2
        sent = jnp.concatenate(
            [
                add(first_kept, first_arrived, half_first, first),
                add(second_kept, second_arrived, half_second, second),
            ],
            axis=0,
        ).astype(BF)
        first_kept = add(first_kept, first_arrived, 0, half_first).astype(BF)
        second_kept = add(second_kept, second_arrived, 0, half_second).astype(BF)
        arrived = yield waits[4 + index], swap_bit(sent, stage)
        first_arrived, second_arrived = arrived[:half_first], arrived[half_first:]
    block = jnp.concatenate(
        [
            add(first_kept, first_arrived, 0, half_first),
            add(second_kept, second_arrived, 0, half_second),
        ],
        axis=0,
    )
    result.append(block[:rows])


class ColumnGrads:
    def __init__(self, lefts, rights, tile):
        self.lefts, self.rights, self.tile = lefts, rights, tile
        self.half = lefts[0].shape[1] // 2
        self.counts = [right.shape[1] // tile for right in rights]

    def call(self, index, arrived, pieces, name):
        half, tile = self.half, self.tile
        tokens = self.lefts[0].shape[0]
        pairs = len(self.lefts)
        starts = [sum(self.counts[:pair]) for pair in range(pairs)]
        columns = sum(self.counts) * tile

        def kernel(*refs):
            lefts, rights = refs[:pairs], refs[pairs : 2 * pairs]
            rest = refs[2 * pairs :]
            if arrived is not None:
                arrived_ref, rest = rest[0], rest[1:]
            out_refs, turned_ref = rest[:-1], rest[-1]
            step = pl.program_id(0)

            def work(left_ref, right_ref, start):
                @pl.when(step == start)
                def _():
                    turned_ref[...] = left_ref[...].astype(F32).T.astype(BF)

                total = jnp.dot(turned_ref[...], right_ref[...], preferred_element_type=F32)
                if arrived is not None:
                    total = total + arrived_ref[...].astype(F32)
                total = total.astype(BF)
                low = 0
                for out_ref, count in zip(out_refs, pieces):
                    out_ref[...] = total[low : low + count]
                    low += count

            for left_ref, right_ref, start, count in zip(lefts, rights, starts, self.counts):
                if pairs == 1:
                    work(left_ref, right_ref, start)
                else:
                    pl.when((step >= start) & (step < start + count))(
                        lambda l=left_ref, r=right_ref, s=start: work(l, r, s)
                    )

        def right_spec(start, count):
            return pl.BlockSpec(
                (tokens, tile), lambda j: (0, jnp.clip(j - start, 0, count - 1))
            )

        operands = [*self.lefts, *self.rights]
        in_specs = [pl.BlockSpec((tokens, half), lambda j: (0, index)) for _ in self.lefts]
        in_specs += [right_spec(*pair) for pair in zip(starts, self.counts)]
        if arrived is not None:
            operands.append(arrived)
            in_specs.append(pl.BlockSpec((half, tile), lambda j: (0, j)))
        outs = [jax.ShapeDtypeStruct((count, columns), BF) for count in pieces]
        return pl.pallas_call(
            kernel,
            out_shape=outs,
            grid=(sum(self.counts),),
            in_specs=in_specs,
            out_specs=[pl.BlockSpec((count, tile), lambda j: (0, j)) for count in pieces],
            scratch_shapes=[pltpu.VMEM((half, tokens), BF)],
            cost_estimate=cost(2 * half * tokens * columns, [*operands, *outs]),
            name=name,
        )(*operands)

    def away(self):
        return self.call(1, None, [self.half], "away_grad")[0]

    def stay(self, arrived, first, second):
        return self.call(0, arrived, [self.half - first - second, first, second], "stay_grad")


class RowGrads:
    def __init__(self, stay, away, right):
        self.stay_rows, self.away_rows, self.right = stay, away, right

    def away(self):
        return contract(self.away_rows, self.right, 1, 0).astype(BF)

    def stay(self, arrived, first, second):
        left, right = self.stay_rows, self.right
        tokens, columns = right.shape
        assert first == second

        def kernel(left_ref, right_ref, arrived_ref, kept_ref, first_ref, second_ref):
            step = pl.program_id(0)
            total = jnp.dot(left_ref[...], right_ref[...], preferred_element_type=F32)
            total = (total + arrived_ref[...].astype(F32)).astype(BF)
            pl.when(step < 2)(lambda: kept_ref.__setitem__(..., total))
            pl.when(step == 2)(lambda: first_ref.__setitem__(..., total))
            pl.when(step == 3)(lambda: second_ref.__setitem__(..., total))

        outs = [jax.ShapeDtypeStruct((count, columns), BF) for count in (2 * first, first, second)]
        return pl.pallas_call(
            kernel,
            out_shape=outs,
            grid=(4,),
            in_specs=[
                pl.BlockSpec((first, tokens), lambda j: (j, 0)),
                pl.BlockSpec(right.shape, lambda j: (0, 0)),
                pl.BlockSpec((first, columns), lambda j: (j, 0)),
            ],
            out_specs=[
                pl.BlockSpec((first, columns), lambda j: (jnp.minimum(j, 1), 0)),
                pl.BlockSpec((first, columns), lambda j: (0, 0)),
                pl.BlockSpec((first, columns), lambda j: (0, 0)),
            ],
            cost_estimate=cost(
                2 * left.shape[0] * tokens * columns, [left, right, arrived, *outs]
            ),
            name="stay_rows",
        )(left, right, arrived)


def wide_tile(columns):
    return next(tile for tile in (1536, 1152, 768, 512, 384, 256, 128) if columns % tile == 0)


def run_through(flight):
    parts = None
    try:
        while True:
            _, parts = flight.send(parts)
    except StopIteration:
        pass


def modulation_flight(block, bias, stages, result):
    for stage in stages[:-1]:
        half = block.shape[0] // 2
        arrived = yield 1, swap_bit(block[half:], stage)
        block = block[:half] + arrived
    arrived = yield 1, swap_bit(block, stages[-1])
    result.append(block + arrived + bias[None])


def gather_flight(shard, rows, cut, routes, waits, result):
    core_stage, first_route, second_route, far_stages = routes
    waits = [1] * (len(far_stages) - 2) + list(waits)
    parts = yield 1, shard
    shard = jnp.concatenate(parts, axis=1) if len(parts) > 1 else parts[0]
    if shard.shape[0] < rows:
        shard = jnp.pad(shard, ((0, rows - shard.shape[0]), (0, 0)))
    blocks = [shard]
    for stage in reversed(far_stages):
        sent = jnp.concatenate(blocks, axis=0) if len(blocks) > 1 else blocks[0]
        arrived = yield waits.pop(0), swap_bit(sent, stage)
        blocks = blocks + [
            arrived[start : start + rows] for start in range(0, arrived.shape[0], rows)
        ]
    owned = [
        jnp.concatenate([block[:cut] for block in blocks], axis=0),
        jnp.concatenate([block[cut:] for block in blocks], axis=0),
    ]
    routes = (second_route, first_route)
    arrived = yield (
        waits.pop(0),
        [swap_bit(part, route[0]) for part, route in zip(owned, routes)],
    )
    pairs = [jnp.concatenate([part, more], axis=0) for part, more in zip(owned, arrived)]
    fars = yield waits.pop(0), [swap_bit(pair, route[1]) for pair, route in zip(pairs, routes)]
    others = yield (
        waits.pop(0),
        [[swap_bit(pair, core_stage), swap_bit(far, core_stage)] for pair, far in zip(pairs, fars)],
    )
    for pair, far, other in zip(pairs, fars, others):
        result.append((pair, far, other[0], other[1]))


def take_chunks(left, places, chunk_rows):
    far_count = places.shape[0] - 3
    columns = left.shape[1]
    part_rows = chunk_rows // 2

    def take(places_ref, in_ref, stay_ref, away_ref):
        x_here, y_here, core_here = places_ref[0], places_ref[1], places_ref[2]
        for half in range(2):
            for one in range(2):
                for two in range(2):
                    x_place = jnp.bitwise_xor(x_here, two if half else one)
                    y_place = jnp.bitwise_xor(y_here, one if half else two)
                    stay_ref[two, half, one, 0] = in_ref[x_place, 0, y_place, core_here, half]
                    away_ref[two, half, one, 0] = in_ref[x_place, 0, y_place, 1 - core_here, half]

    shape = (2, 2, 2, far_count, part_rows, columns)
    out_spec = pl.BlockSpec(
        (2, 2, 2, 1, part_rows, columns), lambda i, places: (0, 0, 0, i, 0, 0)
    )
    parts = pl.pallas_call(
        take,
        out_shape=[jax.ShapeDtypeStruct(shape, left.dtype)] * 2,
        grid_spec=pltpu.PrefetchScalarGridSpec(
            num_scalar_prefetch=1,
            grid=(far_count,),
            in_specs=[
                pl.BlockSpec(
                    (2, 1, 2, 2, 2, part_rows, columns),
                    lambda i, places: (0, places[3 + i], 0, 0, 0, 0, 0),
                )
            ],
            out_specs=[out_spec, out_spec],
        ),
        cost_estimate=pl.CostEstimate(
            flops=0, bytes_accessed=4 * left.size, transcendentals=0
        ),
        name="take_chunks",
    )(places, left.reshape(2, far_count, 2, 2, 2, part_rows, columns))
    return [part.reshape(left.shape[0] // 2, columns) for part in parts]


def place_chunks(first, second, places, out_shape):
    far_count = places.shape[0] - 3
    columns = out_shape[1]
    rows = first[0].shape[0] // (2 * far_count)
    pieces = [piece.reshape(2, far_count, rows, columns) for piece in (*first, *second)]

    def place(places_ref, *refs):
        out_ref = refs[-1]
        x_here, y_here, core_here = places_ref[0], places_ref[1], places_ref[2]
        for half in range(2):
            for core in range(2):
                for two in range(2):
                    ref = refs[4 * half + 2 * core + two]
                    for one in range(2):
                        x_place = jnp.bitwise_xor(x_here, two if half else one)
                        y_place = jnp.bitwise_xor(y_here, one if half else two)
                        core_place = jnp.bitwise_xor(core_here, core)
                        out_ref[x_place, 0, y_place, core_place, half] = ref[one, 0]

    in_spec = pl.BlockSpec((2, 1, rows, columns), lambda i, places: (0, i, 0, 0))
    view = (2, far_count, 2, 2, 2, rows, columns)
    return pl.pallas_call(
        place,
        out_shape=jax.ShapeDtypeStruct(view, BF),
        grid_spec=pltpu.PrefetchScalarGridSpec(
            num_scalar_prefetch=1,
            grid=(far_count,),
            in_specs=[in_spec] * 8,
            out_specs=pl.BlockSpec(
                (2, 1, 2, 2, 2, rows, columns), lambda i, places: (0, places[3 + i], 0, 0, 0, 0, 0)
            ),
        ),
        cost_estimate=pl.CostEstimate(
            flops=0, bytes_accessed=4 * out_shape[0] * columns, transcendentals=0
        ),
        name="place_chunks",
    )(places, *pieces).reshape(out_shape)


class Tiles:
    def __init__(self, parts, tile, start, count):
        first, second = parts
        self.pieces = [piece for pair in zip(first, second) for piece in pair]
        self.tile, self.start, self.count = tile, start, count
        self.rows = sum(piece.shape[0] for piece in self.pieces)

    def operands(self):
        return list(self.pieces)

    def specs(self):
        return [
            pl.BlockSpec((piece.shape[0], self.tile), lambda j: (0, self.start + j))
            for piece in self.pieces
        ]

    def weight(self, refs):
        return jnp.concatenate([ref[...] for ref in refs[:8]], axis=0)

    def columns(self):
        return self.count * self.tile


def cost(flops, arrays, transcendentals=0):
    return pl.CostEstimate(
        flops=int(flops),
        bytes_accessed=int(sum(array.size * array.dtype.itemsize for array in arrays)),
        transcendentals=int(transcendentals),
    )


def project(left, tiles, bias, out_dtype, name):
    rows = left.shape[0]
    operands = tiles.operands()

    def kernel(left_ref, bias_ref, *refs):
        out_ref = refs[-1]

        total = jnp.dot(left_ref[...], tiles.weight(refs), preferred_element_type=F32)
        out_ref[...] = (total + bias_ref[...]).astype(out_dtype)

    out = jax.ShapeDtypeStruct((rows, tiles.columns()), out_dtype)
    return pl.pallas_call(
        kernel,
        out_shape=out,
        grid=(tiles.count,),
        in_specs=[
            pl.BlockSpec(left.shape, lambda j: (0, 0)),
            pl.BlockSpec((1, tiles.tile), lambda j: (0, j)),
            *tiles.specs(),
        ],
        out_specs=pl.BlockSpec((rows, tiles.tile), lambda j: (0, j)),
        cost_estimate=cost(2 * rows * left.shape[1] * tiles.columns(), [left, out, *operands]),
        name=name,
    )(left, bias.reshape(1, -1), *operands)


def gelu_parts(value):
    inner = math.sqrt(2.0 / math.pi) * (value + 0.044715 * (value * value * value))
    return jnp.tanh(inner)


def project_up(left, tiles, bias, channel_on):
    rows = left.shape[0]
    groups = channel_on.shape[0]
    operands = tiles.operands()

    def kernel(left_ref, bias_ref, channel_ref, *refs):
        pre_ref, turned_ref = refs[-2:]

        pre = jnp.dot(left_ref[...], tiles.weight(refs), preferred_element_type=F32)
        pre = pre + bias_ref[...]
        pre_ref[...] = pre
        hidden = 0.5 * pre * (1.0 + gelu_parts(pre))
        span = rows // groups
        for group in range(groups):
            part = hidden[group * span : (group + 1) * span] * channel_ref[group : group + 1]
            turned_ref[:, group * span : (group + 1) * span] = part.T.astype(BF)

    pre = jax.ShapeDtypeStruct((rows, tiles.columns()), F32)
    turned = jax.ShapeDtypeStruct((tiles.columns(), rows), BF)
    return pl.pallas_call(
        kernel,
        out_shape=[pre, turned],
        grid=(tiles.count,),
        in_specs=[
            pl.BlockSpec(left.shape, lambda j: (0, 0)),
            pl.BlockSpec((1, tiles.tile), lambda j: (0, j)),
            pl.BlockSpec((groups, tiles.tile), lambda j: (0, j)),
            *tiles.specs(),
        ],
        out_specs=[
            pl.BlockSpec((rows, tiles.tile), lambda j: (0, j)),
            pl.BlockSpec((tiles.tile, rows), lambda j: (j, 0)),
        ],
        cost_estimate=cost(
            2 * rows * left.shape[1] * tiles.columns(), [left, pre, turned, *operands], pre.size
        ),
        name="project_up",
    )(left, bias.reshape(1, -1), channel_on, *operands)


def project_back(right, tiles, order, parts, name):
    rows = right.shape[0]
    operands = tiles.operands()
    width = order.shape[1]

    def kernel(right_ref, order_ref, *refs):
        out_ref, total_ref = refs[-2:]
        index = pl.program_id(0)

        @pl.when(index == 0)
        def _():
            total_ref[...] = jnp.zeros_like(total_ref)

        total_ref[...] += contract(right_ref[...], tiles.weight(refs), 1, 1)

        @pl.when(index == tiles.count - 1)
        def _():
            rest = total_ref[...]
            out = None
            for part in range(parts):
                high = rest.astype(BF)
                placed = jnp.dot(high, order_ref[...], preferred_element_type=F32)
                out = placed if out is None else out + placed
                if part < parts - 1:
                    rest = rest - high.astype(F32)
            out_ref[...] = out

    out = jax.ShapeDtypeStruct((rows, width), F32)
    return pl.pallas_call(
        kernel,
        out_shape=out,
        grid=(tiles.count,),
        in_specs=[
            pl.BlockSpec((rows, tiles.tile), lambda j: (0, j)),
            pl.BlockSpec(order.shape, lambda j: (0, 0)),
            *tiles.specs(),
        ],
        out_specs=pl.BlockSpec(out.shape, lambda j: (0, 0)),
        scratch_shapes=[pltpu.VMEM((rows, tiles.rows), F32)],
        cost_estimate=cost(
            2 * rows * tiles.rows * (tiles.columns() + parts * width), [right, out, order, *operands]
        ),
        name=name,
    )(right, order, *operands)


def hidden_back(down_grad, full_down, pre, channel_on, tile):
    rows, width = down_grad.shape
    groups = channel_on.shape[0]
    columns = pre.shape[1]

    def kernel(grad_ref, weight_ref, pre_ref, channel_ref, out_ref, sum_ref):
        value = pre_ref[...]
        tanh = gelu_parts(value)
        slope = 0.5 * (1.0 + tanh) + 0.5 * value * (1.0 - tanh * tanh) * math.sqrt(
            2.0 / math.pi
        ) * (1.0 + 3.0 * 0.044715 * value * value)
        grad = contract(grad_ref[...], weight_ref[...], 1, 1) * slope
        span = rows // groups
        total = None
        for group in range(groups):
            part = (
                grad[group * span : (group + 1) * span] * channel_ref[group : group + 1]
            ).astype(BF)
            out_ref[group * span : (group + 1) * span] = part
            along = jnp.sum(part.astype(F32), axis=0, keepdims=True)
            total = along if total is None else total + along
        sum_ref[...] = total

    out = jax.ShapeDtypeStruct((rows, columns), BF)
    sums = jax.ShapeDtypeStruct((1, columns), F32)
    return pl.pallas_call(
        kernel,
        out_shape=[out, sums],
        grid=(columns // tile,),
        in_specs=[
            pl.BlockSpec(down_grad.shape, lambda j: (0, 0)),
            pl.BlockSpec((tile, width), lambda j: (j, 0)),
            pl.BlockSpec((rows, tile), lambda j: (0, j)),
            pl.BlockSpec((groups, tile), lambda j: (0, j)),
        ],
        out_specs=[
            pl.BlockSpec((rows, tile), lambda j: (0, j)),
            pl.BlockSpec((1, tile), lambda j: (0, j)),
        ],
        cost_estimate=cost(
            2 * rows * width * columns, [down_grad, full_down, pre, out], rows * columns
        ),
        name="hidden_back",
    )(down_grad, full_down, pre, channel_on)


def head_window(head, head_size, width):
    start = jnp.minimum(head * head_size // 128, width // 128 - 2) * 128
    lane = lax.broadcasted_iota(jnp.int32, (1, 256), 1) + start
    inside = (lane >= head * head_size) & (lane < (head + 1) * head_size)
    return pl.multiple_of(start, 128), inside


def attend(qkv, other, head_on, block_mask, head_count):
    rows = qkv.shape[0]
    width = qkv.shape[1] // 3
    head_size = width // head_count
    groups = head_on.shape[0]
    span = rows // groups
    factor = 1.0 / math.sqrt(head_size) / math.log(2.0)

    def kernel(
        qkv_ref, key_ref, value_ref, head_ref, mask_ref, mixed_ref, wide_ref, total_ref
    ):
        head = pl.program_id(0)
        start, inside = head_window(head, head_size, width)
        window = pl.ds(start, 256)
        key_window = pl.ds(start + width, 256)
        value_window = pl.ds(start + 2 * width, 256)
        keys = (qkv_ref[:, key_window], key_ref[:, window])
        values = (qkv_ref[:, value_window], value_ref[:, window])
        for group in range(groups):
            at = pl.ds(group * span, span)
            query = qkv_ref[at, window]
            query = jnp.where(inside, query, jnp.zeros_like(query))
            scores = [
                contract(query, key, 1, 1) * factor
                + mask_ref[group : group + 1, side * rows : (side + 1) * rows]
                for side, key in enumerate(keys)
            ]
            largest = jnp.maximum(
                jnp.max(scores[0], axis=1, keepdims=True), jnp.max(scores[1], axis=1, keepdims=True)
            )
            powers = [jnp.exp2(score - largest) for score in scores]
            total = jnp.sum(powers[0], axis=1, keepdims=True) + jnp.sum(
                powers[1], axis=1, keepdims=True
            )
            inverse = 1.0 / total
            out = None
            for power, value in zip(powers, values):
                part = jnp.dot((power * inverse).astype(BF), value, preferred_element_type=F32)
                out = part if out is None else out + part
            out = out * head_ref[group : group + 1, window]
            wide_ref[at, window] = jnp.where(inside, out, wide_ref[at, window])
            mixed_ref[at, window] = jnp.where(inside, out.astype(BF), mixed_ref[at, window])
            lane = lax.broadcasted_iota(jnp.int32, (1, 128), 1)
            total_ref[at, :] = jnp.where(
                lane == head, largest + jnp.log2(total), total_ref[at, :]
            )

    mixed = jax.ShapeDtypeStruct((rows, width), BF)
    wide = jax.ShapeDtypeStruct((rows, width), F32)
    totals = jax.ShapeDtypeStruct((rows, 128), F32)
    operands = (qkv, other, other, head_on, block_mask)
    in_specs = [pl.BlockSpec(array.shape, lambda h: (0, 0)) for array in operands]
    in_specs[1] = pl.BlockSpec((rows, width), lambda h: (0, 1))
    in_specs[2] = pl.BlockSpec((rows, width), lambda h: (0, 2))
    return pl.pallas_call(
        kernel,
        out_shape=[mixed, wide, totals],
        grid=(head_count,),
        in_specs=in_specs,
        out_specs=[pl.BlockSpec(array.shape, lambda h: (0, 0)) for array in (mixed, wide, totals)],
        cost_estimate=cost(
            4 * head_count * rows * 2 * rows * 256, [qkv, other, mixed], head_count * rows * 2 * rows
        ),
        name="attend",
    )(*operands)


def head_terms(key, value, query, grad, row, along, factor):
    probs = jnp.exp2(contract(key, query, 1, 1) * factor + row)
    grad_scores = (probs * (contract(value, grad, 1, 1) - along)).astype(BF)
    return probs.astype(BF), grad_scores


def head_rows(ref, window, inside):
    values = ref[:, window]
    return jnp.where(inside, values, jnp.zeros_like(values))


def attend_back(qkv, other, grad_mixed, totals, along, block_mask, head_count):
    rows = qkv.shape[0]
    width = qkv.shape[1] // 3
    head_size = width // head_count
    blocks = block_mask.shape[0]
    span = 2 * rows // blocks
    scale = 1.0 / math.sqrt(head_size)
    factor = scale / math.log(2.0)

    def kernel(
        qkv_ref, key_ref, value_ref, grad_ref, totals_ref, along_ref, mask_ref, query_out, pair_out
    ):
        head = pl.program_id(0)
        start, inside = head_window(head, head_size, width)
        window = pl.ds(start, 256)
        key_window = pl.ds(start + width, 256)
        value_window = pl.ds(start + 2 * width, 256)
        query = head_rows(qkv_ref, window, inside)
        grad = head_rows(grad_ref, window, inside)
        total = totals_ref[pl.ds(head, 1), :]
        along = along_ref[pl.ds(head, 1), :]
        query_grad = None
        for block in range(blocks):
            own = block < blocks // 2
            at = pl.ds((block if own else block - blocks // 2) * span, span)
            key = qkv_ref[at, key_window] if own else key_ref[at, window]
            value = qkv_ref[at, value_window] if own else value_ref[at, window]
            row = mask_ref[block : block + 1, :] - total
            probs, grad_scores = head_terms(key, value, query, grad, row, along, factor)
            if own:
                key_part = jnp.dot(grad_scores, query, preferred_element_type=F32)
                value_part = jnp.dot(probs, grad, preferred_element_type=F32)
                pair_out[at, window] = jnp.where(inside, key_part, pair_out[at, window])
                pair_out[at, key_window] = jnp.where(inside, value_part, pair_out[at, key_window])
            part = contract(grad_scores, key, 0, 0)
            query_grad = part if query_grad is None else query_grad + part
        query_out[:, window] = jnp.where(
            inside, (query_grad * scale).astype(BF), query_out[:, window]
        )

    outs = [
        jax.ShapeDtypeStruct((rows, width), BF),
        jax.ShapeDtypeStruct((rows, 2 * width), F32),
    ]
    operands = (qkv, other, other, grad_mixed, totals, along, block_mask)
    in_specs = [pl.BlockSpec(array.shape, lambda h: (0, 0)) for array in operands]
    in_specs[1] = pl.BlockSpec((rows, width), lambda h: (0, 1))
    in_specs[2] = pl.BlockSpec((rows, width), lambda h: (0, 2))
    return pl.pallas_call(
        kernel,
        out_shape=outs,
        grid=(head_count,),
        in_specs=in_specs,
        out_specs=[pl.BlockSpec(array.shape, lambda h: (0, 0)) for array in outs],
        cost_estimate=cost(
            8 * head_count * rows * 2 * rows * 256, [qkv, qkv, *outs], head_count * rows * 2 * rows
        ),
        name="attend_back",
    )(*operands)


def attend_back_other(
    qkv, other, other_grad, other_totals, other_along, block_mask, query_grad, pair, head_count
):
    rows = qkv.shape[0]
    width = qkv.shape[1] // 3
    head_size = width // head_count
    blocks = block_mask.shape[0]
    span = rows // blocks
    scale = 1.0 / math.sqrt(head_size)
    factor = scale / math.log(2.0)

    def kernel(
        key_ref, value_ref, other_ref, grad_ref, totals_ref, along_ref, mask_ref, query_ref, pair_ref,
        out_ref,
    ):
        head = pl.program_id(0)

        @pl.when(head == 0)
        def _():
            out_ref[:, :width] = query_ref[...]

        start, inside = head_window(head, head_size, width)
        window = pl.ds(start, 256)
        key_window = pl.ds(start + width, 256)
        value_window = pl.ds(start + 2 * width, 256)
        query = head_rows(other_ref, window, inside)
        grad = head_rows(grad_ref, window, inside)
        total = totals_ref[pl.ds(head, 1), :]
        along = along_ref[pl.ds(head, 1), :]
        for block in range(blocks):
            at = pl.ds(block * span, span)
            row = mask_ref[block : block + 1, :] - total
            probs, grad_scores = head_terms(
                key_ref[at, window], value_ref[at, window], query, grad, row, along, factor
            )
            key_part = pair_ref[at, window] + jnp.dot(
                grad_scores, query, preferred_element_type=F32
            )
            value_part = pair_ref[at, key_window] + jnp.dot(
                probs, grad, preferred_element_type=F32
            )
            out_ref[at, key_window] = jnp.where(
                inside, (key_part * scale).astype(BF), out_ref[at, key_window]
            )
            out_ref[at, value_window] = jnp.where(
                inside, value_part.astype(BF), out_ref[at, value_window]
            )

    out = jax.ShapeDtypeStruct(qkv.shape, BF)
    operands = (
        qkv, qkv, other, other_grad, other_totals, other_along, block_mask, query_grad, pair
    )
    in_specs = [pl.BlockSpec(array.shape, lambda h: (0, 0)) for array in operands]
    in_specs[0] = pl.BlockSpec((rows, width), lambda h: (0, 1))
    in_specs[1] = pl.BlockSpec((rows, width), lambda h: (0, 2))
    in_specs[2] = pl.BlockSpec((rows, width), lambda h: (0, 0))
    return pl.pallas_call(
        kernel,
        out_shape=out,
        grid=(head_count,),
        in_specs=in_specs,
        out_specs=pl.BlockSpec(out.shape, lambda h: (0, 0)),
        cost_estimate=cost(
            8 * head_count * rows * rows * 256, [qkv, pair, out], head_count * rows * rows
        ),
        name="attend_back_other",
    )(*operands)


def cond_columns(steps, first, count, model_width):
    half_width = model_width // 2
    index = first + jnp.arange(count, dtype=jnp.int32)
    is_sine = index >= half_width
    place = jnp.where(is_sine, index - half_width, index).astype(F32)
    frequency = jnp.exp(-math.log(10000.0) * place / half_width)
    angles = steps.astype(F32)[:, None] * frequency[None, :]
    values = jnp.where(is_sine[None, :], jnp.sin(angles), jnp.cos(angles))
    return jax.nn.silu(values).astype(BF)


def normalize(values):
    centered = values - jnp.mean(values, axis=-1, keepdims=True)
    spread = jnp.mean(centered * centered, axis=-1, keepdims=True)
    inverse = lax.rsqrt(spread + 1e-06)
    return centered * inverse, inverse


def normalize_back(grad_normed, normed, inverse):
    along = jnp.mean(grad_normed * normed, axis=-1, keepdims=True)
    level = jnp.mean(grad_normed, axis=-1, keepdims=True)
    return inverse * (grad_normed - level - normed * along)


def body(
    tokens,
    qkv_weight,
    out_weight,
    up_weight,
    down_weight,
    mod_weight,
    qv_bias,
    out_bias,
    up_bias,
    down_bias,
    mod_bias,
    row_items,
    timesteps,
    head_mask,
    channel_mask,
    token_keep,
    cotangent,
):
    layer_count = qkv_weight.shape[0]
    width = out_weight.shape[2]
    hidden_width = up_weight.shape[2]
    head_count = head_mask.shape[3]
    head_size = width // head_count
    item_count = timesteps.shape[1]
    local_rows = tokens.shape[0]
    row_len = 2 * local_rows
    group_rows = row_len // item_count
    group_count = local_rows // group_rows
    scale_factor = 1.0 / math.sqrt(head_size)
    seq_count = lax.axis_size("seq")
    seq_bits = seq_count.bit_length() - 1
    device_count = 2 * seq_count
    half_index = lax.axis_index("fsdp")
    seq_index = lax.axis_index("seq")
    flat_index = half_index * seq_count + seq_index
    shard_rows = mod_weight.shape[1]
    items_here = row_items[0]
    far_stages = [("seq", bit) for bit in range(2, seq_bits)]
    core_stage = ("seq", 0)

    padded_rows = -(-shard_rows // 8) * 8
    row_cut = (padded_rows + 8) // 16 * 8
    x_stage, y_stage = ("fsdp", 0), ("seq", 1)
    routes = (core_stage, (y_stage, x_stage), (x_stage, y_stage), far_stages)
    far_count = 1 << len(far_stages)

    def flat_mask(stage):
        return seq_count if stage[0] == "fsdp" else 1 << stage[1]

    chunk_masks, chunk_places = [], []
    for core_mask in (0, 1):
        for two in range(2):
            for part, route in enumerate(routes[1:3]):
                part_rows = padded_rows - row_cut if part else row_cut
                first_mask = flat_mask(route[0]) if two else 0
                for mask in relative_masks([route[1], *far_stages], flat_mask):
                    chunk_masks += [core_mask ^ first_mask ^ mask] * part_rows
                    chunk_places += list(range(row_cut * part, row_cut * part + part_rows))
    chunk_masks = jnp.array(chunk_masks, jnp.int32)
    chunk_places = jnp.array(chunk_places, jnp.int32)
    source = jnp.where(
        chunk_places < shard_rows, (flat_index ^ chunk_masks) * shard_rows + chunk_places, -1
    )
    order = (source[:, None] == jnp.arange(width, dtype=jnp.int32)[None, :]).astype(BF)

    def ordered(left):
        return contract(left, order, 1, 1).astype(BF)

    feed = Feed()
    place_table = jnp.stack(
        [half_index, (seq_index >> 1) & 1, seq_index & 1]
        + [
            (seq_index >> 2) ^ (mask >> 2)
            for mask in relative_masks(far_stages, lambda stage: 1 << stage[1])
        ]
    ).astype(jnp.int32)

    def scatter_ordered(lefts, rights, waits, result):
        cuts = (far_count * 2 * row_cut, far_count * 2 * (padded_rows - row_cut))
        grads = ColumnGrads(lefts, rights, width)
        feed.start(reduce_flight(grads, routes, cuts, shard_rows, waits, result))

    def scatter_chunks(turned, right, waits, result):
        rows = turned.shape[0] // device_count
        grads = RowGrads(*take_chunks(turned, place_table, rows), right)
        cuts = (far_count * rows, far_count * rows)
        feed.start(reduce_flight(grads, routes, cuts, rows, waits, result))

    gathered = []

    def unit_ticks(unit):
        early = ((0, 1, 2, 4, 7, 8), (0, 2, 4, 9, 11, 12), (5, 9, 10, 12, 14, 15))
        late = ((9, 10, 13, 14, 16, 17), (10, 13, 14, 16, 20, 21), (14, 16, 19, 20, 24, 25))
        if unit < 3:
            return early[unit]
        return tuple(tick + 10 * (unit // 3 - 1) for tick in late[unit % 3])

    for layer in range(layer_count):
        for index, (shard, rows, cut) in enumerate(
            (
                ((qkv_weight[layer],), padded_rows, row_cut),
                ((up_weight[layer], out_weight[layer]), padded_rows, row_cut),
                ((down_weight[layer],), down_weight.shape[1], down_weight.shape[1] // 2),
            )
        ):
            result = []
            gathered.append(result)
            start, *due = unit_ticks(3 * layer + index)
            waits = [after - before for before, after in zip([start] + due, due)]
            feed.at(start, gather_flight(list(shard), rows, cut, routes, waits, result))

    def qkv_tiles(layer):
        return Tiles(gathered[3 * layer], width, 0, 3)

    def up_tiles(layer):
        tile = wide_tile(hidden_width) // 2
        return Tiles(gathered[3 * layer + 1], tile, 0, hidden_width // tile)

    def out_tiles(layer):
        return Tiles(gathered[3 * layer + 1], width, hidden_width // width, 1)

    biases = (qv_bias, out_bias, up_bias, down_bias, mod_bias)
    steps_high = (timesteps // 32).astype(BF)
    steps_low = (timesteps % 32).astype(BF)
    step_rows = jnp.concatenate([steps_high, steps_low], axis=0)
    if layer_count > 2:
        step_rows = jnp.pad(step_rows, ((0, layer_count - 2), (0, 0)))
    small = jnp.concatenate([*biases, step_rows], axis=1)
    small = feed.tick(small)
    small_stages = [("seq", bit) for bit in reversed(range(seq_bits))] + [x_stage]
    for index, stage in enumerate(small_stages):
        small = jnp.concatenate([small, swap_bit(small, stage)], axis=0)
        if index == 1:
            small = feed.tick(small)
    small_masks = jnp.array(relative_masks(list(reversed(small_stages)), flat_mask), jnp.int32)
    put_back = (flat_index ^ small_masks)[None, :] == jnp.arange(device_count)[:, None]
    small_columns = small.shape[1]
    every_small = jnp.dot(
        put_back.astype(BF),
        small.reshape(device_count, layer_count * small_columns),
        preferred_element_type=F32,
    ).reshape(device_count, layer_count, small_columns)
    bias_columns = small_columns - item_count
    every_small, tokens, head_mask, channel_mask, token_keep = feed.tick(
        (every_small, tokens, head_mask, channel_mask, token_keep)
    )
    step_parts = every_small[:seq_count, :2, bias_columns:].reshape(seq_count, 2 * item_count)

    def unpack_biases(every):
        offset = 0
        full = []
        for bias in biases:
            columns = bias.shape[1]
            full.append(
                [every[:, layer, offset : offset + columns].reshape(-1) for layer in range(layer_count)]
            )
            offset += columns
        return full

    every_step = step_parts[:, :item_count] * 32.0 + step_parts[:, item_count:]

    cond_every = cond_columns(every_step.reshape(-1), flat_index * shard_rows, shard_rows, width)
    seq_masks = jnp.array(
        relative_masks([("seq", bit) for bit in range(seq_bits)], lambda stage: 1 << stage[1]),
        jnp.int32,
    )
    pick_row = (seq_index ^ seq_masks)[:, None] == jnp.arange(seq_count)[None, :]
    cond_relative = (
        jnp.sum(
            jnp.where(
                pick_row[:, :, None, None],
                cond_every.astype(F32).reshape(1, seq_count, item_count, shard_rows),
                0.0,
            ),
            axis=1,
        )
        .astype(BF)
        .reshape(seq_count * item_count, shard_rows)
    )

    mod_stages = [("seq", bit) for bit in range(seq_bits)] + [("fsdp", 0)]
    modulations = [[] for _ in range(layer_count)]

    def modulation_part(layer):
        return jnp.dot(cond_relative, mod_weight[layer], preferred_element_type=F32)

    full_biases = unpack_biases(every_small)
    block = feed.tick(modulation_part(0))
    for index, stage in enumerate(mod_stages[:-1]):
        half = block.shape[0] // 2
        block = block[:half] + swap_bit(block[half:], stage)
        if index == 1:
            block, full_biases = feed.tick((block, full_biases))
    block = feed.tick(block + swap_bit(block, mod_stages[-1]))
    modulations[0].append(block + full_biases[4][0][None])
    for layer in range(1, layer_count):
        flight = modulation_flight(
            modulation_part(layer), full_biases[4][layer], mod_stages, modulations[layer]
        )
        feed.at(10 * layer - 1, flight)

    group_item = (
        (half_index * local_rows + jnp.arange(group_count, dtype=jnp.int32) * group_rows)
        * items_here
        // row_len
    )
    other_item = (
        ((1 - half_index) * local_rows + jnp.arange(group_count, dtype=jnp.int32) * group_rows)
        * items_here
        // row_len
    )
    group_is = group_item[:, None] == jnp.arange(item_count, dtype=jnp.int32)[None, :]

    def of_groups(table):
        return jnp.sum(
            jnp.where(group_is[:, :, None], table.astype(F32)[None], 0.0), axis=1, keepdims=False
        )[:, None, :]

    block_item = jnp.concatenate([group_item, other_item])
    block_mask = jnp.where(group_item[:, None] == block_item[None, :], 0.0, -1e30).astype(F32)
    query_mask = jnp.repeat(block_mask, group_rows, axis=1)
    key_mask = jnp.repeat(block_mask.T, group_rows, axis=1)
    cross_mask = jnp.repeat(block_mask[:, group_count:], group_rows, axis=1)

    head_lanes = (
        jnp.arange(width, dtype=jnp.int32)[None, :] // head_size
        == jnp.arange(head_count, dtype=jnp.int32)[:, None]
    ).astype(F32)

    def grouped(values):
        return values.reshape(group_count, group_rows, values.shape[-1])

    def ungrouped(values):
        return values.reshape(local_rows, values.shape[-1])

    current = grouped(tokens.astype(F32))
    saved_layers = []
    full_downs = []
    for layer in range(layer_count):
        pair_bias, out_b, up_b, down_b = (full_biases[index][layer] for index in range(4))
        current = feed.until(modulations[layer], current)
        (modulation,) = modulations[layer]
        shift_one, scale_one, gate_one, shift_two, scale_two, gate_two = jnp.split(
            of_groups(modulation), 6, axis=2
        )
        head_on = jnp.repeat(of_groups(head_mask[0, layer]), head_size, axis=2)[:, 0]
        channel_on = of_groups(channel_mask[0, layer])[:, 0]
        keep_tok = grouped(token_keep[:, layer].astype(F32)[:, None])
        normed_one, inverse_one = normalize(current)
        low_one = ungrouped((normed_one * (1.0 + scale_one) + shift_one).astype(BF))
        other_one = swap_bit(low_one, x_stage)
        bias_three = jnp.concatenate(
            [pair_bias[:width], jnp.zeros((width,), F32), pair_bias[width:]]
        )
        low_one = feed.tick(low_one)
        low_one = feed.tick(ordered(low_one))
        low_one = feed.tick(low_one)
        low_one = feed.until(gathered[3 * layer], low_one)
        qkv_low = project(low_one, qkv_tiles(layer), bias_three, BF, "project_qkv")
        qkv_low, other_one = lax.optimization_barrier((qkv_low, other_one))
        other_low = project(
            ordered(other_one), qkv_tiles(layer), bias_three, BF, "project_other"
        )
        other_low = feed.tick(other_low)
        mixed_low, mixed_wide, totals = attend(qkv_low, other_low, head_on, query_mask, head_count)
        totals = totals[:, :head_count].T
        other_totals = swap_bit(totals, x_stage)
        mixed_low = feed.tick(mixed_low)
        mixed_low = feed.tick(ordered(mixed_low))
        mixed_low = feed.tick(mixed_low)
        mixed_low = feed.until(gathered[3 * layer + 1], mixed_low)
        branch_one = grouped(project(mixed_low, out_tiles(layer), out_b, F32, "project_out"))
        after_attn = current + gate_one * branch_one
        normed_two, inverse_two = normalize(after_attn)
        low_two = ungrouped((normed_two * (1.0 + scale_two) + shift_two).astype(BF))
        low_two = feed.tick(ordered(low_two))
        hidden_pre, hidden_turned = project_up(low_two, up_tiles(layer), up_b, channel_on)
        hidden_turned = feed.tick(hidden_turned)
        hidden_turned = feed.tick(hidden_turned)
        hidden_turned = feed.until(gathered[3 * layer + 2], hidden_turned)
        full_down = place_chunks(*gathered[3 * layer + 2], place_table, (hidden_width, width))
        full_downs.append(full_down)
        branch_two = grouped(contract(hidden_turned, full_down, 0, 0) + down_b)
        saved_layers.append(
            dict(
                inputs=current,
                scale_one=scale_one,
                gate_one=gate_one,
                scale_two=scale_two,
                gate_two=gate_two,
                head_on=head_on,
                channel_on=channel_on,
                keep_tok=keep_tok,
                low_one=low_one,
                qkv_low=qkv_low,
                other_low=other_low,
                totals=totals,
                other_totals=other_totals,
                mixed_low=mixed_low,
                mixed_wide=mixed_wide,
                branch_one=branch_one,
                after_attn=after_attn,
                low_two=low_two,
                hidden_pre=hidden_pre,
                hidden_turned=hidden_turned,
                branch_two=branch_two,
            )
        )
        current = after_attn + keep_tok * gate_two * branch_two
    output = ungrouped(current).astype(BF)
    output = feed.finish(output)

    cond_rows = jnp.concatenate(
        [
            cond_every.reshape(seq_count, item_count, shard_rows),
            jnp.zeros((seq_count, 8 - item_count, shard_rows), BF),
        ],
        axis=1,
    ).reshape(seq_count * 8, shard_rows)
    cond_twice = jnp.concatenate([cond_rows, cond_rows], axis=0)

    def packet_flight(packet, wait, result):
        every = yield wait, lax.all_gather(packet, AXES, axis=0, tiled=True)
        grad_mod_weight = contract(cond_twice, every, 0, 0)
        sums = jnp.sum(every.astype(F32).reshape(device_count, *packet.shape), axis=0)

        def shard_of(row, start, columns):
            return lax.dynamic_slice_in_dim(row, start + flat_index * columns, columns, 0)

        grad_mod_bias = shard_of(jnp.sum(sums[:item_count], axis=0), 0, mod_bias.shape[1])
        bias_sum = sums[item_count:].reshape(-1)
        parts = []
        start = 0
        for bias in (qv_bias, out_bias, up_bias, down_bias):
            parts.append(shard_of(bias_sum, start, bias.shape[1]))
            start += device_count * bias.shape[1]
        grads = yield 1, (grad_mod_weight, *parts, grad_mod_bias)
        result.append(grads)

    grad_current = grouped(cotangent)
    layer_totals = [None] * layer_count
    for layer in reversed(range(layer_count)):
        saved = saved_layers[layer]
        kept_grad = grad_current * saved["keep_tok"]
        down_grad = ungrouped((kept_grad * saved["gate_two"]).astype(BF))
        grad_gate_two = jnp.sum(kept_grad * saved["branch_two"], axis=1)
        grad_down_bias = jnp.sum(down_grad.astype(F32), axis=0)
        down_rows, up_rows, out_rows, qkv_rows = [], [], [], []
        last = layer == 0
        scatter_chunks(saved["hidden_turned"], down_grad, (1, 1, 1, 2, 1, 1), down_rows)
        up_grad, grad_up_bias = hidden_back(
            down_grad, full_downs[layer], saved["hidden_pre"], saved["channel_on"], wide_tile(hidden_width) // 2
        )
        grad_up_bias = grad_up_bias[0]
        up_grad = feed.tick(feed.tick(up_grad))
        grad_h2 = grouped(project_back(up_grad, up_tiles(layer), order, 2, "back_up"))
        grad_h2 = feed.tick(grad_h2)
        normed_two, inverse_two = normalize(saved["after_attn"])
        grad_shift_two = jnp.sum(grad_h2, axis=1)
        grad_scale_two = jnp.sum(grad_h2 * normed_two, axis=1)
        grad_after = grad_current + normalize_back(
            grad_h2 * (1.0 + saved["scale_two"]), normed_two, inverse_two
        )
        out_grad = ungrouped((grad_after * saved["gate_one"]).astype(BF))
        grad_gate_one = jnp.sum(grad_after * saved["branch_one"], axis=1)
        grad_out_bias = jnp.sum(out_grad.astype(F32), axis=0)
        out_grad = feed.tick(out_grad)
        lefts, rights = (saved["low_two"], saved["mixed_low"]), (up_grad, out_grad)
        up_waits = (2, 0, 2, 2, 2, 1) if last else (2, 0, 2, 2, 2, 3)
        scatter_ordered(lefts, rights, up_waits, up_rows)
        grad_mixed = ungrouped(
            (
                grouped(project_back(out_grad, out_tiles(layer), order, 1, "back_out"))
                * saved["head_on"][:, None]
            ).astype(BF)
        )
        grad_mixed = feed.tick(grad_mixed)
        other_mixed = swap_bit(grad_mixed, x_stage)
        along = lax.dot_general(
            head_lanes,
            saved["mixed_wide"] * grad_mixed.astype(F32),
            (((1,), (1,)), ((), ())),
            precision=lax.Precision.HIGHEST,
            preferred_element_type=F32,
        )
        other_along = swap_bit(along, x_stage)
        grad_query, grad_pair = attend_back(
            saved["qkv_low"],
            saved["other_low"],
            grad_mixed,
            saved["totals"],
            along,
            key_mask,
            head_count,
        )
        grad_pair = feed.tick(grad_pair)
        grad_qkv = attend_back_other(
            saved["qkv_low"],
            saved["other_low"],
            other_mixed,
            saved["other_totals"],
            other_along,
            cross_mask,
            grad_query,
            grad_pair,
            head_count,
        )
        grad_qkv = feed.tick(grad_qkv)
        grad_qkv_bias = jnp.sum(grad_qkv.astype(F32), axis=0)
        qkv_waits = (1, 1, 3, 1) if last else (1, 0, 4, 2, 1, 2)
        scatter_ordered((saved["low_one"],), (grad_qkv,), qkv_waits, qkv_rows)
        if last:
            grad_qkv = feed.tick(feed.tick(grad_qkv))
        grad_h1 = grouped(project_back(grad_qkv, qkv_tiles(layer), order, 2, "back_qkv"))
        grad_h1 = feed.tick(grad_h1)
        normed_one, inverse_one = normalize(saved["inputs"])
        grad_shift_one = jnp.sum(grad_h1, axis=1)
        grad_scale_one = jnp.sum(grad_h1 * normed_one, axis=1)
        grad_inputs = grad_after + normalize_back(
            grad_h1 * (1.0 + saved["scale_one"]), normed_one, inverse_one
        )
        grad_groups = jnp.concatenate(
            [
                grad_shift_one,
                grad_scale_one,
                grad_gate_one,
                grad_shift_two,
                grad_scale_two,
                grad_gate_two,
            ],
            axis=1,
        )
        grad_slots = jnp.sum(jnp.where(group_is[:, :, None], grad_groups[:, None, :], 0.0), axis=0)
        mod_width = grad_slots.shape[1]
        bias_row = jnp.concatenate(
            [
                grad_qkv_bias[:width],
                grad_qkv_bias[2 * width :],
                grad_out_bias,
                grad_up_bias,
                grad_down_bias,
            ]
        )
        spare = jnp.zeros(((8 - item_count) * mod_width - bias_row.shape[0],), F32)
        packet = jnp.concatenate(
            [grad_slots, jnp.concatenate([bias_row, spare]).reshape(8 - item_count, mod_width)],
            axis=0,
        ).astype(BF)
        if last:
            grad_inputs, packet = feed.tick((grad_inputs, packet))
        shared_grads = []
        feed.start(packet_flight(packet, 3 if last else 7, shared_grads))
        grad_current = grad_inputs if last else feed.tick(grad_inputs)
        layer_totals[layer] = (
            qkv_rows,
            up_rows,
            up_rows,
            down_rows,
            shared_grads,
        )
    grad_current = feed.finish(grad_current)
    layer_totals = [
        (
            qkv[0],
            up[0][:, hidden_width:],
            up[0][:, :hidden_width],
            down[0],
            *shared[0],
        )
        for qkv, up, _, down, shared in layer_totals
    ]
    stacked = tuple(
        jnp.stack([layer_totals[layer][index] for layer in range(layer_count)])
        for index in range(10)
    )
    return (output, ungrouped(grad_current), *stacked)


def solution(mesh):
    rows = P(AXES, None)
    matrix = P(None, AXES, None)
    vector = P(None, AXES)
    return jax.shard_map(
        body,
        mesh=mesh,
        in_specs=(
            rows,
            matrix,
            matrix,
            matrix,
            matrix,
            matrix,
            vector,
            vector,
            vector,
            vector,
            vector,
            P("seq"),
            P("seq", None),
            P("seq", None, None, None),
            P("seq", None, None, None),
            rows,
            rows,
        ),
        out_specs=(
            rows,
            rows,
            matrix,
            matrix,
            matrix,
            matrix,
            matrix,
            vector,
            vector,
            vector,
            vector,
            vector,
        ),
        check_vma=False,
    )
```

```python
import math

import jax
import jax.numpy as jnp
from jax import lax
from jax.experimental import pallas as pl
from jax.experimental.pallas import tpu as pltpu
from jax.sharding import PartitionSpec as P

BF = jnp.bfloat16
F32 = jnp.float32
AXES = ("fsdp", "seq")


def swap_bit(block, stage):
    axis, bit = stage
    count = lax.axis_size(axis)
    return lax.ppermute(block, axis, [(low, low ^ (1 << bit)) for low in range(count)])


def stage_bit(stage):
    axis, bit = stage
    return (lax.axis_index(axis) >> bit) & 1


def contract(left, right, left_dim, right_dim):
    return lax.dot_general(
        left, right, (((left_dim,), (right_dim,)), ((), ())), preferred_element_type=F32
    )


def relative_masks(stages, mask_of):
    masks = [0]
    for stage in reversed(stages):
        masks = masks + [mask ^ mask_of(stage) for mask in masks]
    return masks


class Feed:
    def __init__(self):
        self.flights = []
        self.ticks = 0
        self.later = {}

    def start(self, flight):
        wait, parts = next(flight)
        self.flights.append((flight, self.ticks + wait - 1, parts))

    def at(self, tick, flight):
        self.later.setdefault(tick, []).append(flight)

    def tick(self, value):
        for flight in self.later.pop(self.ticks, []):
            self.start(flight)
        due = [entry for entry in self.flights if entry[1] <= self.ticks]
        flying = [entry for entry in self.flights if entry[1] > self.ticks]
        self.ticks += 1
        value, arrived = lax.optimization_barrier((value, [parts for _, _, parts in due]))
        for (flight, _, _), parts in zip(due, arrived):
            try:
                wait, sent = flight.send(parts)
                flying.append((flight, self.ticks + wait - 1, sent))
            except StopIteration:
                pass
        self.flights = flying
        return value

    def until(self, result, value):
        while not result:
            value = self.tick(value)
        return value

    def finish(self, value):
        while self.flights or self.later:
            value = self.tick(value)
        return value


def reduce_flight(grads, routes, cuts, rows, waits, result):
    core_stage, first_route, second_route, far_stages = routes
    first, second = cuts
    waits = list(waits) + [1] * 8
    arrived = yield waits[0], swap_bit(grads.away(), core_stage)
    parts = grads.stay(arrived, first, second)
    if waits[1]:
        parts = yield waits[1], parts
    kept, first_sent, second_sent = parts
    first_arrived, second_arrived = yield waits[2], (
        swap_bit(first_sent, first_route[0]),
        swap_bit(second_sent, second_route[0]),
    )

    def add(left, other, low, high):
        return left[low:high].astype(F32) + other[low:high].astype(F32)

    first_kept, second_kept = kept[:first], kept[first:]
    half_first, half_second = first // 2, second // 2
    first_sent = add(first_kept, first_arrived, half_first, first).astype(BF)
    second_sent = add(second_kept, second_arrived, half_second, second).astype(BF)
    first_kept = add(first_kept, first_arrived, 0, half_first).astype(BF)
    second_kept = add(second_kept, second_arrived, 0, half_second).astype(BF)
    first_arrived, second_arrived = yield waits[3], (
        swap_bit(first_sent, first_route[1]),
        swap_bit(second_sent, second_route[1]),
    )
    for index, stage in enumerate(far_stages):
        first, second = half_first, half_second
        half_first, half_second = first // 2, second // 2
        sent = jnp.concatenate(
            [
                add(first_kept, first_arrived, half_first, first),
                add(second_kept, second_arrived, half_second, second),
            ],
            axis=0,
        ).astype(BF)
        first_kept = add(first_kept, first_arrived, 0, half_first).astype(BF)
        second_kept = add(second_kept, second_arrived, 0, half_second).astype(BF)
        arrived = yield waits[4 + index], swap_bit(sent, stage)
        first_arrived, second_arrived = arrived[:half_first], arrived[half_first:]
    block = jnp.concatenate(
        [
            add(first_kept, first_arrived, 0, half_first),
            add(second_kept, second_arrived, 0, half_second),
        ],
        axis=0,
    )
    result.append(block[:rows])


class ColumnGrads:
    def __init__(self, lefts, rights, tile):
        self.lefts, self.rights, self.tile = lefts, rights, tile
        self.half = lefts[0].shape[1] // 2
        self.counts = [right.shape[1] // tile for right in rights]

    def call(self, index, arrived, pieces, name):
        half, tile = self.half, self.tile
        tokens = self.lefts[0].shape[0]
        pairs = len(self.lefts)
        starts = [sum(self.counts[:pair]) for pair in range(pairs)]
        columns = sum(self.counts) * tile

        def kernel(*refs):
            lefts, rights = refs[:pairs], refs[pairs : 2 * pairs]
            rest = refs[2 * pairs :]
            if arrived is not None:
                arrived_ref, rest = rest[0], rest[1:]
            out_refs, turned_ref = rest[:-1], rest[-1]
            step = pl.program_id(0)

            def work(left_ref, right_ref, start):
                @pl.when(step == start)
                def _():
                    turned_ref[...] = left_ref[...].astype(F32).T.astype(BF)

                total = jnp.dot(turned_ref[...], right_ref[...], preferred_element_type=F32)
                if arrived is not None:
                    total = total + arrived_ref[...].astype(F32)
                total = total.astype(BF)
                low = 0
                for out_ref, count in zip(out_refs, pieces):
                    out_ref[...] = total[low : low + count]
                    low += count

            for left_ref, right_ref, start, count in zip(lefts, rights, starts, self.counts):
                if pairs == 1:
                    work(left_ref, right_ref, start)
                else:
                    pl.when((step >= start) & (step < start + count))(
                        lambda l=left_ref, r=right_ref, s=start: work(l, r, s)
                    )

        def right_spec(start, count):
            return pl.BlockSpec(
                (tokens, tile), lambda j: (0, jnp.clip(j - start, 0, count - 1))
            )

        operands = [*self.lefts, *self.rights]
        in_specs = [pl.BlockSpec((tokens, half), lambda j: (0, index)) for _ in self.lefts]
        in_specs += [right_spec(*pair) for pair in zip(starts, self.counts)]
        if arrived is not None:
            operands.append(arrived)
            in_specs.append(pl.BlockSpec((half, tile), lambda j: (0, j)))
        outs = [jax.ShapeDtypeStruct((count, columns), BF) for count in pieces]
        return pl.pallas_call(
            kernel,
            out_shape=outs,
            grid=(sum(self.counts),),
            in_specs=in_specs,
            out_specs=[pl.BlockSpec((count, tile), lambda j: (0, j)) for count in pieces],
            scratch_shapes=[pltpu.VMEM((half, tokens), BF)],
            cost_estimate=cost(2 * half * tokens * columns, [*operands, *outs]),
            name=name,
        )(*operands)

    def away(self):
        return self.call(1, None, [self.half], "away_grad")[0]

    def stay(self, arrived, first, second):
        return self.call(0, arrived, [self.half - first - second, first, second], "stay_grad")


class RowGrads:
    def __init__(self, stay, away, right):
        self.stay_rows, self.away_rows, self.right = stay, away, right

    def away(self):
        return contract(self.away_rows, self.right, 1, 0).astype(BF)

    def stay(self, arrived, first, second):
        left, right = self.stay_rows, self.right
        tokens, columns = right.shape
        assert first == second

        def kernel(left_ref, right_ref, arrived_ref, kept_ref, first_ref, second_ref):
            step = pl.program_id(0)
            total = jnp.dot(left_ref[...], right_ref[...], preferred_element_type=F32)
            total = (total + arrived_ref[...].astype(F32)).astype(BF)
            pl.when(step < 2)(lambda: kept_ref.__setitem__(..., total))
            pl.when(step == 2)(lambda: first_ref.__setitem__(..., total))
            pl.when(step == 3)(lambda: second_ref.__setitem__(..., total))

        outs = [jax.ShapeDtypeStruct((count, columns), BF) for count in (2 * first, first, second)]
        return pl.pallas_call(
            kernel,
            out_shape=outs,
            grid=(4,),
            in_specs=[
                pl.BlockSpec((first, tokens), lambda j: (j, 0)),
                pl.BlockSpec(right.shape, lambda j: (0, 0)),
                pl.BlockSpec((first, columns), lambda j: (j, 0)),
            ],
            out_specs=[
                pl.BlockSpec((first, columns), lambda j: (jnp.minimum(j, 1), 0)),
                pl.BlockSpec((first, columns), lambda j: (0, 0)),
                pl.BlockSpec((first, columns), lambda j: (0, 0)),
            ],
            cost_estimate=cost(
                2 * left.shape[0] * tokens * columns, [left, right, arrived, *outs]
            ),
            name="stay_rows",
        )(left, right, arrived)


def wide_tile(columns):
    return next(tile for tile in (1536, 1152, 768, 512, 384, 256, 128) if columns % tile == 0)


def run_through(flight):
    parts = None
    try:
        while True:
            _, parts = flight.send(parts)
    except StopIteration:
        pass


def gather_flight(shard, rows, cut, routes, waits, result):
    core_stage, first_route, second_route, far_stages = routes
    waits = [1] * (len(far_stages) - 2) + list(waits)
    parts = yield 1, shard
    shard = jnp.concatenate(parts, axis=1) if len(parts) > 1 else parts[0]
    if shard.shape[0] < rows:
        shard = jnp.pad(shard, ((0, rows - shard.shape[0]), (0, 0)))
    blocks = [shard]
    for stage in reversed(far_stages):
        sent = jnp.concatenate(blocks, axis=0) if len(blocks) > 1 else blocks[0]
        arrived = yield waits.pop(0), swap_bit(sent, stage)
        blocks = blocks + [
            arrived[start : start + rows] for start in range(0, arrived.shape[0], rows)
        ]
    owned = [
        jnp.concatenate([block[:cut] for block in blocks], axis=0),
        jnp.concatenate([block[cut:] for block in blocks], axis=0),
    ]
    routes = (second_route, first_route)
    arrived = yield (
        waits.pop(0),
        [swap_bit(part, route[0]) for part, route in zip(owned, routes)],
    )
    pairs = [jnp.concatenate([part, more], axis=0) for part, more in zip(owned, arrived)]
    fars = yield waits.pop(0), [swap_bit(pair, route[1]) for pair, route in zip(pairs, routes)]
    others = yield (
        waits.pop(0),
        [[swap_bit(pair, core_stage), swap_bit(far, core_stage)] for pair, far in zip(pairs, fars)],
    )
    for pair, far, other in zip(pairs, fars, others):
        result.append((pair, far, other[0], other[1]))


def take_chunks(left, places, chunk_rows):
    far_count = places.shape[0] - 3
    columns = left.shape[1]
    part_rows = chunk_rows // 2

    def take(places_ref, in_ref, stay_ref, away_ref):
        x_here, y_here, core_here = places_ref[0], places_ref[1], places_ref[2]
        for half in range(2):
            for one in range(2):
                for two in range(2):
                    x_place = jnp.bitwise_xor(x_here, two if half else one)
                    y_place = jnp.bitwise_xor(y_here, one if half else two)
                    stay_ref[two, half, one, 0] = in_ref[x_place, 0, y_place, core_here, half]
                    away_ref[two, half, one, 0] = in_ref[x_place, 0, y_place, 1 - core_here, half]

    shape = (2, 2, 2, far_count, part_rows, columns)
    out_spec = pl.BlockSpec(
        (2, 2, 2, 1, part_rows, columns), lambda i, places: (0, 0, 0, i, 0, 0)
    )
    parts = pl.pallas_call(
        take,
        out_shape=[jax.ShapeDtypeStruct(shape, left.dtype)] * 2,
        grid_spec=pltpu.PrefetchScalarGridSpec(
            num_scalar_prefetch=1,
            grid=(far_count,),
            in_specs=[
                pl.BlockSpec(
                    (2, 1, 2, 2, 2, part_rows, columns),
                    lambda i, places: (0, places[3 + i], 0, 0, 0, 0, 0),
                )
            ],
            out_specs=[out_spec, out_spec],
        ),
        cost_estimate=pl.CostEstimate(
            flops=0, bytes_accessed=4 * left.size, transcendentals=0
        ),
        name="take_chunks",
    )(places, left.reshape(2, far_count, 2, 2, 2, part_rows, columns))
    return [part.reshape(left.shape[0] // 2, columns) for part in parts]


def place_chunks(first, second, places, out_shape):
    far_count = places.shape[0] - 3
    columns = out_shape[1]
    rows = first[0].shape[0] // (2 * far_count)
    pieces = [piece.reshape(2, far_count, rows, columns) for piece in (*first, *second)]

    def place(places_ref, *refs):
        out_ref = refs[-1]
        x_here, y_here, core_here = places_ref[0], places_ref[1], places_ref[2]
        for half in range(2):
            for core in range(2):
                for two in range(2):
                    ref = refs[4 * half + 2 * core + two]
                    for one in range(2):
                        x_place = jnp.bitwise_xor(x_here, two if half else one)
                        y_place = jnp.bitwise_xor(y_here, one if half else two)
                        core_place = jnp.bitwise_xor(core_here, core)
                        out_ref[x_place, 0, y_place, core_place, half] = ref[one, 0]

    in_spec = pl.BlockSpec((2, 1, rows, columns), lambda i, places: (0, i, 0, 0))
    view = (2, far_count, 2, 2, 2, rows, columns)
    return pl.pallas_call(
        place,
        out_shape=jax.ShapeDtypeStruct(view, BF),
        grid_spec=pltpu.PrefetchScalarGridSpec(
            num_scalar_prefetch=1,
            grid=(far_count,),
            in_specs=[in_spec] * 8,
            out_specs=pl.BlockSpec(
                (2, 1, 2, 2, 2, rows, columns), lambda i, places: (0, places[3 + i], 0, 0, 0, 0, 0)
            ),
        ),
        cost_estimate=pl.CostEstimate(
            flops=0, bytes_accessed=4 * out_shape[0] * columns, transcendentals=0
        ),
        name="place_chunks",
    )(places, *pieces).reshape(out_shape)


class Tiles:
    def __init__(self, parts, tile, start, count):
        first, second = parts
        self.pieces = [piece for pair in zip(first, second) for piece in pair]
        self.tile, self.start, self.count = tile, start, count
        self.rows = sum(piece.shape[0] for piece in self.pieces)

    def operands(self):
        return list(self.pieces)

    def specs(self):
        return [
            pl.BlockSpec((piece.shape[0], self.tile), lambda j: (0, self.start + j))
            for piece in self.pieces
        ]

    def weight(self, refs):
        return jnp.concatenate([ref[...] for ref in refs[:8]], axis=0)

    def columns(self):
        return self.count * self.tile


def cost(flops, arrays, transcendentals=0):
    return pl.CostEstimate(
        flops=int(flops),
        bytes_accessed=int(sum(array.size * array.dtype.itemsize for array in arrays)),
        transcendentals=int(transcendentals),
    )


def project(left, tiles, bias, out_dtype, name):
    rows = left.shape[0]
    operands = tiles.operands()

    def kernel(left_ref, bias_ref, *refs):
        out_ref = refs[-1]

        total = jnp.dot(left_ref[...], tiles.weight(refs), preferred_element_type=F32)
        out_ref[...] = (total + bias_ref[...]).astype(out_dtype)

    out = jax.ShapeDtypeStruct((rows, tiles.columns()), out_dtype)
    return pl.pallas_call(
        kernel,
        out_shape=out,
        grid=(tiles.count,),
        in_specs=[
            pl.BlockSpec(left.shape, lambda j: (0, 0)),
            pl.BlockSpec((1, tiles.tile), lambda j: (0, j)),
            *tiles.specs(),
        ],
        out_specs=pl.BlockSpec((rows, tiles.tile), lambda j: (0, j)),
        cost_estimate=cost(2 * rows * left.shape[1] * tiles.columns(), [left, out, *operands]),
        name=name,
    )(left, bias.reshape(1, -1), *operands)


def gelu_parts(value):
    inner = math.sqrt(2.0 / math.pi) * (value + 0.044715 * (value * value * value))
    return jnp.tanh(inner)


def project_up(left, tiles, bias, channel_on):
    rows = left.shape[0]
    groups = channel_on.shape[0]
    operands = tiles.operands()

    def kernel(left_ref, bias_ref, channel_ref, *refs):
        pre_ref, turned_ref = refs[-2:]

        pre = jnp.dot(left_ref[...], tiles.weight(refs), preferred_element_type=F32)
        pre = pre + bias_ref[...]
        pre_ref[...] = pre
        hidden = 0.5 * pre * (1.0 + gelu_parts(pre))
        span = rows // groups
        for group in range(groups):
            part = hidden[group * span : (group + 1) * span] * channel_ref[group : group + 1]
            turned_ref[:, group * span : (group + 1) * span] = part.T.astype(BF)

    pre = jax.ShapeDtypeStruct((rows, tiles.columns()), F32)
    turned = jax.ShapeDtypeStruct((tiles.columns(), rows), BF)
    return pl.pallas_call(
        kernel,
        out_shape=[pre, turned],
        grid=(tiles.count,),
        in_specs=[
            pl.BlockSpec(left.shape, lambda j: (0, 0)),
            pl.BlockSpec((1, tiles.tile), lambda j: (0, j)),
            pl.BlockSpec((groups, tiles.tile), lambda j: (0, j)),
            *tiles.specs(),
        ],
        out_specs=[
            pl.BlockSpec((rows, tiles.tile), lambda j: (0, j)),
            pl.BlockSpec((tiles.tile, rows), lambda j: (j, 0)),
        ],
        cost_estimate=cost(
            2 * rows * left.shape[1] * tiles.columns(), [left, pre, turned, *operands], pre.size
        ),
        name="project_up",
    )(left, bias.reshape(1, -1), channel_on, *operands)


def project_back(right, tiles, order, parts, name):
    rows = right.shape[0]
    operands = tiles.operands()
    width = order.shape[1]

    def kernel(right_ref, order_ref, *refs):
        out_ref, total_ref = refs[-2:]
        index = pl.program_id(0)

        @pl.when(index == 0)
        def _():
            total_ref[...] = jnp.zeros_like(total_ref)

        total_ref[...] += contract(right_ref[...], tiles.weight(refs), 1, 1)

        @pl.when(index == tiles.count - 1)
        def _():
            rest = total_ref[...]
            out = None
            for part in range(parts):
                high = rest.astype(BF)
                placed = jnp.dot(high, order_ref[...], preferred_element_type=F32)
                out = placed if out is None else out + placed
                if part < parts - 1:
                    rest = rest - high.astype(F32)
            out_ref[...] = out

    out = jax.ShapeDtypeStruct((rows, width), F32)
    return pl.pallas_call(
        kernel,
        out_shape=out,
        grid=(tiles.count,),
        in_specs=[
            pl.BlockSpec((rows, tiles.tile), lambda j: (0, j)),
            pl.BlockSpec(order.shape, lambda j: (0, 0)),
            *tiles.specs(),
        ],
        out_specs=pl.BlockSpec(out.shape, lambda j: (0, 0)),
        scratch_shapes=[pltpu.VMEM((rows, tiles.rows), F32)],
        cost_estimate=cost(
            2 * rows * tiles.rows * (tiles.columns() + parts * width), [right, out, order, *operands]
        ),
        name=name,
    )(right, order, *operands)


def project_norm_back(right, tiles, order, inputs, residual, scale, branch, gate, name):
    rows = right.shape[0]
    operands = tiles.operands()
    width = order.shape[1]
    groups = scale.shape[0]
    span = rows // groups
    gated = branch is not None
    chunk = min(span, 128)

    def kernel(right_ref, order_ref, inputs_ref, residual_ref, scale_ref, *refs):
        if gated:
            branch_ref, gate_ref, refs = refs[0], refs[1], refs[2:]
        pieces, refs = refs[:8], refs[8:]
        if gated:
            after_ref, product_ref, sums_ref, total_ref = refs
        else:
            after_ref, sums_ref, total_ref = refs
        index = pl.program_id(0)

        @pl.when(index == 0)
        def _():
            total_ref[...] = jnp.zeros_like(total_ref)

        total_ref[...] += contract(right_ref[...], tiles.weight(pieces), 1, 1)

        @pl.when(index == tiles.count - 1)
        def _():
            sums_ref[...] = jnp.zeros_like(sums_ref)

            def add_sum(row, values):
                along = jnp.sum(values, axis=0, keepdims=True)
                sums_ref[row : row + 1, :] = sums_ref[row : row + 1, :] + along

            for low in range(0, rows, chunk):
                at = pl.ds(low, chunk)
                group = low // span
                rest = total_ref[at, :]
                high = rest.astype(BF)
                grad = jnp.dot(high, order_ref[...], preferred_element_type=F32)
                lower = (rest - high.astype(F32)).astype(BF)
                grad = grad + jnp.dot(lower, order_ref[...], preferred_element_type=F32)
                normed, inverse = normalize(inputs_ref[at, :])
                add_sum(group, grad)
                add_sum(groups + group, grad * normed)
                after = residual_ref[at, :] + normalize_back(
                    grad * (1.0 + scale_ref[group : group + 1, :]), normed, inverse
                )
                after_ref[at, :] = after
                if gated:
                    product = (after * gate_ref[group : group + 1, :]).astype(BF)
                    product_ref[at, :] = product
                    add_sum(2 * groups + group, after * branch_ref[at, :])
                    add_sum(3 * groups, product.astype(F32))

    whole = lambda shape: pl.BlockSpec(shape, lambda j: (0, 0))
    wide = jax.ShapeDtypeStruct((rows, width), F32)
    outs = [wide] + ([jax.ShapeDtypeStruct((rows, width), BF)] if gated else [])
    outs.append(jax.ShapeDtypeStruct((3 * groups + 2, width), F32))
    extra = [branch, gate] if gated else []
    others = [order, inputs, residual, scale, *extra]
    return pl.pallas_call(
        kernel,
        out_shape=outs,
        grid=(tiles.count,),
        in_specs=[
            pl.BlockSpec((rows, tiles.tile), lambda j: (0, j)),
            *[whole(array.shape) for array in others],
            *tiles.specs(),
        ],
        out_specs=[whole(out.shape) for out in outs],
        scratch_shapes=[pltpu.VMEM((rows, tiles.rows), F32)],
        cost_estimate=cost(
            2 * rows * tiles.rows * (tiles.columns() + 2 * width), [right, *others, *outs, *operands]
        ),
        name=name,
    )(right, *others, *operands)


def hidden_back(down_grad, full_down, pre, channel_on, tile):
    rows, width = down_grad.shape
    groups = channel_on.shape[0]
    columns = pre.shape[1]

    def kernel(grad_ref, weight_ref, pre_ref, channel_ref, out_ref, sum_ref):
        value = pre_ref[...]
        tanh = gelu_parts(value)
        slope = 0.5 * (1.0 + tanh) + 0.5 * value * (1.0 - tanh * tanh) * math.sqrt(
            2.0 / math.pi
        ) * (1.0 + 3.0 * 0.044715 * value * value)
        grad = contract(grad_ref[...], weight_ref[...], 1, 1) * slope
        span = rows // groups
        total = None
        for group in range(groups):
            part = (
                grad[group * span : (group + 1) * span] * channel_ref[group : group + 1]
            ).astype(BF)
            out_ref[group * span : (group + 1) * span] = part
            along = jnp.sum(part.astype(F32), axis=0, keepdims=True)
            total = along if total is None else total + along
        sum_ref[...] = total

    out = jax.ShapeDtypeStruct((rows, columns), BF)
    sums = jax.ShapeDtypeStruct((1, columns), F32)
    return pl.pallas_call(
        kernel,
        out_shape=[out, sums],
        grid=(columns // tile,),
        in_specs=[
            pl.BlockSpec(down_grad.shape, lambda j: (0, 0)),
            pl.BlockSpec((tile, width), lambda j: (j, 0)),
            pl.BlockSpec((rows, tile), lambda j: (0, j)),
            pl.BlockSpec((groups, tile), lambda j: (0, j)),
        ],
        out_specs=[
            pl.BlockSpec((rows, tile), lambda j: (0, j)),
            pl.BlockSpec((1, tile), lambda j: (0, j)),
        ],
        cost_estimate=cost(
            2 * rows * width * columns, [down_grad, full_down, pre, out], rows * columns
        ),
        name="hidden_back",
    )(down_grad, full_down, pre, channel_on)


def head_window(head, head_size, width):
    start = jnp.minimum(head * head_size // 128, width // 128 - 2) * 128
    lane = lax.broadcasted_iota(jnp.int32, (1, 256), 1) + start
    inside = (lane >= head * head_size) & (lane < (head + 1) * head_size)
    return pl.multiple_of(start, 128), inside


def attend(qkv, other, head_on, block_mask, head_count):
    rows = qkv.shape[0]
    width = qkv.shape[1] // 3
    head_size = width // head_count
    groups = head_on.shape[0]
    span = rows // groups
    factor = 1.0 / math.sqrt(head_size) / math.log(2.0)

    def kernel(
        qkv_ref, key_ref, value_ref, head_ref, mask_ref, mixed_ref, wide_ref, total_ref
    ):
        head = pl.program_id(0)
        start, inside = head_window(head, head_size, width)
        window = pl.ds(start, 256)
        key_window = pl.ds(start + width, 256)
        value_window = pl.ds(start + 2 * width, 256)
        keys = (qkv_ref[:, key_window], key_ref[:, window])
        values = (qkv_ref[:, value_window], value_ref[:, window])
        for group in range(groups):
            at = pl.ds(group * span, span)
            query = qkv_ref[at, window]
            query = jnp.where(inside, query, jnp.zeros_like(query))
            scores = [
                contract(query, key, 1, 1) * factor
                + mask_ref[group : group + 1, side * rows : (side + 1) * rows]
                for side, key in enumerate(keys)
            ]
            largest = jnp.maximum(
                jnp.max(scores[0], axis=1, keepdims=True), jnp.max(scores[1], axis=1, keepdims=True)
            )
            powers = [jnp.exp2(score - largest) for score in scores]
            total = jnp.sum(powers[0], axis=1, keepdims=True) + jnp.sum(
                powers[1], axis=1, keepdims=True
            )
            inverse = 1.0 / total
            out = None
            for power, value in zip(powers, values):
                part = jnp.dot((power * inverse).astype(BF), value, preferred_element_type=F32)
                out = part if out is None else out + part
            out = out * head_ref[group : group + 1, window]
            wide_ref[at, window] = jnp.where(inside, out, wide_ref[at, window])
            mixed_ref[at, window] = jnp.where(inside, out.astype(BF), mixed_ref[at, window])
            lane = lax.broadcasted_iota(jnp.int32, (1, 128), 1)
            total_ref[at, :] = jnp.where(
                lane == head, largest + jnp.log2(total), total_ref[at, :]
            )

    mixed = jax.ShapeDtypeStruct((rows, width), BF)
    wide = jax.ShapeDtypeStruct((rows, width), F32)
    totals = jax.ShapeDtypeStruct((rows, 128), F32)
    operands = (qkv, other, other, head_on, block_mask)
    in_specs = [pl.BlockSpec(array.shape, lambda h: (0, 0)) for array in operands]
    in_specs[1] = pl.BlockSpec((rows, width), lambda h: (0, 1))
    in_specs[2] = pl.BlockSpec((rows, width), lambda h: (0, 2))
    return pl.pallas_call(
        kernel,
        out_shape=[mixed, wide, totals],
        grid=(head_count,),
        in_specs=in_specs,
        out_specs=[pl.BlockSpec(array.shape, lambda h: (0, 0)) for array in (mixed, wide, totals)],
        cost_estimate=cost(
            4 * head_count * rows * 2 * rows * 256, [qkv, other, mixed], head_count * rows * 2 * rows
        ),
        name="attend",
    )(*operands)


def head_terms(key, value, query, grad, row, along, factor):
    probs = jnp.exp2(contract(key, query, 1, 1) * factor + row)
    grad_scores = (probs * (contract(value, grad, 1, 1) - along)).astype(BF)
    return probs.astype(BF), grad_scores


def head_rows(ref, window, inside):
    values = ref[:, window]
    return jnp.where(inside, values, jnp.zeros_like(values))


def attend_back(qkv, other, grad_mixed, totals, along, block_mask, head_count):
    rows = qkv.shape[0]
    width = qkv.shape[1] // 3
    head_size = width // head_count
    blocks = block_mask.shape[0]
    span = 2 * rows // blocks
    scale = 1.0 / math.sqrt(head_size)
    factor = scale / math.log(2.0)

    def kernel(
        qkv_ref, key_ref, value_ref, grad_ref, totals_ref, along_ref, mask_ref, query_out, pair_out
    ):
        head = pl.program_id(0)
        start, inside = head_window(head, head_size, width)
        window = pl.ds(start, 256)
        key_window = pl.ds(start + width, 256)
        value_window = pl.ds(start + 2 * width, 256)
        query = head_rows(qkv_ref, window, inside)
        grad = head_rows(grad_ref, window, inside)
        total = totals_ref[pl.ds(head, 1), :]
        along = along_ref[pl.ds(head, 1), :]
        query_grad = None
        for block in range(blocks):
            own = block < blocks // 2
            at = pl.ds((block if own else block - blocks // 2) * span, span)
            key = qkv_ref[at, key_window] if own else key_ref[at, window]
            value = qkv_ref[at, value_window] if own else value_ref[at, window]
            row = mask_ref[block : block + 1, :] - total
            probs, grad_scores = head_terms(key, value, query, grad, row, along, factor)
            if own:
                key_part = jnp.dot(grad_scores, query, preferred_element_type=F32)
                value_part = jnp.dot(probs, grad, preferred_element_type=F32)
                pair_out[at, window] = jnp.where(inside, key_part, pair_out[at, window])
                pair_out[at, key_window] = jnp.where(inside, value_part, pair_out[at, key_window])
            part = contract(grad_scores, key, 0, 0)
            query_grad = part if query_grad is None else query_grad + part
        query_out[:, window] = jnp.where(
            inside, (query_grad * scale).astype(BF), query_out[:, window]
        )

    outs = [
        jax.ShapeDtypeStruct((rows, width), BF),
        jax.ShapeDtypeStruct((rows, 2 * width), F32),
    ]
    operands = (qkv, other, other, grad_mixed, totals, along, block_mask)
    in_specs = [pl.BlockSpec(array.shape, lambda h: (0, 0)) for array in operands]
    in_specs[1] = pl.BlockSpec((rows, width), lambda h: (0, 1))
    in_specs[2] = pl.BlockSpec((rows, width), lambda h: (0, 2))
    return pl.pallas_call(
        kernel,
        out_shape=outs,
        grid=(head_count,),
        in_specs=in_specs,
        out_specs=[pl.BlockSpec(array.shape, lambda h: (0, 0)) for array in outs],
        cost_estimate=cost(
            8 * head_count * rows * 2 * rows * 256, [qkv, qkv, *outs], head_count * rows * 2 * rows
        ),
        name="attend_back",
    )(*operands)


def attend_back_other(
    qkv, other, other_grad, other_totals, other_along, block_mask, query_grad, pair, head_count
):
    rows = qkv.shape[0]
    width = qkv.shape[1] // 3
    head_size = width // head_count
    blocks = block_mask.shape[0]
    span = rows // blocks
    scale = 1.0 / math.sqrt(head_size)
    factor = scale / math.log(2.0)

    def kernel(
        key_ref, value_ref, other_ref, grad_ref, totals_ref, along_ref, mask_ref, query_ref, pair_ref,
        out_ref,
    ):
        head = pl.program_id(0)

        @pl.when(head == 0)
        def _():
            out_ref[:, :width] = query_ref[...]

        start, inside = head_window(head, head_size, width)
        window = pl.ds(start, 256)
        key_window = pl.ds(start + width, 256)
        value_window = pl.ds(start + 2 * width, 256)
        query = head_rows(other_ref, window, inside)
        grad = head_rows(grad_ref, window, inside)
        total = totals_ref[pl.ds(head, 1), :]
        along = along_ref[pl.ds(head, 1), :]
        for block in range(blocks):
            at = pl.ds(block * span, span)
            row = mask_ref[block : block + 1, :] - total
            probs, grad_scores = head_terms(
                key_ref[at, window], value_ref[at, window], query, grad, row, along, factor
            )
            key_part = pair_ref[at, window] + jnp.dot(
                grad_scores, query, preferred_element_type=F32
            )
            value_part = pair_ref[at, key_window] + jnp.dot(
                probs, grad, preferred_element_type=F32
            )
            out_ref[at, key_window] = jnp.where(
                inside, (key_part * scale).astype(BF), out_ref[at, key_window]
            )
            out_ref[at, value_window] = jnp.where(
                inside, value_part.astype(BF), out_ref[at, value_window]
            )

    out = jax.ShapeDtypeStruct(qkv.shape, BF)
    operands = (
        qkv, qkv, other, other_grad, other_totals, other_along, block_mask, query_grad, pair
    )
    in_specs = [pl.BlockSpec(array.shape, lambda h: (0, 0)) for array in operands]
    in_specs[0] = pl.BlockSpec((rows, width), lambda h: (0, 1))
    in_specs[1] = pl.BlockSpec((rows, width), lambda h: (0, 2))
    in_specs[2] = pl.BlockSpec((rows, width), lambda h: (0, 0))
    return pl.pallas_call(
        kernel,
        out_shape=out,
        grid=(head_count,),
        in_specs=in_specs,
        out_specs=pl.BlockSpec(out.shape, lambda h: (0, 0)),
        cost_estimate=cost(
            8 * head_count * rows * rows * 256, [qkv, pair, out], head_count * rows * rows
        ),
        name="attend_back_other",
    )(*operands)


def cond_columns(steps, first, count, model_width):
    half_width = model_width // 2
    index = first + jnp.arange(count, dtype=jnp.int32)
    is_sine = index >= half_width
    place = jnp.where(is_sine, index - half_width, index).astype(F32)
    frequency = jnp.exp(-math.log(10000.0) * place / half_width)
    angles = steps.astype(F32)[:, None] * frequency[None, :]
    values = jnp.where(is_sine[None, :], jnp.sin(angles), jnp.cos(angles))
    return jax.nn.silu(values).astype(BF)


def normalize(values):
    centered = values - jnp.mean(values, axis=-1, keepdims=True)
    spread = jnp.mean(centered * centered, axis=-1, keepdims=True)
    inverse = lax.rsqrt(spread + 1e-06)
    return centered * inverse, inverse


def normalize_back(grad_normed, normed, inverse):
    along = jnp.mean(grad_normed * normed, axis=-1, keepdims=True)
    level = jnp.mean(grad_normed, axis=-1, keepdims=True)
    return inverse * (grad_normed - level - normed * along)


def body(
    tokens,
    qkv_weight,
    out_weight,
    up_weight,
    down_weight,
    mod_weight,
    qv_bias,
    out_bias,
    up_bias,
    down_bias,
    mod_bias,
    row_items,
    timesteps,
    head_mask,
    channel_mask,
    token_keep,
    cotangent,
):
    layer_count = qkv_weight.shape[0]
    width = out_weight.shape[2]
    hidden_width = up_weight.shape[2]
    head_count = head_mask.shape[3]
    head_size = width // head_count
    item_count = timesteps.shape[1]
    local_rows = tokens.shape[0]
    row_len = 2 * local_rows
    group_rows = row_len // item_count
    group_count = local_rows // group_rows
    scale_factor = 1.0 / math.sqrt(head_size)
    seq_count = lax.axis_size("seq")
    seq_bits = seq_count.bit_length() - 1
    device_count = 2 * seq_count
    half_index = lax.axis_index("fsdp")
    seq_index = lax.axis_index("seq")
    flat_index = half_index * seq_count + seq_index
    shard_rows = mod_weight.shape[1]
    items_here = row_items[0]
    far_stages = [("seq", bit) for bit in range(2, seq_bits)]
    core_stage = ("seq", 0)

    padded_rows = -(-shard_rows // 8) * 8
    row_cut = (padded_rows + 8) // 16 * 8
    x_stage, y_stage = ("fsdp", 0), ("seq", 1)
    routes = (core_stage, (y_stage, x_stage), (x_stage, y_stage), far_stages)
    far_count = 1 << len(far_stages)

    def flat_mask(stage):
        return seq_count if stage[0] == "fsdp" else 1 << stage[1]

    chunk_masks, chunk_places = [], []
    for core_mask in (0, 1):
        for two in range(2):
            for part, route in enumerate(routes[1:3]):
                part_rows = padded_rows - row_cut if part else row_cut
                first_mask = flat_mask(route[0]) if two else 0
                for mask in relative_masks([route[1], *far_stages], flat_mask):
                    chunk_masks += [core_mask ^ first_mask ^ mask] * part_rows
                    chunk_places += list(range(row_cut * part, row_cut * part + part_rows))
    chunk_masks = jnp.array(chunk_masks, jnp.int32)
    chunk_places = jnp.array(chunk_places, jnp.int32)
    source = jnp.where(
        chunk_places < shard_rows, (flat_index ^ chunk_masks) * shard_rows + chunk_places, -1
    )
    order = (source[:, None] == jnp.arange(width, dtype=jnp.int32)[None, :]).astype(BF)

    def ordered(left):
        return contract(left, order, 1, 1).astype(BF)

    feed = Feed()
    place_table = jnp.stack(
        [half_index, (seq_index >> 1) & 1, seq_index & 1]
        + [
            (seq_index >> 2) ^ (mask >> 2)
            for mask in relative_masks(far_stages, lambda stage: 1 << stage[1])
        ]
    ).astype(jnp.int32)

    def scatter_ordered(lefts, rights, waits, result):
        cuts = (far_count * 2 * row_cut, far_count * 2 * (padded_rows - row_cut))
        grads = ColumnGrads(lefts, rights, width)
        feed.start(reduce_flight(grads, routes, cuts, shard_rows, waits, result))

    def scatter_chunks(turned, right, waits, result):
        rows = turned.shape[0] // device_count
        grads = RowGrads(*take_chunks(turned, place_table, rows), right)
        cuts = (far_count * rows, far_count * rows)
        feed.start(reduce_flight(grads, routes, cuts, rows, waits, result))

    gathered = []

    def unit_ticks(unit):
        early = ((0, 1, 2, 4, 7, 8), (0, 2, 4, 9, 11, 12), (5, 9, 10, 13, 14, 15))
        late = ((9, 10, 13, 14, 16, 17), (10, 13, 14, 16, 20, 21), (14, 16, 19, 20, 24, 25))
        if unit < 3:
            return early[unit]
        return tuple(tick + 10 * (unit // 3 - 1) for tick in late[unit % 3])

    for layer in range(layer_count):
        for index, (shard, rows, cut) in enumerate(
            (
                ((qkv_weight[layer],), padded_rows, row_cut),
                ((up_weight[layer], out_weight[layer]), padded_rows, row_cut),
                ((down_weight[layer],), down_weight.shape[1], down_weight.shape[1] // 2),
            )
        ):
            result = []
            gathered.append(result)
            start, *due = unit_ticks(3 * layer + index)
            waits = [after - before for before, after in zip([start] + due, due)]
            feed.at(start, gather_flight(list(shard), rows, cut, routes, waits, result))

    def qkv_tiles(layer):
        return Tiles(gathered[3 * layer], width, 0, 3)

    def up_tiles(layer):
        tile = wide_tile(hidden_width) // 2
        return Tiles(gathered[3 * layer + 1], tile, 0, hidden_width // tile)

    def out_tiles(layer):
        return Tiles(gathered[3 * layer + 1], width, hidden_width // width, 1)

    biases = (qv_bias, out_bias, up_bias, down_bias, mod_bias)
    steps_high = (timesteps // 32).astype(BF)
    steps_low = (timesteps % 32).astype(BF)
    step_rows = jnp.concatenate([steps_high, steps_low], axis=0)
    if layer_count > 2:
        step_rows = jnp.pad(step_rows, ((0, layer_count - 2), (0, 0)))
    small = jnp.concatenate([*biases, step_rows], axis=1)
    small = feed.tick(small)
    small_stages = [("seq", bit) for bit in reversed(range(seq_bits))] + [x_stage]
    for index, stage in enumerate(small_stages):
        small = jnp.concatenate([small, swap_bit(small, stage)], axis=0)
        if index == 1:
            small = feed.tick(small)
    small_masks = jnp.array(relative_masks(list(reversed(small_stages)), flat_mask), jnp.int32)
    put_back = (flat_index ^ small_masks)[None, :] == jnp.arange(device_count)[:, None]
    small_columns = small.shape[1]
    every_small = jnp.dot(
        put_back.astype(BF),
        small.reshape(device_count, layer_count * small_columns),
        preferred_element_type=F32,
    ).reshape(device_count, layer_count, small_columns)
    bias_columns = small_columns - item_count
    every_small, tokens, head_mask, channel_mask, token_keep = feed.tick(
        (every_small, tokens, head_mask, channel_mask, token_keep)
    )
    step_parts = every_small[:seq_count, :2, bias_columns:].reshape(seq_count, 2 * item_count)

    def unpack_biases(every):
        offset = 0
        full = []
        for bias in biases:
            columns = bias.shape[1]
            full.append(
                [every[:, layer, offset : offset + columns].reshape(-1) for layer in range(layer_count)]
            )
            offset += columns
        return full

    every_step = step_parts[:, :item_count] * 32.0 + step_parts[:, item_count:]

    cond_every = cond_columns(every_step.reshape(-1), flat_index * shard_rows, shard_rows, width)
    seq_masks = jnp.array(
        relative_masks([("seq", bit) for bit in range(seq_bits)], lambda stage: 1 << stage[1]),
        jnp.int32,
    )
    pick_row = (seq_index ^ seq_masks)[:, None] == jnp.arange(seq_count)[None, :]
    cond_relative = (
        jnp.sum(
            jnp.where(
                pick_row[:, :, None, None],
                cond_every.astype(F32).reshape(1, seq_count, item_count, shard_rows),
                0.0,
            ),
            axis=1,
        )
        .astype(BF)
        .reshape(seq_count * item_count, shard_rows)
    )

    mod_stages = [("seq", bit) for bit in range(seq_bits)] + [("fsdp", 0)]

    def modulation_part(layer):
        return jnp.dot(cond_relative, mod_weight[layer], preferred_element_type=F32)

    full_biases = unpack_biases(every_small)
    block = jnp.concatenate([modulation_part(layer) for layer in range(layer_count)], axis=1)
    block = feed.tick(block)
    for index, stage in enumerate(mod_stages[:-1]):
        half = block.shape[0] // 2
        block = block[:half] + swap_bit(block[half:], stage)
        if index == 1:
            block = feed.tick(block)
    block, full_biases = feed.tick((block + swap_bit(block, mod_stages[-1]), full_biases))
    mod_width = block.shape[1] // layer_count
    modulations = [
        block[:, layer * mod_width : (layer + 1) * mod_width] + full_biases[4][layer][None]
        for layer in range(layer_count)
    ]

    group_item = (
        (half_index * local_rows + jnp.arange(group_count, dtype=jnp.int32) * group_rows)
        * items_here
        // row_len
    )
    other_item = (
        ((1 - half_index) * local_rows + jnp.arange(group_count, dtype=jnp.int32) * group_rows)
        * items_here
        // row_len
    )
    group_is = group_item[:, None] == jnp.arange(item_count, dtype=jnp.int32)[None, :]

    def of_groups(table):
        return jnp.sum(
            jnp.where(group_is[:, :, None], table.astype(F32)[None], 0.0), axis=1, keepdims=False
        )[:, None, :]

    block_item = jnp.concatenate([group_item, other_item])
    block_mask = jnp.where(group_item[:, None] == block_item[None, :], 0.0, -1e30).astype(F32)
    query_mask = jnp.repeat(block_mask, group_rows, axis=1)
    key_mask = jnp.repeat(block_mask.T, group_rows, axis=1)
    cross_mask = jnp.repeat(block_mask[:, group_count:], group_rows, axis=1)

    head_lanes = (
        jnp.arange(width, dtype=jnp.int32)[None, :] // head_size
        == jnp.arange(head_count, dtype=jnp.int32)[:, None]
    ).astype(F32)

    def grouped(values):
        return values.reshape(group_count, group_rows, values.shape[-1])

    def ungrouped(values):
        return values.reshape(local_rows, values.shape[-1])

    current = grouped(tokens.astype(F32))
    saved_layers = []
    full_downs = []
    for layer in range(layer_count):
        pair_bias, out_b, up_b, down_b = (full_biases[index][layer] for index in range(4))
        modulation = modulations[layer]
        shift_one, scale_one, gate_one, shift_two, scale_two, gate_two = jnp.split(
            of_groups(modulation), 6, axis=2
        )
        head_on = jnp.repeat(of_groups(head_mask[0, layer]), head_size, axis=2)[:, 0]
        channel_on = of_groups(channel_mask[0, layer])[:, 0]
        keep_tok = grouped(token_keep[:, layer].astype(F32)[:, None])
        normed_one, inverse_one = normalize(current)
        low_one = ungrouped((normed_one * (1.0 + scale_one) + shift_one).astype(BF))
        other_one = swap_bit(low_one, x_stage)
        bias_three = jnp.concatenate(
            [pair_bias[:width], jnp.zeros((width,), F32), pair_bias[width:]]
        )
        low_one = feed.tick(low_one)
        low_one = feed.tick(ordered(low_one))
        low_one = feed.tick(low_one)
        low_one = feed.until(gathered[3 * layer], low_one)
        qkv_low = project(low_one, qkv_tiles(layer), bias_three, BF, "project_qkv")
        qkv_low, other_one = lax.optimization_barrier((qkv_low, other_one))
        other_low = project(
            ordered(other_one), qkv_tiles(layer), bias_three, BF, "project_other"
        )
        other_low = feed.tick(other_low)
        mixed_low, mixed_wide, totals = attend(qkv_low, other_low, head_on, query_mask, head_count)
        totals = totals[:, :head_count].T
        other_totals = swap_bit(totals, x_stage)
        mixed_low = feed.tick(mixed_low)
        mixed_low = feed.tick(ordered(mixed_low))
        mixed_low = feed.tick(mixed_low)
        mixed_low = feed.until(gathered[3 * layer + 1], mixed_low)
        branch_one = grouped(project(mixed_low, out_tiles(layer), out_b, F32, "project_out"))
        after_attn = current + gate_one * branch_one
        normed_two, inverse_two = normalize(after_attn)
        low_two = ungrouped((normed_two * (1.0 + scale_two) + shift_two).astype(BF))
        low_two = feed.tick(ordered(low_two))
        hidden_pre, hidden_turned = project_up(low_two, up_tiles(layer), up_b, channel_on)
        hidden_turned = feed.tick(hidden_turned)
        hidden_turned = feed.tick(hidden_turned)
        hidden_turned = feed.until(gathered[3 * layer + 2], hidden_turned)
        full_down = place_chunks(*gathered[3 * layer + 2], place_table, (hidden_width, width))
        full_downs.append(full_down)
        branch_two = grouped(contract(hidden_turned, full_down, 0, 0) + down_b)
        saved_layers.append(
            dict(
                inputs=current,
                scale_one=scale_one,
                gate_one=gate_one,
                scale_two=scale_two,
                gate_two=gate_two,
                head_on=head_on,
                channel_on=channel_on,
                keep_tok=keep_tok,
                low_one=low_one,
                qkv_low=qkv_low,
                other_low=other_low,
                totals=totals,
                other_totals=other_totals,
                mixed_low=mixed_low,
                mixed_wide=mixed_wide,
                branch_one=branch_one,
                after_attn=after_attn,
                low_two=low_two,
                hidden_pre=hidden_pre,
                hidden_turned=hidden_turned,
                branch_two=branch_two,
            )
        )
        current = after_attn + keep_tok * gate_two * branch_two
    output = ungrouped(current).astype(BF)
    output = feed.finish(output)

    cond_rows = jnp.concatenate(
        [
            cond_every.reshape(seq_count, item_count, shard_rows),
            jnp.zeros((seq_count, 8 - item_count, shard_rows), BF),
        ],
        axis=1,
    ).reshape(seq_count * 8, shard_rows)
    cond_twice = jnp.concatenate([cond_rows, cond_rows], axis=0)

    def packet_flight(packet, wait, result):
        every = yield wait, lax.all_gather(packet, AXES, axis=0, tiled=True)
        grad_mod_weight = contract(cond_twice, every, 0, 0)
        sums = jnp.sum(every.astype(F32).reshape(device_count, *packet.shape), axis=0)

        def shard_of(row, start, columns):
            return lax.dynamic_slice_in_dim(row, start + flat_index * columns, columns, 0)

        grad_mod_bias = shard_of(jnp.sum(sums[:item_count], axis=0), 0, mod_bias.shape[1])
        bias_sum = sums[item_count:].reshape(-1)
        parts = []
        start = 0
        for bias in (qv_bias, out_bias, up_bias, down_bias):
            parts.append(shard_of(bias_sum, start, bias.shape[1]))
            start += device_count * bias.shape[1]
        grads = yield 1, (grad_mod_weight, *parts, grad_mod_bias)
        result.append(grads)

    grad_current = grouped(cotangent)
    layer_totals = [None] * layer_count
    for layer in reversed(range(layer_count)):
        saved = saved_layers[layer]
        kept_grad = grad_current * saved["keep_tok"]
        down_grad = ungrouped((kept_grad * saved["gate_two"]).astype(BF))
        grad_gate_two = jnp.sum(kept_grad * saved["branch_two"], axis=1)
        grad_down_bias = jnp.sum(down_grad.astype(F32), axis=0)
        down_rows, up_rows, out_rows, qkv_rows = [], [], [], []
        last = layer == 0
        scatter_chunks(saved["hidden_turned"], down_grad, (1, 1, 1, 2, 1, 1), down_rows)
        up_grad, grad_up_bias = hidden_back(
            down_grad, full_downs[layer], saved["hidden_pre"], saved["channel_on"], wide_tile(hidden_width) // 2
        )
        grad_up_bias = grad_up_bias[0]
        up_grad = feed.tick(feed.tick(up_grad))
        grad_after, out_grad, sums_two = project_norm_back(
            up_grad,
            up_tiles(layer),
            order,
            ungrouped(saved["after_attn"]),
            ungrouped(grad_current),
            saved["scale_two"][:, 0],
            ungrouped(saved["branch_one"]),
            saved["gate_one"][:, 0],
            "back_up",
        )
        grad_shift_two, grad_scale_two, grad_gate_one = (
            sums_two[part * group_count : (part + 1) * group_count] for part in range(3)
        )
        grad_out_bias = sums_two[3 * group_count]
        out_grad = feed.tick(feed.tick(out_grad))
        lefts, rights = (saved["low_two"], saved["mixed_low"]), (up_grad, out_grad)
        up_waits = (2, 0, 2, 2, 2, 1) if last else (2, 0, 2, 2, 2, 3)
        scatter_ordered(lefts, rights, up_waits, up_rows)
        grad_mixed = ungrouped(
            (
                grouped(project_back(out_grad, out_tiles(layer), order, 1, "back_out"))
                * saved["head_on"][:, None]
            ).astype(BF)
        )
        grad_mixed = feed.tick(grad_mixed)
        other_mixed = swap_bit(grad_mixed, x_stage)
        along = lax.dot_general(
            head_lanes,
            saved["mixed_wide"] * grad_mixed.astype(F32),
            (((1,), (1,)), ((), ())),
            precision=lax.Precision.HIGHEST,
            preferred_element_type=F32,
        )
        other_along = swap_bit(along, x_stage)
        grad_query, grad_pair = attend_back(
            saved["qkv_low"],
            saved["other_low"],
            grad_mixed,
            saved["totals"],
            along,
            key_mask,
            head_count,
        )
        grad_pair = feed.tick(grad_pair)
        grad_qkv = attend_back_other(
            saved["qkv_low"],
            saved["other_low"],
            other_mixed,
            saved["other_totals"],
            other_along,
            cross_mask,
            grad_query,
            grad_pair,
            head_count,
        )
        grad_qkv = feed.tick(grad_qkv)
        grad_qkv_bias = jnp.sum(grad_qkv.astype(F32), axis=0)
        qkv_waits = (1, 1, 1, 2) if last else (1, 0, 4, 2, 1, 2)
        scatter_ordered((saved["low_one"],), (grad_qkv,), qkv_waits, qkv_rows)
        if last:
            grad_qkv = feed.tick(feed.tick(grad_qkv))
        grad_inputs, sums_one = project_norm_back(
            grad_qkv,
            qkv_tiles(layer),
            order,
            ungrouped(saved["inputs"]),
            grad_after,
            saved["scale_one"][:, 0],
            None,
            None,
            "back_qkv",
        )
        grad_inputs = grouped(feed.tick(grad_inputs))
        grad_shift_one, grad_scale_one = (
            sums_one[part * group_count : (part + 1) * group_count] for part in range(2)
        )
        grad_groups = jnp.concatenate(
            [
                grad_shift_one,
                grad_scale_one,
                grad_gate_one,
                grad_shift_two,
                grad_scale_two,
                grad_gate_two,
            ],
            axis=1,
        )
        grad_slots = jnp.sum(jnp.where(group_is[:, :, None], grad_groups[:, None, :], 0.0), axis=0)
        mod_width = grad_slots.shape[1]
        bias_row = jnp.concatenate(
            [
                grad_qkv_bias[:width],
                grad_qkv_bias[2 * width :],
                grad_out_bias,
                grad_up_bias,
                grad_down_bias,
            ]
        )
        spare = jnp.zeros(((8 - item_count) * mod_width - bias_row.shape[0],), F32)
        packet = jnp.concatenate(
            [grad_slots, jnp.concatenate([bias_row, spare]).reshape(8 - item_count, mod_width)],
            axis=0,
        ).astype(BF)
        if last:
            grad_inputs, packet = feed.tick((grad_inputs, packet))
        shared_grads = []
        feed.start(packet_flight(packet, 3 if last else 7, shared_grads))
        grad_current = grad_inputs if last else feed.tick(grad_inputs)
        layer_totals[layer] = (
            qkv_rows,
            up_rows,
            up_rows,
            down_rows,
            shared_grads,
        )
    grad_current = feed.finish(grad_current)
    layer_totals = [
        (
            qkv[0],
            up[0][:, hidden_width:],
            up[0][:, :hidden_width],
            down[0],
            *shared[0],
        )
        for qkv, up, _, down, shared in layer_totals
    ]
    stacked = tuple(
        jnp.stack([layer_totals[layer][index] for layer in range(layer_count)])
        for index in range(10)
    )
    return (output, ungrouped(grad_current), *stacked)


def solution(mesh):
    rows = P(AXES, None)
    matrix = P(None, AXES, None)
    vector = P(None, AXES)
    return jax.shard_map(
        body,
        mesh=mesh,
        in_specs=(
            rows,
            matrix,
            matrix,
            matrix,
            matrix,
            matrix,
            vector,
            vector,
            vector,
            vector,
            vector,
            P("seq"),
            P("seq", None),
            P("seq", None, None, None),
            P("seq", None, None, None),
            rows,
            rows,
        ),
        out_specs=(
            rows,
            rows,
            matrix,
            matrix,
            matrix,
            matrix,
            matrix,
            vector,
            vector,
            vector,
            vector,
            vector,
        ),
        check_vma=False,
    )
```

```python
import math

import jax
import jax.numpy as jnp
from jax import lax
from jax.experimental import pallas as pl
from jax.experimental.pallas import tpu as pltpu
from jax.sharding import PartitionSpec as P

BF = jnp.bfloat16
F32 = jnp.float32
AXES = ("fsdp", "seq")


def swap_bit(block, stage):
    axis, bit = stage
    count = lax.axis_size(axis)
    return lax.ppermute(block, axis, [(low, low ^ (1 << bit)) for low in range(count)])


def stage_bit(stage):
    axis, bit = stage
    return (lax.axis_index(axis) >> bit) & 1


def contract(left, right, left_dim, right_dim):
    return lax.dot_general(
        left, right, (((left_dim,), (right_dim,)), ((), ())), preferred_element_type=F32
    )


def relative_masks(stages, mask_of):
    masks = [0]
    for stage in reversed(stages):
        masks = masks + [mask ^ mask_of(stage) for mask in masks]
    return masks


class Feed:
    def __init__(self):
        self.flights = []
        self.ticks = 0
        self.later = {}

    def start(self, flight):
        wait, parts = next(flight)
        self.flights.append((flight, self.ticks + wait - 1, parts))

    def at(self, tick, flight):
        self.later.setdefault(tick, []).append(flight)

    def tick(self, value):
        for flight in self.later.pop(self.ticks, []):
            self.start(flight)
        due = [entry for entry in self.flights if entry[1] <= self.ticks]
        flying = [entry for entry in self.flights if entry[1] > self.ticks]
        self.ticks += 1
        value, arrived = lax.optimization_barrier((value, [parts for _, _, parts in due]))
        for (flight, _, _), parts in zip(due, arrived):
            try:
                wait, sent = flight.send(parts)
                flying.append((flight, self.ticks + wait - 1, sent))
            except StopIteration:
                pass
        self.flights = flying
        return value

    def until(self, result, value):
        while not result:
            value = self.tick(value)
        return value

    def finish(self, value):
        while self.flights or self.later:
            value = self.tick(value)
        return value


def reduce_flight(grads, routes, cuts, rows, waits, result):
    core_stage, first_route, second_route, far_stages = routes
    first, second = cuts
    waits = list(waits) + [1] * 8
    arrived = yield waits[0], swap_bit(grads.away(), core_stage)
    parts = grads.stay(arrived, first, second)
    if waits[1]:
        parts = yield waits[1], parts
    kept, first_sent, second_sent = parts
    first_arrived, second_arrived = yield waits[2], (
        swap_bit(first_sent, first_route[0]),
        swap_bit(second_sent, second_route[0]),
    )

    def add(left, other, low, high):
        return left[low:high].astype(F32) + other[low:high].astype(F32)

    first_kept, second_kept = kept[:first], kept[first:]
    half_first, half_second = first // 2, second // 2
    first_sent = add(first_kept, first_arrived, half_first, first).astype(BF)
    second_sent = add(second_kept, second_arrived, half_second, second).astype(BF)
    first_kept = add(first_kept, first_arrived, 0, half_first).astype(BF)
    second_kept = add(second_kept, second_arrived, 0, half_second).astype(BF)
    first_arrived, second_arrived = yield waits[3], (
        swap_bit(first_sent, first_route[1]),
        swap_bit(second_sent, second_route[1]),
    )
    for index, stage in enumerate(far_stages):
        first, second = half_first, half_second
        half_first, half_second = first // 2, second // 2
        sent = jnp.concatenate(
            [
                add(first_kept, first_arrived, half_first, first),
                add(second_kept, second_arrived, half_second, second),
            ],
            axis=0,
        ).astype(BF)
        first_kept = add(first_kept, first_arrived, 0, half_first).astype(BF)
        second_kept = add(second_kept, second_arrived, 0, half_second).astype(BF)
        arrived = yield waits[4 + index], swap_bit(sent, stage)
        first_arrived, second_arrived = arrived[:half_first], arrived[half_first:]
    block = jnp.concatenate(
        [
            add(first_kept, first_arrived, 0, half_first),
            add(second_kept, second_arrived, 0, half_second),
        ],
        axis=0,
    )
    result.append(block[:rows])


class ColumnGrads:
    def __init__(self, lefts, rights, tile):
        self.lefts, self.rights, self.tile = lefts, rights, tile
        self.half = lefts[0].shape[1] // 2
        self.counts = [right.shape[1] // tile for right in rights]

    def call(self, index, arrived, pieces, name):
        half, tile = self.half, self.tile
        tokens = self.lefts[0].shape[0]
        pairs = len(self.lefts)
        starts = [sum(self.counts[:pair]) for pair in range(pairs)]
        columns = sum(self.counts) * tile

        def kernel(*refs):
            lefts, rights = refs[:pairs], refs[pairs : 2 * pairs]
            rest = refs[2 * pairs :]
            if arrived is not None:
                arrived_ref, rest = rest[0], rest[1:]
            out_refs, turned_ref = rest[:-1], rest[-1]
            step = pl.program_id(0)

            def work(left_ref, right_ref, start):
                @pl.when(step == start)
                def _():
                    turned_ref[...] = left_ref[...].astype(F32).T.astype(BF)

                total = jnp.dot(turned_ref[...], right_ref[...], preferred_element_type=F32)
                if arrived is not None:
                    total = total + arrived_ref[...].astype(F32)
                total = total.astype(BF)
                low = 0
                for out_ref, count in zip(out_refs, pieces):
                    out_ref[...] = total[low : low + count]
                    low += count

            for left_ref, right_ref, start, count in zip(lefts, rights, starts, self.counts):
                if pairs == 1:
                    work(left_ref, right_ref, start)
                else:
                    pl.when((step >= start) & (step < start + count))(
                        lambda l=left_ref, r=right_ref, s=start: work(l, r, s)
                    )

        def right_spec(start, count):
            return pl.BlockSpec(
                (tokens, tile), lambda j: (0, jnp.clip(j - start, 0, count - 1))
            )

        operands = [*self.lefts, *self.rights]
        in_specs = [pl.BlockSpec((tokens, half), lambda j: (0, index)) for _ in self.lefts]
        in_specs += [right_spec(*pair) for pair in zip(starts, self.counts)]
        if arrived is not None:
            operands.append(arrived)
            in_specs.append(pl.BlockSpec((half, tile), lambda j: (0, j)))
        outs = [jax.ShapeDtypeStruct((count, columns), BF) for count in pieces]
        return pl.pallas_call(
            kernel,
            out_shape=outs,
            grid=(sum(self.counts),),
            in_specs=in_specs,
            out_specs=[pl.BlockSpec((count, tile), lambda j: (0, j)) for count in pieces],
            scratch_shapes=[pltpu.VMEM((half, tokens), BF)],
            cost_estimate=cost(2 * half * tokens * columns, [*operands, *outs]),
            name=name,
        )(*operands)

    def away(self):
        return self.call(1, None, [self.half], "away_grad")[0]

    def stay(self, arrived, first, second):
        return self.call(0, arrived, [self.half - first - second, first, second], "stay_grad")


class RowGrads:
    def __init__(self, stay, away, right):
        self.stay_rows, self.away_rows, self.right = stay, away, right

    def away(self):
        return contract(self.away_rows, self.right, 1, 0).astype(BF)

    def stay(self, arrived, first, second):
        left, right = self.stay_rows, self.right
        tokens, columns = right.shape
        assert first == second

        def kernel(left_ref, right_ref, arrived_ref, kept_ref, first_ref, second_ref):
            step = pl.program_id(0)
            total = jnp.dot(left_ref[...], right_ref[...], preferred_element_type=F32)
            total = (total + arrived_ref[...].astype(F32)).astype(BF)
            pl.when(step < 2)(lambda: kept_ref.__setitem__(..., total))
            pl.when(step == 2)(lambda: first_ref.__setitem__(..., total))
            pl.when(step == 3)(lambda: second_ref.__setitem__(..., total))

        outs = [jax.ShapeDtypeStruct((count, columns), BF) for count in (2 * first, first, second)]
        return pl.pallas_call(
            kernel,
            out_shape=outs,
            grid=(4,),
            in_specs=[
                pl.BlockSpec((first, tokens), lambda j: (j, 0)),
                pl.BlockSpec(right.shape, lambda j: (0, 0)),
                pl.BlockSpec((first, columns), lambda j: (j, 0)),
            ],
            out_specs=[
                pl.BlockSpec((first, columns), lambda j: (jnp.minimum(j, 1), 0)),
                pl.BlockSpec((first, columns), lambda j: (0, 0)),
                pl.BlockSpec((first, columns), lambda j: (0, 0)),
            ],
            cost_estimate=cost(
                2 * left.shape[0] * tokens * columns, [left, right, arrived, *outs]
            ),
            name="stay_rows",
        )(left, right, arrived)


def wide_tile(columns):
    return next(tile for tile in (1536, 1152, 768, 512, 384, 256, 128) if columns % tile == 0)


def run_through(flight):
    parts = None
    try:
        while True:
            _, parts = flight.send(parts)
    except StopIteration:
        pass


def gather_flight(shard, rows, cut, routes, waits, result):
    core_stage, first_route, second_route, far_stages = routes
    waits = [1] * (len(far_stages) - 2) + list(waits)
    parts = yield 1, shard
    shard = jnp.concatenate(parts, axis=1) if len(parts) > 1 else parts[0]
    if shard.shape[0] < rows:
        shard = jnp.pad(shard, ((0, rows - shard.shape[0]), (0, 0)))
    blocks = [shard]
    for stage in reversed(far_stages):
        sent = jnp.concatenate(blocks, axis=0) if len(blocks) > 1 else blocks[0]
        arrived = yield waits.pop(0), swap_bit(sent, stage)
        blocks = blocks + [
            arrived[start : start + rows] for start in range(0, arrived.shape[0], rows)
        ]
    owned = [
        jnp.concatenate([block[:cut] for block in blocks], axis=0),
        jnp.concatenate([block[cut:] for block in blocks], axis=0),
    ]
    routes = (second_route, first_route)
    arrived = yield (
        waits.pop(0),
        [swap_bit(part, route[0]) for part, route in zip(owned, routes)],
    )
    pairs = [jnp.concatenate([part, more], axis=0) for part, more in zip(owned, arrived)]
    fars = yield waits.pop(0), [swap_bit(pair, route[1]) for pair, route in zip(pairs, routes)]
    others = yield (
        waits.pop(0),
        [[swap_bit(pair, core_stage), swap_bit(far, core_stage)] for pair, far in zip(pairs, fars)],
    )
    for pair, far, other in zip(pairs, fars, others):
        result.append((pair, far, other[0], other[1]))


def take_chunks(left, places, chunk_rows):
    far_count = places.shape[0] - 3
    columns = left.shape[1]
    part_rows = chunk_rows // 2

    def take(places_ref, in_ref, stay_ref, away_ref):
        x_here, y_here, core_here = places_ref[0], places_ref[1], places_ref[2]
        for half in range(2):
            for one in range(2):
                for two in range(2):
                    x_place = jnp.bitwise_xor(x_here, two if half else one)
                    y_place = jnp.bitwise_xor(y_here, one if half else two)
                    stay_ref[two, half, one, 0] = in_ref[x_place, 0, y_place, core_here, half]
                    away_ref[two, half, one, 0] = in_ref[x_place, 0, y_place, 1 - core_here, half]

    shape = (2, 2, 2, far_count, part_rows, columns)
    out_spec = pl.BlockSpec(
        (2, 2, 2, 1, part_rows, columns), lambda i, places: (0, 0, 0, i, 0, 0)
    )
    parts = pl.pallas_call(
        take,
        out_shape=[jax.ShapeDtypeStruct(shape, left.dtype)] * 2,
        grid_spec=pltpu.PrefetchScalarGridSpec(
            num_scalar_prefetch=1,
            grid=(far_count,),
            in_specs=[
                pl.BlockSpec(
                    (2, 1, 2, 2, 2, part_rows, columns),
                    lambda i, places: (0, places[3 + i], 0, 0, 0, 0, 0),
                )
            ],
            out_specs=[out_spec, out_spec],
        ),
        cost_estimate=pl.CostEstimate(
            flops=0, bytes_accessed=4 * left.size, transcendentals=0
        ),
        name="take_chunks",
    )(places, left.reshape(2, far_count, 2, 2, 2, part_rows, columns))
    return [part.reshape(left.shape[0] // 2, columns) for part in parts]


def place_chunks(first, second, places, out_shape):
    far_count = places.shape[0] - 3
    columns = out_shape[1]
    rows = first[0].shape[0] // (2 * far_count)
    pieces = [piece.reshape(2, far_count, rows, columns) for piece in (*first, *second)]

    def place(places_ref, *refs):
        out_ref = refs[-1]
        x_here, y_here, core_here = places_ref[0], places_ref[1], places_ref[2]
        for half in range(2):
            for core in range(2):
                for two in range(2):
                    ref = refs[4 * half + 2 * core + two]
                    for one in range(2):
                        x_place = jnp.bitwise_xor(x_here, two if half else one)
                        y_place = jnp.bitwise_xor(y_here, one if half else two)
                        core_place = jnp.bitwise_xor(core_here, core)
                        out_ref[x_place, 0, y_place, core_place, half] = ref[one, 0]

    in_spec = pl.BlockSpec((2, 1, rows, columns), lambda i, places: (0, i, 0, 0))
    view = (2, far_count, 2, 2, 2, rows, columns)
    return pl.pallas_call(
        place,
        out_shape=jax.ShapeDtypeStruct(view, BF),
        grid_spec=pltpu.PrefetchScalarGridSpec(
            num_scalar_prefetch=1,
            grid=(far_count,),
            in_specs=[in_spec] * 8,
            out_specs=pl.BlockSpec(
                (2, 1, 2, 2, 2, rows, columns), lambda i, places: (0, places[3 + i], 0, 0, 0, 0, 0)
            ),
        ),
        cost_estimate=pl.CostEstimate(
            flops=0, bytes_accessed=4 * out_shape[0] * columns, transcendentals=0
        ),
        name="place_chunks",
    )(places, *pieces).reshape(out_shape)


class Tiles:
    def __init__(self, parts, tile, start, count):
        first, second = parts
        self.pieces = [piece for pair in zip(first, second) for piece in pair]
        self.tile, self.start, self.count = tile, start, count
        self.rows = sum(piece.shape[0] for piece in self.pieces)

    def operands(self):
        return list(self.pieces)

    def specs(self):
        return [
            pl.BlockSpec((piece.shape[0], self.tile), lambda j: (0, self.start + j))
            for piece in self.pieces
        ]

    def weight(self, refs):
        return jnp.concatenate([ref[...] for ref in refs[:8]], axis=0)

    def columns(self):
        return self.count * self.tile


def cost(flops, arrays, transcendentals=0):
    return pl.CostEstimate(
        flops=int(flops),
        bytes_accessed=int(sum(array.size * array.dtype.itemsize for array in arrays)),
        transcendentals=int(transcendentals),
    )


def project(left, tiles, bias, out_dtype, name):
    rows = left.shape[0]
    operands = tiles.operands()

    def kernel(left_ref, bias_ref, *refs):
        out_ref = refs[-1]

        total = jnp.dot(left_ref[...], tiles.weight(refs), preferred_element_type=F32)
        out_ref[...] = (total + bias_ref[...]).astype(out_dtype)

    out = jax.ShapeDtypeStruct((rows, tiles.columns()), out_dtype)
    return pl.pallas_call(
        kernel,
        out_shape=out,
        grid=(tiles.count,),
        in_specs=[
            pl.BlockSpec(left.shape, lambda j: (0, 0)),
            pl.BlockSpec((1, tiles.tile), lambda j: (0, j)),
            *tiles.specs(),
        ],
        out_specs=pl.BlockSpec((rows, tiles.tile), lambda j: (0, j)),
        cost_estimate=cost(2 * rows * left.shape[1] * tiles.columns(), [left, out, *operands]),
        name=name,
    )(left, bias.reshape(1, -1), *operands)


def gelu_parts(value):
    inner = math.sqrt(2.0 / math.pi) * (value + 0.044715 * (value * value * value))
    return jnp.tanh(inner)


def project_up(left, tiles, bias, channel_on):
    rows = left.shape[0]
    groups = channel_on.shape[0]
    operands = tiles.operands()

    def kernel(left_ref, bias_ref, channel_ref, *refs):
        pre_ref, turned_ref = refs[-2:]

        pre = jnp.dot(left_ref[...], tiles.weight(refs), preferred_element_type=F32)
        pre = pre + bias_ref[...]
        pre_ref[...] = pre
        hidden = 0.5 * pre * (1.0 + gelu_parts(pre))
        span = rows // groups
        for group in range(groups):
            part = hidden[group * span : (group + 1) * span] * channel_ref[group : group + 1]
            turned_ref[:, group * span : (group + 1) * span] = part.T.astype(BF)

    pre = jax.ShapeDtypeStruct((rows, tiles.columns()), F32)
    turned = jax.ShapeDtypeStruct((tiles.columns(), rows), BF)
    return pl.pallas_call(
        kernel,
        out_shape=[pre, turned],
        grid=(tiles.count,),
        in_specs=[
            pl.BlockSpec(left.shape, lambda j: (0, 0)),
            pl.BlockSpec((1, tiles.tile), lambda j: (0, j)),
            pl.BlockSpec((groups, tiles.tile), lambda j: (0, j)),
            *tiles.specs(),
        ],
        out_specs=[
            pl.BlockSpec((rows, tiles.tile), lambda j: (0, j)),
            pl.BlockSpec((tiles.tile, rows), lambda j: (j, 0)),
        ],
        cost_estimate=cost(
            2 * rows * left.shape[1] * tiles.columns(), [left, pre, turned, *operands], pre.size
        ),
        name="project_up",
    )(left, bias.reshape(1, -1), channel_on, *operands)


def project_back(right, tiles, order, parts, name):
    rows = right.shape[0]
    operands = tiles.operands()
    width = order.shape[1]

    def kernel(right_ref, order_ref, *refs):
        out_ref, total_ref = refs[-2:]
        index = pl.program_id(0)

        @pl.when(index == 0)
        def _():
            total_ref[...] = jnp.zeros_like(total_ref)

        total_ref[...] += contract(right_ref[...], tiles.weight(refs), 1, 1)

        @pl.when(index == tiles.count - 1)
        def _():
            rest = total_ref[...]
            out = None
            for part in range(parts):
                high = rest.astype(BF)
                placed = jnp.dot(high, order_ref[...], preferred_element_type=F32)
                out = placed if out is None else out + placed
                if part < parts - 1:
                    rest = rest - high.astype(F32)
            out_ref[...] = out

    out = jax.ShapeDtypeStruct((rows, width), F32)
    return pl.pallas_call(
        kernel,
        out_shape=out,
        grid=(tiles.count,),
        in_specs=[
            pl.BlockSpec((rows, tiles.tile), lambda j: (0, j)),
            pl.BlockSpec(order.shape, lambda j: (0, 0)),
            *tiles.specs(),
        ],
        out_specs=pl.BlockSpec(out.shape, lambda j: (0, 0)),
        scratch_shapes=[pltpu.VMEM((rows, tiles.rows), F32)],
        cost_estimate=cost(
            2 * rows * tiles.rows * (tiles.columns() + parts * width), [right, out, order, *operands]
        ),
        name=name,
    )(right, order, *operands)


def project_norm_back(right, tiles, order, inputs, residual, scale, branch, gate, name):
    rows = right.shape[0]
    operands = tiles.operands()
    width = order.shape[1]
    groups = scale.shape[0]
    span = rows // groups
    gated = branch is not None
    chunk = min(span, 128)

    def kernel(right_ref, order_ref, inputs_ref, residual_ref, scale_ref, *refs):
        if gated:
            branch_ref, gate_ref, refs = refs[0], refs[1], refs[2:]
        pieces, refs = refs[:8], refs[8:]
        if gated:
            after_ref, product_ref, sums_ref, total_ref = refs
        else:
            after_ref, sums_ref, total_ref = refs
        index = pl.program_id(0)

        @pl.when(index == 0)
        def _():
            total_ref[...] = jnp.zeros_like(total_ref)

        total_ref[...] += contract(right_ref[...], tiles.weight(pieces), 1, 1)

        @pl.when(index == tiles.count - 1)
        def _():
            sums_ref[...] = jnp.zeros_like(sums_ref)

            def add_sum(row, values):
                along = jnp.sum(values, axis=0, keepdims=True)
                sums_ref[row : row + 1, :] = sums_ref[row : row + 1, :] + along

            for low in range(0, rows, chunk):
                at = pl.ds(low, chunk)
                group = low // span
                rest = total_ref[at, :]
                high = rest.astype(BF)
                grad = jnp.dot(high, order_ref[...], preferred_element_type=F32)
                lower = (rest - high.astype(F32)).astype(BF)
                grad = grad + jnp.dot(lower, order_ref[...], preferred_element_type=F32)
                normed, inverse = normalize(inputs_ref[at, :])
                add_sum(group, grad)
                add_sum(groups + group, grad * normed)
                after = residual_ref[at, :] + normalize_back(
                    grad * (1.0 + scale_ref[group : group + 1, :]), normed, inverse
                )
                after_ref[at, :] = after
                if gated:
                    product = (after * gate_ref[group : group + 1, :]).astype(BF)
                    product_ref[at, :] = product
                    add_sum(2 * groups + group, after * branch_ref[at, :])
                    add_sum(3 * groups, product.astype(F32))

    whole = lambda shape: pl.BlockSpec(shape, lambda j: (0, 0))
    wide = jax.ShapeDtypeStruct((rows, width), F32)
    outs = [wide] + ([jax.ShapeDtypeStruct((rows, width), BF)] if gated else [])
    outs.append(jax.ShapeDtypeStruct((3 * groups + 2, width), F32))
    extra = [branch, gate] if gated else []
    others = [order, inputs, residual, scale, *extra]
    return pl.pallas_call(
        kernel,
        out_shape=outs,
        grid=(tiles.count,),
        in_specs=[
            pl.BlockSpec((rows, tiles.tile), lambda j: (0, j)),
            *[whole(array.shape) for array in others],
            *tiles.specs(),
        ],
        out_specs=[whole(out.shape) for out in outs],
        scratch_shapes=[pltpu.VMEM((rows, tiles.rows), F32)],
        cost_estimate=cost(
            2 * rows * tiles.rows * (tiles.columns() + 2 * width), [right, *others, *outs, *operands]
        ),
        name=name,
    )(right, *others, *operands)


def hidden_back(down_grad, full_down, pre, channel_on, tile):
    rows, width = down_grad.shape
    groups = channel_on.shape[0]
    columns = pre.shape[1]

    def kernel(grad_ref, weight_ref, pre_ref, channel_ref, out_ref, sum_ref):
        value = pre_ref[...]
        tanh = gelu_parts(value)
        slope = 0.5 * (1.0 + tanh) + 0.5 * value * (1.0 - tanh * tanh) * math.sqrt(
            2.0 / math.pi
        ) * (1.0 + 3.0 * 0.044715 * value * value)
        grad = contract(grad_ref[...], weight_ref[...], 1, 1) * slope
        span = rows // groups
        total = None
        for group in range(groups):
            part = (
                grad[group * span : (group + 1) * span] * channel_ref[group : group + 1]
            ).astype(BF)
            out_ref[group * span : (group + 1) * span] = part
            along = jnp.sum(part.astype(F32), axis=0, keepdims=True)
            total = along if total is None else total + along
        sum_ref[...] = total

    out = jax.ShapeDtypeStruct((rows, columns), BF)
    sums = jax.ShapeDtypeStruct((1, columns), F32)
    return pl.pallas_call(
        kernel,
        out_shape=[out, sums],
        grid=(columns // tile,),
        in_specs=[
            pl.BlockSpec(down_grad.shape, lambda j: (0, 0)),
            pl.BlockSpec((tile, width), lambda j: (j, 0)),
            pl.BlockSpec((rows, tile), lambda j: (0, j)),
            pl.BlockSpec((groups, tile), lambda j: (0, j)),
        ],
        out_specs=[
            pl.BlockSpec((rows, tile), lambda j: (0, j)),
            pl.BlockSpec((1, tile), lambda j: (0, j)),
        ],
        cost_estimate=cost(
            2 * rows * width * columns, [down_grad, full_down, pre, out], rows * columns
        ),
        name="hidden_back",
    )(down_grad, full_down, pre, channel_on)


def head_window(head, head_size, width):
    start = jnp.minimum(head * head_size // 128, width // 128 - 2) * 128
    lane = lax.broadcasted_iota(jnp.int32, (1, 256), 1) + start
    inside = (lane >= head * head_size) & (lane < (head + 1) * head_size)
    return pl.multiple_of(start, 128), inside


def attend(qkv, other, head_on, block_mask, head_count):
    rows = qkv.shape[0]
    width = qkv.shape[1] // 3
    head_size = width // head_count
    groups = head_on.shape[0]
    span = rows // groups
    factor = 1.0 / math.sqrt(head_size) / math.log(2.0)

    def kernel(
        qkv_ref, key_ref, value_ref, head_ref, mask_ref, mixed_ref, wide_ref, total_ref
    ):
        head = pl.program_id(0)
        start, inside = head_window(head, head_size, width)
        window = pl.ds(start, 256)
        key_window = pl.ds(start + width, 256)
        value_window = pl.ds(start + 2 * width, 256)
        keys = (qkv_ref[:, key_window], key_ref[:, window])
        values = (qkv_ref[:, value_window], value_ref[:, window])
        for group in range(groups):
            at = pl.ds(group * span, span)
            query = qkv_ref[at, window]
            query = jnp.where(inside, query, jnp.zeros_like(query))
            scores = [
                contract(query, key, 1, 1) * factor
                + mask_ref[group : group + 1, side * rows : (side + 1) * rows]
                for side, key in enumerate(keys)
            ]
            largest = jnp.maximum(
                jnp.max(scores[0], axis=1, keepdims=True), jnp.max(scores[1], axis=1, keepdims=True)
            )
            powers = [jnp.exp2(score - largest) for score in scores]
            total = jnp.sum(powers[0], axis=1, keepdims=True) + jnp.sum(
                powers[1], axis=1, keepdims=True
            )
            inverse = 1.0 / total
            out = None
            for power, value in zip(powers, values):
                part = jnp.dot((power * inverse).astype(BF), value, preferred_element_type=F32)
                out = part if out is None else out + part
            out = out * head_ref[group : group + 1, window]
            wide_ref[at, window] = jnp.where(inside, out, wide_ref[at, window])
            mixed_ref[at, window] = jnp.where(inside, out.astype(BF), mixed_ref[at, window])
            lane = lax.broadcasted_iota(jnp.int32, (1, 128), 1)
            total_ref[at, :] = jnp.where(
                lane == head, largest + jnp.log2(total), total_ref[at, :]
            )

    mixed = jax.ShapeDtypeStruct((rows, width), BF)
    wide = jax.ShapeDtypeStruct((rows, width), F32)
    totals = jax.ShapeDtypeStruct((rows, 128), F32)
    operands = (qkv, other, other, head_on, block_mask)
    in_specs = [pl.BlockSpec(array.shape, lambda h: (0, 0)) for array in operands]
    in_specs[1] = pl.BlockSpec((rows, width), lambda h: (0, 1))
    in_specs[2] = pl.BlockSpec((rows, width), lambda h: (0, 2))
    return pl.pallas_call(
        kernel,
        out_shape=[mixed, wide, totals],
        grid=(head_count,),
        in_specs=in_specs,
        out_specs=[pl.BlockSpec(array.shape, lambda h: (0, 0)) for array in (mixed, wide, totals)],
        cost_estimate=cost(
            4 * head_count * rows * 2 * rows * 256, [qkv, other, mixed], head_count * rows * 2 * rows
        ),
        name="attend",
    )(*operands)


def head_terms(key, value, query, grad, row, along, factor):
    probs = jnp.exp2(contract(key, query, 1, 1) * factor + row)
    grad_scores = (probs * (contract(value, grad, 1, 1) - along)).astype(BF)
    return probs.astype(BF), grad_scores


def head_rows(ref, window, inside):
    values = ref[:, window]
    return jnp.where(inside, values, jnp.zeros_like(values))


def attend_back(qkv, other, grad_mixed, totals, along, block_mask, head_count):
    rows = qkv.shape[0]
    width = qkv.shape[1] // 3
    head_size = width // head_count
    blocks = block_mask.shape[0]
    span = 2 * rows // blocks
    scale = 1.0 / math.sqrt(head_size)
    factor = scale / math.log(2.0)

    def kernel(
        qkv_ref, key_ref, value_ref, grad_ref, totals_ref, along_ref, mask_ref, query_out, pair_out
    ):
        head = pl.program_id(0)
        start, inside = head_window(head, head_size, width)
        window = pl.ds(start, 256)
        key_window = pl.ds(start + width, 256)
        value_window = pl.ds(start + 2 * width, 256)
        query = head_rows(qkv_ref, window, inside)
        grad = head_rows(grad_ref, window, inside)
        total = totals_ref[pl.ds(head, 1), :]
        along = along_ref[pl.ds(head, 1), :]
        query_grad = None
        for block in range(blocks):
            own = block < blocks // 2
            at = pl.ds((block if own else block - blocks // 2) * span, span)
            key = qkv_ref[at, key_window] if own else key_ref[at, window]
            value = qkv_ref[at, value_window] if own else value_ref[at, window]
            row = mask_ref[block : block + 1, :] - total
            probs, grad_scores = head_terms(key, value, query, grad, row, along, factor)
            if own:
                key_part = jnp.dot(grad_scores, query, preferred_element_type=F32)
                value_part = jnp.dot(probs, grad, preferred_element_type=F32)
                pair_out[at, window] = jnp.where(inside, key_part, pair_out[at, window])
                pair_out[at, key_window] = jnp.where(inside, value_part, pair_out[at, key_window])
            part = contract(grad_scores, key, 0, 0)
            query_grad = part if query_grad is None else query_grad + part
        query_out[:, window] = jnp.where(
            inside, (query_grad * scale).astype(BF), query_out[:, window]
        )

    outs = [
        jax.ShapeDtypeStruct((rows, width), BF),
        jax.ShapeDtypeStruct((rows, 2 * width), F32),
    ]
    operands = (qkv, other, other, grad_mixed, totals, along, block_mask)
    in_specs = [pl.BlockSpec(array.shape, lambda h: (0, 0)) for array in operands]
    in_specs[1] = pl.BlockSpec((rows, width), lambda h: (0, 1))
    in_specs[2] = pl.BlockSpec((rows, width), lambda h: (0, 2))
    return pl.pallas_call(
        kernel,
        out_shape=outs,
        grid=(head_count,),
        in_specs=in_specs,
        out_specs=[pl.BlockSpec(array.shape, lambda h: (0, 0)) for array in outs],
        cost_estimate=cost(
            8 * head_count * rows * 2 * rows * 256, [qkv, qkv, *outs], head_count * rows * 2 * rows
        ),
        name="attend_back",
    )(*operands)


def attend_back_other(
    qkv, other, other_grad, other_totals, other_along, block_mask, query_grad, pair, head_count
):
    rows = qkv.shape[0]
    width = qkv.shape[1] // 3
    head_size = width // head_count
    blocks = block_mask.shape[0]
    span = rows // blocks
    scale = 1.0 / math.sqrt(head_size)
    factor = scale / math.log(2.0)

    def kernel(
        key_ref, value_ref, other_ref, grad_ref, totals_ref, along_ref, mask_ref, query_ref, pair_ref,
        out_ref,
    ):
        head = pl.program_id(0)

        @pl.when(head == 0)
        def _():
            out_ref[:, :width] = query_ref[...]

        start, inside = head_window(head, head_size, width)
        window = pl.ds(start, 256)
        key_window = pl.ds(start + width, 256)
        value_window = pl.ds(start + 2 * width, 256)
        query = head_rows(other_ref, window, inside)
        grad = head_rows(grad_ref, window, inside)
        total = totals_ref[pl.ds(head, 1), :]
        along = along_ref[pl.ds(head, 1), :]
        for block in range(blocks):
            at = pl.ds(block * span, span)
            row = mask_ref[block : block + 1, :] - total
            probs, grad_scores = head_terms(
                key_ref[at, window], value_ref[at, window], query, grad, row, along, factor
            )
            key_part = pair_ref[at, window] + jnp.dot(
                grad_scores, query, preferred_element_type=F32
            )
            value_part = pair_ref[at, key_window] + jnp.dot(
                probs, grad, preferred_element_type=F32
            )
            out_ref[at, key_window] = jnp.where(
                inside, (key_part * scale).astype(BF), out_ref[at, key_window]
            )
            out_ref[at, value_window] = jnp.where(
                inside, value_part.astype(BF), out_ref[at, value_window]
            )

    out = jax.ShapeDtypeStruct(qkv.shape, BF)
    operands = (
        qkv, qkv, other, other_grad, other_totals, other_along, block_mask, query_grad, pair
    )
    in_specs = [pl.BlockSpec(array.shape, lambda h: (0, 0)) for array in operands]
    in_specs[0] = pl.BlockSpec((rows, width), lambda h: (0, 1))
    in_specs[1] = pl.BlockSpec((rows, width), lambda h: (0, 2))
    in_specs[2] = pl.BlockSpec((rows, width), lambda h: (0, 0))
    return pl.pallas_call(
        kernel,
        out_shape=out,
        grid=(head_count,),
        in_specs=in_specs,
        out_specs=pl.BlockSpec(out.shape, lambda h: (0, 0)),
        cost_estimate=cost(
            8 * head_count * rows * rows * 256, [qkv, pair, out], head_count * rows * rows
        ),
        name="attend_back_other",
    )(*operands)


def cond_columns(steps, first, count, model_width):
    half_width = model_width // 2
    index = first + jnp.arange(count, dtype=jnp.int32)
    is_sine = index >= half_width
    place = jnp.where(is_sine, index - half_width, index).astype(F32)
    frequency = jnp.exp(-math.log(10000.0) * place / half_width)
    angles = steps.astype(F32)[:, None] * frequency[None, :]
    values = jnp.where(is_sine[None, :], jnp.sin(angles), jnp.cos(angles))
    return jax.nn.silu(values).astype(BF)


def normalize(values):
    centered = values - jnp.mean(values, axis=-1, keepdims=True)
    spread = jnp.mean(centered * centered, axis=-1, keepdims=True)
    inverse = lax.rsqrt(spread + 1e-06)
    return centered * inverse, inverse


def normalize_back(grad_normed, normed, inverse):
    along = jnp.mean(grad_normed * normed, axis=-1, keepdims=True)
    level = jnp.mean(grad_normed, axis=-1, keepdims=True)
    return inverse * (grad_normed - level - normed * along)


def body(
    tokens,
    qkv_weight,
    out_weight,
    up_weight,
    down_weight,
    mod_weight,
    qv_bias,
    out_bias,
    up_bias,
    down_bias,
    mod_bias,
    row_items,
    timesteps,
    head_mask,
    channel_mask,
    token_keep,
    cotangent,
):
    layer_count = qkv_weight.shape[0]
    width = out_weight.shape[2]
    hidden_width = up_weight.shape[2]
    head_count = head_mask.shape[3]
    head_size = width // head_count
    item_count = timesteps.shape[1]
    local_rows = tokens.shape[0]
    row_len = 2 * local_rows
    group_rows = row_len // item_count
    group_count = local_rows // group_rows
    scale_factor = 1.0 / math.sqrt(head_size)
    seq_count = lax.axis_size("seq")
    seq_bits = seq_count.bit_length() - 1
    device_count = 2 * seq_count
    half_index = lax.axis_index("fsdp")
    seq_index = lax.axis_index("seq")
    flat_index = half_index * seq_count + seq_index
    shard_rows = mod_weight.shape[1]
    items_here = row_items[0]
    far_stages = [("seq", bit) for bit in range(2, seq_bits)]
    core_stage = ("seq", 0)

    padded_rows = -(-shard_rows // 8) * 8
    row_cut = (padded_rows + 8) // 16 * 8
    x_stage, y_stage = ("fsdp", 0), ("seq", 1)
    routes = (core_stage, (y_stage, x_stage), (x_stage, y_stage), far_stages)
    far_count = 1 << len(far_stages)

    def flat_mask(stage):
        return seq_count if stage[0] == "fsdp" else 1 << stage[1]

    chunk_masks, chunk_places = [], []
    for core_mask in (0, 1):
        for two in range(2):
            for part, route in enumerate(routes[1:3]):
                part_rows = padded_rows - row_cut if part else row_cut
                first_mask = flat_mask(route[0]) if two else 0
                for mask in relative_masks([route[1], *far_stages], flat_mask):
                    chunk_masks += [core_mask ^ first_mask ^ mask] * part_rows
                    chunk_places += list(range(row_cut * part, row_cut * part + part_rows))
    chunk_masks = jnp.array(chunk_masks, jnp.int32)
    chunk_places = jnp.array(chunk_places, jnp.int32)
    source = jnp.where(
        chunk_places < shard_rows, (flat_index ^ chunk_masks) * shard_rows + chunk_places, -1
    )
    order = (source[:, None] == jnp.arange(width, dtype=jnp.int32)[None, :]).astype(BF)

    def ordered(left):
        return contract(left, order, 1, 1).astype(BF)

    feed = Feed()
    place_table = jnp.stack(
        [half_index, (seq_index >> 1) & 1, seq_index & 1]
        + [
            (seq_index >> 2) ^ (mask >> 2)
            for mask in relative_masks(far_stages, lambda stage: 1 << stage[1])
        ]
    ).astype(jnp.int32)

    def scatter_ordered(lefts, rights, waits, result):
        cuts = (far_count * 2 * row_cut, far_count * 2 * (padded_rows - row_cut))
        grads = ColumnGrads(lefts, rights, width)
        feed.start(reduce_flight(grads, routes, cuts, shard_rows, waits, result))

    def scatter_chunks(turned, right, waits, result):
        rows = turned.shape[0] // device_count
        grads = RowGrads(*take_chunks(turned, place_table, rows), right)
        cuts = (far_count * rows, far_count * rows)
        feed.start(reduce_flight(grads, routes, cuts, rows, waits, result))

    gathered = []

    def unit_ticks(unit):
        early = ((0, 1, 2, 4, 7, 8), (0, 2, 4, 9, 11, 12), (5, 9, 10, 13, 14, 15))
        late = ((8, 9, 13, 14, 16, 17), (9, 10, 14, 16, 20, 21), (14, 16, 19, 20, 24, 25))
        if unit < 3:
            return early[unit]
        return tuple(tick + 10 * (unit // 3 - 1) for tick in late[unit % 3])

    for layer in range(layer_count):
        for index, (shard, rows, cut) in enumerate(
            (
                ((qkv_weight[layer],), padded_rows, row_cut),
                ((up_weight[layer], out_weight[layer]), padded_rows, row_cut),
                ((down_weight[layer],), down_weight.shape[1], down_weight.shape[1] // 2),
            )
        ):
            result = []
            gathered.append(result)
            start, *due = unit_ticks(3 * layer + index)
            waits = [after - before for before, after in zip([start] + due, due)]
            feed.at(start, gather_flight(list(shard), rows, cut, routes, waits, result))

    def qkv_tiles(layer):
        return Tiles(gathered[3 * layer], width, 0, 3)

    def up_tiles(layer):
        tile = wide_tile(hidden_width) // 2
        return Tiles(gathered[3 * layer + 1], tile, 0, hidden_width // tile)

    def out_tiles(layer):
        return Tiles(gathered[3 * layer + 1], width, hidden_width // width, 1)

    biases = (qv_bias, out_bias, up_bias, down_bias, mod_bias)
    steps_high = (timesteps // 32).astype(BF)
    steps_low = (timesteps % 32).astype(BF)
    step_rows = jnp.concatenate([steps_high, steps_low], axis=0)
    if layer_count > 2:
        step_rows = jnp.pad(step_rows, ((0, layer_count - 2), (0, 0)))
    small = jnp.concatenate([*biases, step_rows], axis=1)
    small = feed.tick(small)
    small_stages = [("seq", bit) for bit in reversed(range(seq_bits))] + [x_stage]
    for index, stage in enumerate(small_stages):
        small = jnp.concatenate([small, swap_bit(small, stage)], axis=0)
        if index == 1:
            small = feed.tick(small)
    small_masks = jnp.array(relative_masks(list(reversed(small_stages)), flat_mask), jnp.int32)
    put_back = (flat_index ^ small_masks)[None, :] == jnp.arange(device_count)[:, None]
    small_columns = small.shape[1]
    every_small = jnp.dot(
        put_back.astype(BF),
        small.reshape(device_count, layer_count * small_columns),
        preferred_element_type=F32,
    ).reshape(device_count, layer_count, small_columns)
    bias_columns = small_columns - item_count
    every_small, tokens, head_mask, channel_mask, token_keep = feed.tick(
        (every_small, tokens, head_mask, channel_mask, token_keep)
    )
    step_parts = every_small[:seq_count, :2, bias_columns:].reshape(seq_count, 2 * item_count)

    def unpack_biases(every):
        offset = 0
        full = []
        for bias in biases:
            columns = bias.shape[1]
            full.append(
                [every[:, layer, offset : offset + columns].reshape(-1) for layer in range(layer_count)]
            )
            offset += columns
        return full

    every_step = step_parts[:, :item_count] * 32.0 + step_parts[:, item_count:]

    cond_every = cond_columns(every_step.reshape(-1), flat_index * shard_rows, shard_rows, width)
    seq_masks = jnp.array(
        relative_masks([("seq", bit) for bit in range(seq_bits)], lambda stage: 1 << stage[1]),
        jnp.int32,
    )
    pick_row = (seq_index ^ seq_masks)[:, None] == jnp.arange(seq_count)[None, :]
    cond_relative = (
        jnp.sum(
            jnp.where(
                pick_row[:, :, None, None],
                cond_every.astype(F32).reshape(1, seq_count, item_count, shard_rows),
                0.0,
            ),
            axis=1,
        )
        .astype(BF)
        .reshape(seq_count * item_count, shard_rows)
    )

    mod_stages = [("seq", bit) for bit in range(seq_bits)] + [("fsdp", 0)]

    def modulation_part(layer):
        return jnp.dot(cond_relative, mod_weight[layer], preferred_element_type=F32)

    full_biases = unpack_biases(every_small)
    block = jnp.concatenate([modulation_part(layer) for layer in range(layer_count)], axis=1)
    block = feed.tick(block)
    for index, stage in enumerate(mod_stages[:-1]):
        half = block.shape[0] // 2
        block = block[:half] + swap_bit(block[half:], stage)
        if index == 1:
            block = feed.tick(block)
    block, full_biases = feed.tick((block + swap_bit(block, mod_stages[-1]), full_biases))
    mod_width = block.shape[1] // layer_count
    modulations = [
        block[:, layer * mod_width : (layer + 1) * mod_width] + full_biases[4][layer][None]
        for layer in range(layer_count)
    ]

    group_item = (
        (half_index * local_rows + jnp.arange(group_count, dtype=jnp.int32) * group_rows)
        * items_here
        // row_len
    )
    other_item = (
        ((1 - half_index) * local_rows + jnp.arange(group_count, dtype=jnp.int32) * group_rows)
        * items_here
        // row_len
    )
    group_is = group_item[:, None] == jnp.arange(item_count, dtype=jnp.int32)[None, :]

    def of_groups(table):
        return jnp.sum(
            jnp.where(group_is[:, :, None], table.astype(F32)[None], 0.0), axis=1, keepdims=False
        )[:, None, :]

    block_item = jnp.concatenate([group_item, other_item])
    block_mask = jnp.where(group_item[:, None] == block_item[None, :], 0.0, -1e30).astype(F32)
    query_mask = jnp.repeat(block_mask, group_rows, axis=1)
    key_mask = jnp.repeat(block_mask.T, group_rows, axis=1)
    cross_mask = jnp.repeat(block_mask[:, group_count:], group_rows, axis=1)

    head_lanes = (
        jnp.arange(width, dtype=jnp.int32)[None, :] // head_size
        == jnp.arange(head_count, dtype=jnp.int32)[:, None]
    ).astype(F32)

    def grouped(values):
        return values.reshape(group_count, group_rows, values.shape[-1])

    def ungrouped(values):
        return values.reshape(local_rows, values.shape[-1])

    current = grouped(tokens.astype(F32))
    saved_layers = []
    full_downs = []
    for layer in range(layer_count):
        pair_bias, out_b, up_b, down_b = (full_biases[index][layer] for index in range(4))
        modulation = modulations[layer]
        shift_one, scale_one, gate_one, shift_two, scale_two, gate_two = jnp.split(
            of_groups(modulation), 6, axis=2
        )
        head_on = jnp.repeat(of_groups(head_mask[0, layer]), head_size, axis=2)[:, 0]
        channel_on = of_groups(channel_mask[0, layer])[:, 0]
        keep_tok = grouped(token_keep[:, layer].astype(F32)[:, None])
        normed_one, inverse_one = normalize(current)
        low_one = ungrouped((normed_one * (1.0 + scale_one) + shift_one).astype(BF))
        other_one = swap_bit(low_one, x_stage)
        bias_three = jnp.concatenate(
            [pair_bias[:width], jnp.zeros((width,), F32), pair_bias[width:]]
        )
        low_one = feed.tick(low_one)
        low_one = feed.tick(ordered(low_one))
        low_one = feed.tick(low_one)
        low_one = feed.until(gathered[3 * layer], low_one)
        qkv_low = project(low_one, qkv_tiles(layer), bias_three, BF, "project_qkv")
        qkv_low, other_one = lax.optimization_barrier((qkv_low, other_one))
        other_low = project(
            ordered(other_one), qkv_tiles(layer), bias_three, BF, "project_other"
        )
        other_low = feed.tick(other_low)
        mixed_low, mixed_wide, totals = attend(qkv_low, other_low, head_on, query_mask, head_count)
        totals = totals[:, :head_count].T
        other_totals = swap_bit(totals, x_stage)
        mixed_low = feed.tick(mixed_low)
        mixed_low = feed.tick(ordered(mixed_low))
        mixed_low = feed.tick(mixed_low)
        mixed_low = feed.until(gathered[3 * layer + 1], mixed_low)
        branch_one = grouped(project(mixed_low, out_tiles(layer), out_b, F32, "project_out"))
        after_attn = current + gate_one * branch_one
        normed_two, inverse_two = normalize(after_attn)
        low_two = ungrouped((normed_two * (1.0 + scale_two) + shift_two).astype(BF))
        low_two = feed.tick(ordered(low_two))
        hidden_pre, hidden_turned = project_up(low_two, up_tiles(layer), up_b, channel_on)
        hidden_turned = feed.tick(hidden_turned)
        hidden_turned = feed.tick(hidden_turned)
        hidden_turned = feed.until(gathered[3 * layer + 2], hidden_turned)
        full_down = place_chunks(*gathered[3 * layer + 2], place_table, (hidden_width, width))
        full_downs.append(full_down)
        branch_two = grouped(contract(hidden_turned, full_down, 0, 0) + down_b)
        saved_layers.append(
            dict(
                inputs=current,
                scale_one=scale_one,
                gate_one=gate_one,
                scale_two=scale_two,
                gate_two=gate_two,
                head_on=head_on,
                channel_on=channel_on,
                keep_tok=keep_tok,
                low_one=low_one,
                qkv_low=qkv_low,
                other_low=other_low,
                totals=totals,
                other_totals=other_totals,
                mixed_low=mixed_low,
                mixed_wide=mixed_wide,
                branch_one=branch_one,
                after_attn=after_attn,
                low_two=low_two,
                hidden_pre=hidden_pre,
                hidden_turned=hidden_turned,
                branch_two=branch_two,
            )
        )
        current = after_attn + keep_tok * gate_two * branch_two
    output = ungrouped(current).astype(BF)
    output = feed.finish(output)

    cond_rows = jnp.concatenate(
        [
            cond_every.reshape(seq_count, item_count, shard_rows),
            jnp.zeros((seq_count, 8 - item_count, shard_rows), BF),
        ],
        axis=1,
    ).reshape(seq_count * 8, shard_rows)
    cond_twice = jnp.concatenate([cond_rows, cond_rows], axis=0)

    def packet_flight(packet, wait, result):
        every = yield wait, lax.all_gather(packet, AXES, axis=0, tiled=True)
        grad_mod_weight = contract(cond_twice, every, 0, 0)
        sums = jnp.sum(every.astype(F32).reshape(device_count, *packet.shape), axis=0)

        def shard_of(row, start, columns):
            return lax.dynamic_slice_in_dim(row, start + flat_index * columns, columns, 0)

        grad_mod_bias = shard_of(jnp.sum(sums[:item_count], axis=0), 0, mod_bias.shape[1])
        bias_sum = sums[item_count:].reshape(-1)
        parts = []
        start = 0
        for bias in (qv_bias, out_bias, up_bias, down_bias):
            parts.append(shard_of(bias_sum, start, bias.shape[1]))
            start += device_count * bias.shape[1]
        grads = yield 1, (grad_mod_weight, *parts, grad_mod_bias)
        result.append(grads)

    grad_current = grouped(cotangent)
    layer_totals = [None] * layer_count
    for layer in reversed(range(layer_count)):
        saved = saved_layers[layer]
        kept_grad = grad_current * saved["keep_tok"]
        down_grad = ungrouped((kept_grad * saved["gate_two"]).astype(BF))
        grad_gate_two = jnp.sum(kept_grad * saved["branch_two"], axis=1)
        grad_down_bias = jnp.sum(down_grad.astype(F32), axis=0)
        down_rows, up_rows, out_rows, qkv_rows = [], [], [], []
        last = layer == 0
        scatter_chunks(saved["hidden_turned"], down_grad, (1, 1, 1, 2, 1, 1), down_rows)
        up_grad, grad_up_bias = hidden_back(
            down_grad, full_downs[layer], saved["hidden_pre"], saved["channel_on"], wide_tile(hidden_width) // 2
        )
        grad_up_bias = grad_up_bias[0]
        up_grad = feed.tick(feed.tick(up_grad))
        grad_after, out_grad, sums_two = project_norm_back(
            up_grad,
            up_tiles(layer),
            order,
            ungrouped(saved["after_attn"]),
            ungrouped(grad_current),
            saved["scale_two"][:, 0],
            ungrouped(saved["branch_one"]),
            saved["gate_one"][:, 0],
            "back_up",
        )
        grad_shift_two, grad_scale_two, grad_gate_one = (
            sums_two[part * group_count : (part + 1) * group_count] for part in range(3)
        )
        grad_out_bias = sums_two[3 * group_count]
        out_grad = feed.tick(feed.tick(out_grad))
        lefts, rights = (saved["low_two"], saved["mixed_low"]), (up_grad, out_grad)
        up_waits = (2, 0, 2, 2, 2, 2) if last else (2, 0, 2, 2, 2, 3)
        scatter_ordered(lefts, rights, up_waits, up_rows)
        grad_mixed = ungrouped(
            (
                grouped(project_back(out_grad, out_tiles(layer), order, 1, "back_out"))
                * saved["head_on"][:, None]
            ).astype(BF)
        )
        grad_mixed = feed.tick(grad_mixed)
        other_mixed = swap_bit(grad_mixed, x_stage)
        along = lax.dot_general(
            head_lanes,
            saved["mixed_wide"] * grad_mixed.astype(F32),
            (((1,), (1,)), ((), ())),
            precision=lax.Precision.HIGHEST,
            preferred_element_type=F32,
        )
        other_along = swap_bit(along, x_stage)
        grad_query, grad_pair = attend_back(
            saved["qkv_low"],
            saved["other_low"],
            grad_mixed,
            saved["totals"],
            along,
            key_mask,
            head_count,
        )
        grad_pair = feed.tick(grad_pair)
        grad_qkv = attend_back_other(
            saved["qkv_low"],
            saved["other_low"],
            other_mixed,
            saved["other_totals"],
            other_along,
            cross_mask,
            grad_query,
            grad_pair,
            head_count,
        )
        grad_qkv = feed.tick(grad_qkv)
        grad_qkv_bias = jnp.sum(grad_qkv.astype(F32), axis=0)
        qkv_waits = (1, 1, 1, 2) if last else (1, 0, 4, 2, 1, 2)
        scatter_ordered((saved["low_one"],), (grad_qkv,), qkv_waits, qkv_rows)
        if last:
            grad_qkv = feed.tick(feed.tick(grad_qkv))
        grad_inputs, sums_one = project_norm_back(
            grad_qkv,
            qkv_tiles(layer),
            order,
            ungrouped(saved["inputs"]),
            grad_after,
            saved["scale_one"][:, 0],
            None,
            None,
            "back_qkv",
        )
        grad_inputs = grouped(feed.tick(grad_inputs))
        grad_shift_one, grad_scale_one = (
            sums_one[part * group_count : (part + 1) * group_count] for part in range(2)
        )
        grad_groups = jnp.concatenate(
            [
                grad_shift_one,
                grad_scale_one,
                grad_gate_one,
                grad_shift_two,
                grad_scale_two,
                grad_gate_two,
            ],
            axis=1,
        )
        grad_slots = jnp.sum(jnp.where(group_is[:, :, None], grad_groups[:, None, :], 0.0), axis=0)
        mod_width = grad_slots.shape[1]
        bias_row = jnp.concatenate(
            [
                grad_qkv_bias[:width],
                grad_qkv_bias[2 * width :],
                grad_out_bias,
                grad_up_bias,
                grad_down_bias,
            ]
        )
        spare = jnp.zeros(((8 - item_count) * mod_width - bias_row.shape[0],), F32)
        packet = jnp.concatenate(
            [grad_slots, jnp.concatenate([bias_row, spare]).reshape(8 - item_count, mod_width)],
            axis=0,
        ).astype(BF)
        if last:
            grad_inputs, packet = feed.tick((grad_inputs, packet))
        shared_grads = []
        feed.start(packet_flight(packet, 3 if last else 7, shared_grads))
        grad_current = grad_inputs if last else feed.tick(grad_inputs)
        layer_totals[layer] = (
            qkv_rows,
            up_rows,
            up_rows,
            down_rows,
            shared_grads,
        )
    grad_current = feed.finish(grad_current)
    layer_totals = [
        (
            qkv[0],
            up[0][:, hidden_width:],
            up[0][:, :hidden_width],
            down[0],
            *shared[0],
        )
        for qkv, up, _, down, shared in layer_totals
    ]
    stacked = tuple(
        jnp.stack([layer_totals[layer][index] for layer in range(layer_count)])
        for index in range(10)
    )
    return (output, ungrouped(grad_current), *stacked)


def solution(mesh):
    rows = P(AXES, None)
    matrix = P(None, AXES, None)
    vector = P(None, AXES)
    return jax.shard_map(
        body,
        mesh=mesh,
        in_specs=(
            rows,
            matrix,
            matrix,
            matrix,
            matrix,
            matrix,
            vector,
            vector,
            vector,
            vector,
            vector,
            P("seq"),
            P("seq", None),
            P("seq", None, None, None),
            P("seq", None, None, None),
            rows,
            rows,
        ),
        out_specs=(
            rows,
            rows,
            matrix,
            matrix,
            matrix,
            matrix,
            matrix,
            vector,
            vector,
            vector,
            vector,
            vector,
        ),
        check_vma=False,
    )
```

```python
import math

import jax
import jax.numpy as jnp
from jax import lax
from jax.experimental import pallas as pl
from jax.experimental.pallas import tpu as pltpu
from jax.sharding import PartitionSpec as P

BF = jnp.bfloat16
F32 = jnp.float32
AXES = ("fsdp", "seq")


def swap_bit(block, stage):
    axis, bit = stage
    count = lax.axis_size(axis)
    return lax.ppermute(block, axis, [(low, low ^ (1 << bit)) for low in range(count)])


def stage_bit(stage):
    axis, bit = stage
    return (lax.axis_index(axis) >> bit) & 1


def contract(left, right, left_dim, right_dim):
    return lax.dot_general(
        left, right, (((left_dim,), (right_dim,)), ((), ())), preferred_element_type=F32
    )


def relative_masks(stages, mask_of):
    masks = [0]
    for stage in reversed(stages):
        masks = masks + [mask ^ mask_of(stage) for mask in masks]
    return masks


class Feed:
    def __init__(self):
        self.flights = []
        self.ticks = 0
        self.later = {}

    def start(self, flight):
        wait, parts = next(flight)
        self.flights.append((flight, self.ticks + wait - 1, parts))

    def at(self, tick, flight):
        self.later.setdefault(tick, []).append(flight)

    def tick(self, value):
        for flight in self.later.pop(self.ticks, []):
            self.start(flight)
        due = [entry for entry in self.flights if entry[1] <= self.ticks]
        flying = [entry for entry in self.flights if entry[1] > self.ticks]
        self.ticks += 1
        value, arrived = lax.optimization_barrier((value, [parts for _, _, parts in due]))
        for (flight, _, _), parts in zip(due, arrived):
            try:
                wait, sent = flight.send(parts)
                flying.append((flight, self.ticks + wait - 1, sent))
            except StopIteration:
                pass
        self.flights = flying
        return value

    def until(self, result, value):
        while not result:
            value = self.tick(value)
        return value

    def finish(self, value):
        while self.flights or self.later:
            value = self.tick(value)
        return value


def reduce_flight(grads, routes, cuts, rows, waits, result):
    core_stage, first_route, second_route, far_stages = routes
    first, second = cuts
    waits = list(waits) + [1] * 8
    arrived = yield waits[0], swap_bit(grads.away(), core_stage)
    parts = grads.stay(arrived, first, second)
    if waits[1]:
        parts = yield waits[1], parts
    kept, first_sent, second_sent = parts
    first_arrived, second_arrived = yield waits[2], (
        swap_bit(first_sent, first_route[0]),
        swap_bit(second_sent, second_route[0]),
    )

    def add(left, other, low, high):
        return left[low:high].astype(F32) + other[low:high].astype(F32)

    first_kept, second_kept = kept[:first], kept[first:]
    half_first, half_second = first // 2, second // 2
    first_sent = add(first_kept, first_arrived, half_first, first).astype(BF)
    second_sent = add(second_kept, second_arrived, half_second, second).astype(BF)
    first_kept = add(first_kept, first_arrived, 0, half_first).astype(BF)
    second_kept = add(second_kept, second_arrived, 0, half_second).astype(BF)
    first_arrived, second_arrived = yield waits[3], (
        swap_bit(first_sent, first_route[1]),
        swap_bit(second_sent, second_route[1]),
    )
    for index, stage in enumerate(far_stages):
        first, second = half_first, half_second
        half_first, half_second = first // 2, second // 2
        sent = jnp.concatenate(
            [
                add(first_kept, first_arrived, half_first, first),
                add(second_kept, second_arrived, half_second, second),
            ],
            axis=0,
        ).astype(BF)
        first_kept = add(first_kept, first_arrived, 0, half_first).astype(BF)
        second_kept = add(second_kept, second_arrived, 0, half_second).astype(BF)
        arrived = yield waits[4 + index], swap_bit(sent, stage)
        first_arrived, second_arrived = arrived[:half_first], arrived[half_first:]
    block = jnp.concatenate(
        [
            add(first_kept, first_arrived, 0, half_first),
            add(second_kept, second_arrived, 0, half_second),
        ],
        axis=0,
    )
    result.append(block[:rows])


class ColumnGrads:
    def __init__(self, lefts, rights, tile):
        self.lefts, self.rights, self.tile = lefts, rights, tile
        self.half = lefts[0].shape[1] // 2
        self.counts = [right.shape[1] // tile for right in rights]

    def call(self, index, arrived, pieces, name):
        half, tile = self.half, self.tile
        tokens = self.lefts[0].shape[0]
        pairs = len(self.lefts)
        starts = [sum(self.counts[:pair]) for pair in range(pairs)]
        columns = sum(self.counts) * tile

        def kernel(*refs):
            lefts, rights = refs[:pairs], refs[pairs : 2 * pairs]
            rest = refs[2 * pairs :]
            if arrived is not None:
                arrived_ref, rest = rest[0], rest[1:]
            out_refs, turned_ref = rest[:-1], rest[-1]
            step = pl.program_id(0)

            def work(left_ref, right_ref, start):
                @pl.when(step == start)
                def _():
                    turned_ref[...] = left_ref[...].astype(F32).T.astype(BF)

                total = jnp.dot(turned_ref[...], right_ref[...], preferred_element_type=F32)
                if arrived is not None:
                    total = total + arrived_ref[...].astype(F32)
                total = total.astype(BF)
                low = 0
                for out_ref, count in zip(out_refs, pieces):
                    out_ref[...] = total[low : low + count]
                    low += count

            for left_ref, right_ref, start, count in zip(lefts, rights, starts, self.counts):
                if pairs == 1:
                    work(left_ref, right_ref, start)
                else:
                    pl.when((step >= start) & (step < start + count))(
                        lambda l=left_ref, r=right_ref, s=start: work(l, r, s)
                    )

        def right_spec(start, count):
            return pl.BlockSpec(
                (tokens, tile), lambda j: (0, jnp.clip(j - start, 0, count - 1))
            )

        operands = [*self.lefts, *self.rights]
        in_specs = [pl.BlockSpec((tokens, half), lambda j: (0, index)) for _ in self.lefts]
        in_specs += [right_spec(*pair) for pair in zip(starts, self.counts)]
        if arrived is not None:
            operands.append(arrived)
            in_specs.append(pl.BlockSpec((half, tile), lambda j: (0, j)))
        outs = [jax.ShapeDtypeStruct((count, columns), BF) for count in pieces]
        return pl.pallas_call(
            kernel,
            out_shape=outs,
            grid=(sum(self.counts),),
            in_specs=in_specs,
            out_specs=[pl.BlockSpec((count, tile), lambda j: (0, j)) for count in pieces],
            scratch_shapes=[pltpu.VMEM((half, tokens), BF)],
            cost_estimate=cost(2 * half * tokens * columns, [*operands, *outs]),
            name=name,
        )(*operands)

    def away(self):
        return self.call(1, None, [self.half], "away_grad")[0]

    def stay(self, arrived, first, second):
        return self.call(0, arrived, [self.half - first - second, first, second], "stay_grad")


class RowGrads:
    def __init__(self, stay, away, right):
        self.stay_rows, self.away_rows, self.right = stay, away, right

    def away(self):
        return contract(self.away_rows, self.right, 1, 0).astype(BF)

    def stay(self, arrived, first, second):
        left, right = self.stay_rows, self.right
        tokens, columns = right.shape
        assert first == second

        def kernel(left_ref, right_ref, arrived_ref, kept_ref, first_ref, second_ref):
            step = pl.program_id(0)
            total = jnp.dot(left_ref[...], right_ref[...], preferred_element_type=F32)
            total = (total + arrived_ref[...].astype(F32)).astype(BF)
            pl.when(step < 2)(lambda: kept_ref.__setitem__(..., total))
            pl.when(step == 2)(lambda: first_ref.__setitem__(..., total))
            pl.when(step == 3)(lambda: second_ref.__setitem__(..., total))

        outs = [jax.ShapeDtypeStruct((count, columns), BF) for count in (2 * first, first, second)]
        return pl.pallas_call(
            kernel,
            out_shape=outs,
            grid=(4,),
            in_specs=[
                pl.BlockSpec((first, tokens), lambda j: (j, 0)),
                pl.BlockSpec(right.shape, lambda j: (0, 0)),
                pl.BlockSpec((first, columns), lambda j: (j, 0)),
            ],
            out_specs=[
                pl.BlockSpec((first, columns), lambda j: (jnp.minimum(j, 1), 0)),
                pl.BlockSpec((first, columns), lambda j: (0, 0)),
                pl.BlockSpec((first, columns), lambda j: (0, 0)),
            ],
            cost_estimate=cost(
                2 * left.shape[0] * tokens * columns, [left, right, arrived, *outs]
            ),
            name="stay_rows",
        )(left, right, arrived)


def wide_tile(columns):
    return next(tile for tile in (1536, 1152, 768, 512, 384, 256, 128) if columns % tile == 0)


def run_through(flight):
    parts = None
    try:
        while True:
            _, parts = flight.send(parts)
    except StopIteration:
        pass


def gather_flight(shard, rows, cut, routes, waits, result):
    core_stage, first_route, second_route, far_stages = routes
    waits = [1] * (len(far_stages) - 2) + list(waits)
    parts = yield 1, shard
    shard = jnp.concatenate(parts, axis=1) if len(parts) > 1 else parts[0]
    if shard.shape[0] < rows:
        shard = jnp.pad(shard, ((0, rows - shard.shape[0]), (0, 0)))
    blocks = [shard]
    for stage in reversed(far_stages):
        sent = jnp.concatenate(blocks, axis=0) if len(blocks) > 1 else blocks[0]
        arrived = yield waits.pop(0), swap_bit(sent, stage)
        blocks = blocks + [
            arrived[start : start + rows] for start in range(0, arrived.shape[0], rows)
        ]
    owned = [
        jnp.concatenate([block[:cut] for block in blocks], axis=0),
        jnp.concatenate([block[cut:] for block in blocks], axis=0),
    ]
    routes = (second_route, first_route)
    arrived = yield (
        waits.pop(0),
        [swap_bit(part, route[0]) for part, route in zip(owned, routes)],
    )
    pairs = [jnp.concatenate([part, more], axis=0) for part, more in zip(owned, arrived)]
    fars = yield waits.pop(0), [swap_bit(pair, route[1]) for pair, route in zip(pairs, routes)]
    others = yield (
        waits.pop(0),
        [[swap_bit(pair, core_stage), swap_bit(far, core_stage)] for pair, far in zip(pairs, fars)],
    )
    for pair, far, other in zip(pairs, fars, others):
        result.append((pair, far, other[0], other[1]))


def take_chunks(left, places, chunk_rows):
    far_count = places.shape[0] - 3
    columns = left.shape[1]
    part_rows = chunk_rows // 2

    def take(places_ref, in_ref, stay_ref, away_ref):
        x_here, y_here, core_here = places_ref[0], places_ref[1], places_ref[2]
        for half in range(2):
            for one in range(2):
                for two in range(2):
                    x_place = jnp.bitwise_xor(x_here, two if half else one)
                    y_place = jnp.bitwise_xor(y_here, one if half else two)
                    stay_ref[two, half, one, 0] = in_ref[x_place, 0, y_place, core_here, half]
                    away_ref[two, half, one, 0] = in_ref[x_place, 0, y_place, 1 - core_here, half]

    shape = (2, 2, 2, far_count, part_rows, columns)
    out_spec = pl.BlockSpec(
        (2, 2, 2, 1, part_rows, columns), lambda i, places: (0, 0, 0, i, 0, 0)
    )
    parts = pl.pallas_call(
        take,
        out_shape=[jax.ShapeDtypeStruct(shape, left.dtype)] * 2,
        grid_spec=pltpu.PrefetchScalarGridSpec(
            num_scalar_prefetch=1,
            grid=(far_count,),
            in_specs=[
                pl.BlockSpec(
                    (2, 1, 2, 2, 2, part_rows, columns),
                    lambda i, places: (0, places[3 + i], 0, 0, 0, 0, 0),
                )
            ],
            out_specs=[out_spec, out_spec],
        ),
        cost_estimate=pl.CostEstimate(
            flops=0, bytes_accessed=4 * left.size, transcendentals=0
        ),
        name="take_chunks",
    )(places, left.reshape(2, far_count, 2, 2, 2, part_rows, columns))
    return [part.reshape(left.shape[0] // 2, columns) for part in parts]


def place_chunks(first, second, places, out_shape):
    far_count = places.shape[0] - 3
    columns = out_shape[1]
    rows = first[0].shape[0] // (2 * far_count)
    pieces = [piece.reshape(2, far_count, rows, columns) for piece in (*first, *second)]

    def place(places_ref, *refs):
        out_ref = refs[-1]
        x_here, y_here, core_here = places_ref[0], places_ref[1], places_ref[2]
        for half in range(2):
            for core in range(2):
                for two in range(2):
                    ref = refs[4 * half + 2 * core + two]
                    for one in range(2):
                        x_place = jnp.bitwise_xor(x_here, two if half else one)
                        y_place = jnp.bitwise_xor(y_here, one if half else two)
                        core_place = jnp.bitwise_xor(core_here, core)
                        out_ref[x_place, 0, y_place, core_place, half] = ref[one, 0]

    in_spec = pl.BlockSpec((2, 1, rows, columns), lambda i, places: (0, i, 0, 0))
    view = (2, far_count, 2, 2, 2, rows, columns)
    return pl.pallas_call(
        place,
        out_shape=jax.ShapeDtypeStruct(view, BF),
        grid_spec=pltpu.PrefetchScalarGridSpec(
            num_scalar_prefetch=1,
            grid=(far_count,),
            in_specs=[in_spec] * 8,
            out_specs=pl.BlockSpec(
                (2, 1, 2, 2, 2, rows, columns), lambda i, places: (0, places[3 + i], 0, 0, 0, 0, 0)
            ),
        ),
        cost_estimate=pl.CostEstimate(
            flops=0, bytes_accessed=4 * out_shape[0] * columns, transcendentals=0
        ),
        name="place_chunks",
    )(places, *pieces).reshape(out_shape)


class Tiles:
    def __init__(self, parts, tile, start, count):
        first, second = parts
        self.pieces = [piece for pair in zip(first, second) for piece in pair]
        self.tile, self.start, self.count = tile, start, count
        self.rows = sum(piece.shape[0] for piece in self.pieces)

    def operands(self):
        return list(self.pieces)

    def specs(self):
        return [
            pl.BlockSpec((piece.shape[0], self.tile), lambda j: (0, self.start + j))
            for piece in self.pieces
        ]

    def weight(self, refs):
        return jnp.concatenate([ref[...] for ref in refs[:8]], axis=0)

    def columns(self):
        return self.count * self.tile


def cost(flops, arrays, transcendentals=0):
    return pl.CostEstimate(
        flops=int(flops),
        bytes_accessed=int(sum(array.size * array.dtype.itemsize for array in arrays)),
        transcendentals=int(transcendentals),
    )


def project(left, tiles, bias, out_dtype, name):
    rows = left.shape[0]
    operands = tiles.operands()

    def kernel(left_ref, bias_ref, *refs):
        out_ref = refs[-1]

        total = jnp.dot(left_ref[...], tiles.weight(refs), preferred_element_type=F32)
        out_ref[...] = (total + bias_ref[...]).astype(out_dtype)

    out = jax.ShapeDtypeStruct((rows, tiles.columns()), out_dtype)
    return pl.pallas_call(
        kernel,
        out_shape=out,
        grid=(tiles.count,),
        in_specs=[
            pl.BlockSpec(left.shape, lambda j: (0, 0)),
            pl.BlockSpec((1, tiles.tile), lambda j: (0, j)),
            *tiles.specs(),
        ],
        out_specs=pl.BlockSpec((rows, tiles.tile), lambda j: (0, j)),
        cost_estimate=cost(2 * rows * left.shape[1] * tiles.columns(), [left, out, *operands]),
        name=name,
    )(left, bias.reshape(1, -1), *operands)


def gelu_parts(value):
    inner = math.sqrt(2.0 / math.pi) * (value + 0.044715 * (value * value * value))
    return jnp.tanh(inner)


def project_up(left, tiles, bias, channel_on):
    rows = left.shape[0]
    groups = channel_on.shape[0]
    operands = tiles.operands()

    def kernel(left_ref, bias_ref, channel_ref, *refs):
        pre_ref, turned_ref = refs[-2:]

        pre = jnp.dot(left_ref[...], tiles.weight(refs), preferred_element_type=F32)
        pre = pre + bias_ref[...]
        pre_ref[...] = pre
        hidden = 0.5 * pre * (1.0 + gelu_parts(pre))
        span = rows // groups
        for group in range(groups):
            part = hidden[group * span : (group + 1) * span] * channel_ref[group : group + 1]
            turned_ref[:, group * span : (group + 1) * span] = part.T.astype(BF)

    pre = jax.ShapeDtypeStruct((rows, tiles.columns()), F32)
    turned = jax.ShapeDtypeStruct((tiles.columns(), rows), BF)
    return pl.pallas_call(
        kernel,
        out_shape=[pre, turned],
        grid=(tiles.count,),
        in_specs=[
            pl.BlockSpec(left.shape, lambda j: (0, 0)),
            pl.BlockSpec((1, tiles.tile), lambda j: (0, j)),
            pl.BlockSpec((groups, tiles.tile), lambda j: (0, j)),
            *tiles.specs(),
        ],
        out_specs=[
            pl.BlockSpec((rows, tiles.tile), lambda j: (0, j)),
            pl.BlockSpec((tiles.tile, rows), lambda j: (j, 0)),
        ],
        cost_estimate=cost(
            2 * rows * left.shape[1] * tiles.columns(), [left, pre, turned, *operands], pre.size
        ),
        name="project_up",
    )(left, bias.reshape(1, -1), channel_on, *operands)


def project_back(right, tiles, order, parts, name):
    rows = right.shape[0]
    operands = tiles.operands()
    width = order.shape[1]

    def kernel(right_ref, order_ref, *refs):
        out_ref, total_ref = refs[-2:]
        index = pl.program_id(0)

        @pl.when(index == 0)
        def _():
            total_ref[...] = jnp.zeros_like(total_ref)

        total_ref[...] += contract(right_ref[...], tiles.weight(refs), 1, 1)

        @pl.when(index == tiles.count - 1)
        def _():
            rest = total_ref[...]
            out = None
            for part in range(parts):
                high = rest.astype(BF)
                placed = jnp.dot(high, order_ref[...], preferred_element_type=F32)
                out = placed if out is None else out + placed
                if part < parts - 1:
                    rest = rest - high.astype(F32)
            out_ref[...] = out

    out = jax.ShapeDtypeStruct((rows, width), F32)
    return pl.pallas_call(
        kernel,
        out_shape=out,
        grid=(tiles.count,),
        in_specs=[
            pl.BlockSpec((rows, tiles.tile), lambda j: (0, j)),
            pl.BlockSpec(order.shape, lambda j: (0, 0)),
            *tiles.specs(),
        ],
        out_specs=pl.BlockSpec(out.shape, lambda j: (0, 0)),
        scratch_shapes=[pltpu.VMEM((rows, tiles.rows), F32)],
        cost_estimate=cost(
            2 * rows * tiles.rows * (tiles.columns() + parts * width), [right, out, order, *operands]
        ),
        name=name,
    )(right, order, *operands)


def project_norm_back(right, tiles, order, inputs, residual, scale, branch, gate, name):
    rows = right.shape[0]
    operands = tiles.operands()
    width = order.shape[1]
    groups = scale.shape[0]
    span = rows // groups
    gated = branch is not None
    chunk = min(span, 128)

    def kernel(right_ref, order_ref, inputs_ref, residual_ref, scale_ref, *refs):
        if gated:
            branch_ref, gate_ref, refs = refs[0], refs[1], refs[2:]
        pieces, refs = refs[:8], refs[8:]
        if gated:
            after_ref, product_ref, sums_ref, total_ref = refs
        else:
            after_ref, sums_ref, total_ref = refs
        index = pl.program_id(0)

        @pl.when(index == 0)
        def _():
            total_ref[...] = jnp.zeros_like(total_ref)

        total_ref[...] += contract(right_ref[...], tiles.weight(pieces), 1, 1)

        @pl.when(index == tiles.count - 1)
        def _():
            sums_ref[...] = jnp.zeros_like(sums_ref)

            def add_sum(row, values):
                along = jnp.sum(values, axis=0, keepdims=True)
                sums_ref[row : row + 1, :] = sums_ref[row : row + 1, :] + along

            for low in range(0, rows, chunk):
                at = pl.ds(low, chunk)
                group = low // span
                rest = total_ref[at, :]
                high = rest.astype(BF)
                grad = jnp.dot(high, order_ref[...], preferred_element_type=F32)
                lower = (rest - high.astype(F32)).astype(BF)
                grad = grad + jnp.dot(lower, order_ref[...], preferred_element_type=F32)
                normed, inverse = normalize(inputs_ref[at, :])
                add_sum(group, grad)
                add_sum(groups + group, grad * normed)
                after = residual_ref[at, :] + normalize_back(
                    grad * (1.0 + scale_ref[group : group + 1, :]), normed, inverse
                )
                after_ref[at, :] = after
                if gated:
                    product = (after * gate_ref[group : group + 1, :]).astype(BF)
                    product_ref[at, :] = product
                    add_sum(2 * groups + group, after * branch_ref[at, :])
                    add_sum(3 * groups, product.astype(F32))

    whole = lambda shape: pl.BlockSpec(shape, lambda j: (0, 0))
    wide = jax.ShapeDtypeStruct((rows, width), F32)
    outs = [wide] + ([jax.ShapeDtypeStruct((rows, width), BF)] if gated else [])
    outs.append(jax.ShapeDtypeStruct((3 * groups + 2, width), F32))
    extra = [branch, gate] if gated else []
    others = [order, inputs, residual, scale, *extra]
    return pl.pallas_call(
        kernel,
        out_shape=outs,
        grid=(tiles.count,),
        in_specs=[
            pl.BlockSpec((rows, tiles.tile), lambda j: (0, j)),
            *[whole(array.shape) for array in others],
            *tiles.specs(),
        ],
        out_specs=[whole(out.shape) for out in outs],
        scratch_shapes=[pltpu.VMEM((rows, tiles.rows), F32)],
        cost_estimate=cost(
            2 * rows * tiles.rows * (tiles.columns() + 2 * width), [right, *others, *outs, *operands]
        ),
        name=name,
    )(right, *others, *operands)


def hidden_back(down_grad, full_down, pre, channel_on, tile):
    rows, width = down_grad.shape
    groups = channel_on.shape[0]
    columns = pre.shape[1]

    def kernel(grad_ref, weight_ref, pre_ref, channel_ref, out_ref, sum_ref):
        value = pre_ref[...]
        tanh = gelu_parts(value)
        slope = 0.5 * (1.0 + tanh) + 0.5 * value * (1.0 - tanh * tanh) * math.sqrt(
            2.0 / math.pi
        ) * (1.0 + 3.0 * 0.044715 * value * value)
        grad = contract(grad_ref[...], weight_ref[...], 1, 1) * slope
        span = rows // groups
        total = None
        for group in range(groups):
            part = (
                grad[group * span : (group + 1) * span] * channel_ref[group : group + 1]
            ).astype(BF)
            out_ref[group * span : (group + 1) * span] = part
            along = jnp.sum(part.astype(F32), axis=0, keepdims=True)
            total = along if total is None else total + along
        sum_ref[...] = total

    out = jax.ShapeDtypeStruct((rows, columns), BF)
    sums = jax.ShapeDtypeStruct((1, columns), F32)
    return pl.pallas_call(
        kernel,
        out_shape=[out, sums],
        grid=(columns // tile,),
        in_specs=[
            pl.BlockSpec(down_grad.shape, lambda j: (0, 0)),
            pl.BlockSpec((tile, width), lambda j: (j, 0)),
            pl.BlockSpec((rows, tile), lambda j: (0, j)),
            pl.BlockSpec((groups, tile), lambda j: (0, j)),
        ],
        out_specs=[
            pl.BlockSpec((rows, tile), lambda j: (0, j)),
            pl.BlockSpec((1, tile), lambda j: (0, j)),
        ],
        cost_estimate=cost(
            2 * rows * width * columns, [down_grad, full_down, pre, out], rows * columns
        ),
        name="hidden_back",
    )(down_grad, full_down, pre, channel_on)


def head_window(head, head_size, width):
    start = jnp.minimum(head * head_size // 128, width // 128 - 2) * 128
    lane = lax.broadcasted_iota(jnp.int32, (1, 256), 1) + start
    inside = (lane >= head * head_size) & (lane < (head + 1) * head_size)
    return pl.multiple_of(start, 128), inside


def attend(qkv, other, head_on, block_mask, head_count):
    rows = qkv.shape[0]
    width = qkv.shape[1] // 3
    head_size = width // head_count
    groups = head_on.shape[0]
    span = rows // groups
    factor = 1.0 / math.sqrt(head_size) / math.log(2.0)

    def kernel(
        qkv_ref, key_ref, value_ref, head_ref, mask_ref, mixed_ref, wide_ref, total_ref
    ):
        head = pl.program_id(0)
        start, inside = head_window(head, head_size, width)
        window = pl.ds(start, 256)
        key_window = pl.ds(start + width, 256)
        value_window = pl.ds(start + 2 * width, 256)
        keys = (qkv_ref[:, key_window], key_ref[:, window])
        values = (qkv_ref[:, value_window], value_ref[:, window])
        for group in range(groups):
            at = pl.ds(group * span, span)
            query = qkv_ref[at, window]
            query = jnp.where(inside, query, jnp.zeros_like(query))
            scores = [
                contract(query, key, 1, 1) * factor
                + mask_ref[group : group + 1, side * rows : (side + 1) * rows]
                for side, key in enumerate(keys)
            ]
            largest = jnp.maximum(
                jnp.max(scores[0], axis=1, keepdims=True), jnp.max(scores[1], axis=1, keepdims=True)
            )
            powers = [jnp.exp2(score - largest) for score in scores]
            total = jnp.sum(powers[0], axis=1, keepdims=True) + jnp.sum(
                powers[1], axis=1, keepdims=True
            )
            inverse = 1.0 / total
            out = None
            for power, value in zip(powers, values):
                part = jnp.dot((power * inverse).astype(BF), value, preferred_element_type=F32)
                out = part if out is None else out + part
            out = out * head_ref[group : group + 1, window]
            wide_ref[at, window] = jnp.where(inside, out, wide_ref[at, window])
            mixed_ref[at, window] = jnp.where(inside, out.astype(BF), mixed_ref[at, window])
            lane = lax.broadcasted_iota(jnp.int32, (1, 128), 1)
            total_ref[at, :] = jnp.where(
                lane == head, largest + jnp.log2(total), total_ref[at, :]
            )

    mixed = jax.ShapeDtypeStruct((rows, width), BF)
    wide = jax.ShapeDtypeStruct((rows, width), F32)
    totals = jax.ShapeDtypeStruct((rows, 128), F32)
    operands = (qkv, other, other, head_on, block_mask)
    in_specs = [pl.BlockSpec(array.shape, lambda h: (0, 0)) for array in operands]
    in_specs[1] = pl.BlockSpec((rows, width), lambda h: (0, 1))
    in_specs[2] = pl.BlockSpec((rows, width), lambda h: (0, 2))
    return pl.pallas_call(
        kernel,
        out_shape=[mixed, wide, totals],
        grid=(head_count,),
        in_specs=in_specs,
        out_specs=[pl.BlockSpec(array.shape, lambda h: (0, 0)) for array in (mixed, wide, totals)],
        cost_estimate=cost(
            4 * head_count * rows * 2 * rows * 256, [qkv, other, mixed], head_count * rows * 2 * rows
        ),
        name="attend",
    )(*operands)


def head_terms(key, value, query, grad, row, along, factor):
    probs = jnp.exp2(contract(key, query, 1, 1) * factor + row)
    grad_scores = (probs * (contract(value, grad, 1, 1) - along)).astype(BF)
    return probs.astype(BF), grad_scores


def head_rows(ref, window, inside):
    values = ref[:, window]
    return jnp.where(inside, values, jnp.zeros_like(values))


def attend_back(qkv, other, grad_mixed, totals, along, block_mask, head_count):
    rows = qkv.shape[0]
    width = qkv.shape[1] // 3
    head_size = width // head_count
    blocks = block_mask.shape[0]
    span = 2 * rows // blocks
    scale = 1.0 / math.sqrt(head_size)
    factor = scale / math.log(2.0)

    def kernel(
        qkv_ref, key_ref, value_ref, grad_ref, totals_ref, along_ref, mask_ref, query_out, pair_out
    ):
        head = pl.program_id(0)
        start, inside = head_window(head, head_size, width)
        window = pl.ds(start, 256)
        key_window = pl.ds(start + width, 256)
        value_window = pl.ds(start + 2 * width, 256)
        query = head_rows(qkv_ref, window, inside)
        grad = head_rows(grad_ref, window, inside)
        total = totals_ref[pl.ds(head, 1), :]
        along = along_ref[pl.ds(head, 1), :]
        query_grad = None
        for block in range(blocks):
            own = block < blocks // 2
            at = pl.ds((block if own else block - blocks // 2) * span, span)
            key = qkv_ref[at, key_window] if own else key_ref[at, window]
            value = qkv_ref[at, value_window] if own else value_ref[at, window]
            row = mask_ref[block : block + 1, :] - total
            probs, grad_scores = head_terms(key, value, query, grad, row, along, factor)
            if own:
                key_part = jnp.dot(grad_scores, query, preferred_element_type=F32)
                value_part = jnp.dot(probs, grad, preferred_element_type=F32)
                pair_out[at, window] = jnp.where(inside, key_part, pair_out[at, window])
                pair_out[at, key_window] = jnp.where(inside, value_part, pair_out[at, key_window])
            part = contract(grad_scores, key, 0, 0)
            query_grad = part if query_grad is None else query_grad + part
        query_out[:, window] = jnp.where(
            inside, (query_grad * scale).astype(BF), query_out[:, window]
        )

    outs = [
        jax.ShapeDtypeStruct((rows, width), BF),
        jax.ShapeDtypeStruct((rows, 2 * width), F32),
    ]
    operands = (qkv, other, other, grad_mixed, totals, along, block_mask)
    in_specs = [pl.BlockSpec(array.shape, lambda h: (0, 0)) for array in operands]
    in_specs[1] = pl.BlockSpec((rows, width), lambda h: (0, 1))
    in_specs[2] = pl.BlockSpec((rows, width), lambda h: (0, 2))
    return pl.pallas_call(
        kernel,
        out_shape=outs,
        grid=(head_count,),
        in_specs=in_specs,
        out_specs=[pl.BlockSpec(array.shape, lambda h: (0, 0)) for array in outs],
        cost_estimate=cost(
            8 * head_count * rows * 2 * rows * 256, [qkv, qkv, *outs], head_count * rows * 2 * rows
        ),
        name="attend_back",
    )(*operands)


def attend_back_other(
    qkv, other, other_grad, other_totals, other_along, block_mask, query_grad, pair, head_count
):
    rows = qkv.shape[0]
    width = qkv.shape[1] // 3
    head_size = width // head_count
    blocks = block_mask.shape[0]
    span = rows // blocks
    scale = 1.0 / math.sqrt(head_size)
    factor = scale / math.log(2.0)

    def kernel(
        key_ref, value_ref, other_ref, grad_ref, totals_ref, along_ref, mask_ref, query_ref, pair_ref,
        out_ref,
    ):
        head = pl.program_id(0)

        @pl.when(head == 0)
        def _():
            out_ref[:, :width] = query_ref[...]

        start, inside = head_window(head, head_size, width)
        window = pl.ds(start, 256)
        key_window = pl.ds(start + width, 256)
        value_window = pl.ds(start + 2 * width, 256)
        query = head_rows(other_ref, window, inside)
        grad = head_rows(grad_ref, window, inside)
        total = totals_ref[pl.ds(head, 1), :]
        along = along_ref[pl.ds(head, 1), :]
        for block in range(blocks):
            at = pl.ds(block * span, span)
            row = mask_ref[block : block + 1, :] - total
            probs, grad_scores = head_terms(
                key_ref[at, window], value_ref[at, window], query, grad, row, along, factor
            )
            key_part = pair_ref[at, window] + jnp.dot(
                grad_scores, query, preferred_element_type=F32
            )
            value_part = pair_ref[at, key_window] + jnp.dot(
                probs, grad, preferred_element_type=F32
            )
            out_ref[at, key_window] = jnp.where(
                inside, (key_part * scale).astype(BF), out_ref[at, key_window]
            )
            out_ref[at, value_window] = jnp.where(
                inside, value_part.astype(BF), out_ref[at, value_window]
            )

    out = jax.ShapeDtypeStruct(qkv.shape, BF)
    operands = (
        qkv, qkv, other, other_grad, other_totals, other_along, block_mask, query_grad, pair
    )
    in_specs = [pl.BlockSpec(array.shape, lambda h: (0, 0)) for array in operands]
    in_specs[0] = pl.BlockSpec((rows, width), lambda h: (0, 1))
    in_specs[1] = pl.BlockSpec((rows, width), lambda h: (0, 2))
    in_specs[2] = pl.BlockSpec((rows, width), lambda h: (0, 0))
    return pl.pallas_call(
        kernel,
        out_shape=out,
        grid=(head_count,),
        in_specs=in_specs,
        out_specs=pl.BlockSpec(out.shape, lambda h: (0, 0)),
        cost_estimate=cost(
            8 * head_count * rows * rows * 256, [qkv, pair, out], head_count * rows * rows
        ),
        name="attend_back_other",
    )(*operands)


def cond_columns(steps, first, count, model_width):
    half_width = model_width // 2
    index = first + jnp.arange(count, dtype=jnp.int32)
    is_sine = index >= half_width
    place = jnp.where(is_sine, index - half_width, index).astype(F32)
    frequency = jnp.exp(-math.log(10000.0) * place / half_width)
    angles = steps.astype(F32)[:, None] * frequency[None, :]
    values = jnp.where(is_sine[None, :], jnp.sin(angles), jnp.cos(angles))
    return jax.nn.silu(values).astype(BF)


def normalize(values):
    centered = values - jnp.mean(values, axis=-1, keepdims=True)
    spread = jnp.mean(centered * centered, axis=-1, keepdims=True)
    inverse = lax.rsqrt(spread + 1e-06)
    return centered * inverse, inverse


def normalize_back(grad_normed, normed, inverse):
    along = jnp.mean(grad_normed * normed, axis=-1, keepdims=True)
    level = jnp.mean(grad_normed, axis=-1, keepdims=True)
    return inverse * (grad_normed - level - normed * along)


def body(
    tokens,
    qkv_weight,
    out_weight,
    up_weight,
    down_weight,
    mod_weight,
    qv_bias,
    out_bias,
    up_bias,
    down_bias,
    mod_bias,
    row_items,
    timesteps,
    head_mask,
    channel_mask,
    token_keep,
    cotangent,
):
    layer_count = qkv_weight.shape[0]
    width = out_weight.shape[2]
    hidden_width = up_weight.shape[2]
    head_count = head_mask.shape[3]
    head_size = width // head_count
    item_count = timesteps.shape[1]
    local_rows = tokens.shape[0]
    row_len = 2 * local_rows
    group_rows = row_len // item_count
    group_count = local_rows // group_rows
    scale_factor = 1.0 / math.sqrt(head_size)
    seq_count = lax.axis_size("seq")
    seq_bits = seq_count.bit_length() - 1
    device_count = 2 * seq_count
    half_index = lax.axis_index("fsdp")
    seq_index = lax.axis_index("seq")
    flat_index = half_index * seq_count + seq_index
    shard_rows = mod_weight.shape[1]
    items_here = row_items[0]
    far_stages = [("seq", bit) for bit in range(2, seq_bits)]
    core_stage = ("seq", 0)

    padded_rows = -(-shard_rows // 8) * 8
    row_cut = (padded_rows + 8) // 16 * 8
    x_stage, y_stage = ("fsdp", 0), ("seq", 1)
    routes = (core_stage, (y_stage, x_stage), (x_stage, y_stage), far_stages)
    far_count = 1 << len(far_stages)

    def flat_mask(stage):
        return seq_count if stage[0] == "fsdp" else 1 << stage[1]

    chunk_masks, chunk_places = [], []
    for core_mask in (0, 1):
        for two in range(2):
            for part, route in enumerate(routes[1:3]):
                part_rows = padded_rows - row_cut if part else row_cut
                first_mask = flat_mask(route[0]) if two else 0
                for mask in relative_masks([route[1], *far_stages], flat_mask):
                    chunk_masks += [core_mask ^ first_mask ^ mask] * part_rows
                    chunk_places += list(range(row_cut * part, row_cut * part + part_rows))
    chunk_masks = jnp.array(chunk_masks, jnp.int32)
    chunk_places = jnp.array(chunk_places, jnp.int32)
    source = jnp.where(
        chunk_places < shard_rows, (flat_index ^ chunk_masks) * shard_rows + chunk_places, -1
    )
    order = (source[:, None] == jnp.arange(width, dtype=jnp.int32)[None, :]).astype(BF)

    def ordered(left):
        return contract(left, order, 1, 1).astype(BF)

    feed = Feed()
    place_table = jnp.stack(
        [half_index, (seq_index >> 1) & 1, seq_index & 1]
        + [
            (seq_index >> 2) ^ (mask >> 2)
            for mask in relative_masks(far_stages, lambda stage: 1 << stage[1])
        ]
    ).astype(jnp.int32)

    def scatter_ordered(lefts, rights, waits, result):
        cuts = (far_count * 2 * row_cut, far_count * 2 * (padded_rows - row_cut))
        grads = ColumnGrads(lefts, rights, width)
        feed.start(reduce_flight(grads, routes, cuts, shard_rows, waits, result))

    def scatter_chunks(turned, right, waits, result):
        rows = turned.shape[0] // device_count
        grads = RowGrads(*take_chunks(turned, place_table, rows), right)
        cuts = (far_count * rows, far_count * rows)
        feed.start(reduce_flight(grads, routes, cuts, rows, waits, result))

    gathered = []

    def unit_ticks(unit):
        early = ((0, 1, 2, 4, 7, 8), (0, 2, 4, 9, 11, 12), (5, 9, 10, 13, 14, 15))
        late = ((9, 10, 13, 14, 16, 17), (10, 13, 14, 16, 20, 21), (14, 16, 19, 20, 24, 25))
        if unit < 3:
            return early[unit]
        return tuple(tick + 10 * (unit // 3 - 1) for tick in late[unit % 3])

    for layer in range(layer_count):
        for index, (shard, rows, cut) in enumerate(
            (
                ((qkv_weight[layer],), padded_rows, row_cut),
                ((up_weight[layer], out_weight[layer]), padded_rows, row_cut),
                ((down_weight[layer],), down_weight.shape[1], down_weight.shape[1] // 2),
            )
        ):
            result = []
            gathered.append(result)
            start, *due = unit_ticks(3 * layer + index)
            waits = [after - before for before, after in zip([start] + due, due)]
            feed.at(start, gather_flight(list(shard), rows, cut, routes, waits, result))

    def qkv_tiles(layer):
        return Tiles(gathered[3 * layer], width, 0, 3)

    def up_tiles(layer):
        tile = wide_tile(hidden_width) // 2
        return Tiles(gathered[3 * layer + 1], tile, 0, hidden_width // tile)

    def out_tiles(layer):
        return Tiles(gathered[3 * layer + 1], width, hidden_width // width, 1)

    biases = (qv_bias, out_bias, up_bias, down_bias, mod_bias)
    steps_high = (timesteps // 32).astype(BF)
    steps_low = (timesteps % 32).astype(BF)
    step_rows = jnp.concatenate([steps_high, steps_low], axis=0)
    if layer_count > 2:
        step_rows = jnp.pad(step_rows, ((0, layer_count - 2), (0, 0)))
    small = jnp.concatenate([*biases, step_rows], axis=1)
    small = feed.tick(small)
    small_stages = [("seq", bit) for bit in reversed(range(seq_bits))] + [x_stage]
    for index, stage in enumerate(small_stages):
        small = jnp.concatenate([small, swap_bit(small, stage)], axis=0)
        if index == 1:
            small = feed.tick(small)
    small_masks = jnp.array(relative_masks(list(reversed(small_stages)), flat_mask), jnp.int32)
    put_back = (flat_index ^ small_masks)[None, :] == jnp.arange(device_count)[:, None]
    small_columns = small.shape[1]
    every_small = jnp.dot(
        put_back.astype(BF),
        small.reshape(device_count, layer_count * small_columns),
        preferred_element_type=F32,
    ).reshape(device_count, layer_count, small_columns)
    bias_columns = small_columns - item_count
    every_small, tokens, head_mask, channel_mask, token_keep = feed.tick(
        (every_small, tokens, head_mask, channel_mask, token_keep)
    )
    step_parts = every_small[:seq_count, :2, bias_columns:].reshape(seq_count, 2 * item_count)

    def unpack_biases(every):
        offset = 0
        full = []
        for bias in biases:
            columns = bias.shape[1]
            full.append(
                [every[:, layer, offset : offset + columns].reshape(-1) for layer in range(layer_count)]
            )
            offset += columns
        return full

    every_step = step_parts[:, :item_count] * 32.0 + step_parts[:, item_count:]

    cond_every = cond_columns(every_step.reshape(-1), flat_index * shard_rows, shard_rows, width)
    seq_masks = jnp.array(
        relative_masks([("seq", bit) for bit in range(seq_bits)], lambda stage: 1 << stage[1]),
        jnp.int32,
    )
    pick_row = (seq_index ^ seq_masks)[:, None] == jnp.arange(seq_count)[None, :]
    cond_relative = (
        jnp.sum(
            jnp.where(
                pick_row[:, :, None, None],
                cond_every.astype(F32).reshape(1, seq_count, item_count, shard_rows),
                0.0,
            ),
            axis=1,
        )
        .astype(BF)
        .reshape(seq_count * item_count, shard_rows)
    )

    mod_stages = [("seq", bit) for bit in range(seq_bits)] + [("fsdp", 0)]

    def modulation_part(layer):
        return jnp.dot(cond_relative, mod_weight[layer], preferred_element_type=F32)

    full_biases = unpack_biases(every_small)
    block = jnp.concatenate([modulation_part(layer) for layer in range(layer_count)], axis=1)
    block = feed.tick(block)
    for index, stage in enumerate(mod_stages[:-1]):
        half = block.shape[0] // 2
        block = block[:half] + swap_bit(block[half:], stage)
        if index == 1:
            block = feed.tick(block)
    block, full_biases = feed.tick((block + swap_bit(block, mod_stages[-1]), full_biases))
    mod_width = block.shape[1] // layer_count
    modulations = [
        block[:, layer * mod_width : (layer + 1) * mod_width] + full_biases[4][layer][None]
        for layer in range(layer_count)
    ]

    group_item = (
        (half_index * local_rows + jnp.arange(group_count, dtype=jnp.int32) * group_rows)
        * items_here
        // row_len
    )
    other_item = (
        ((1 - half_index) * local_rows + jnp.arange(group_count, dtype=jnp.int32) * group_rows)
        * items_here
        // row_len
    )
    group_is = group_item[:, None] == jnp.arange(item_count, dtype=jnp.int32)[None, :]

    def of_groups(table):
        return jnp.sum(
            jnp.where(group_is[:, :, None], table.astype(F32)[None], 0.0), axis=1, keepdims=False
        )[:, None, :]

    block_item = jnp.concatenate([group_item, other_item])
    block_mask = jnp.where(group_item[:, None] == block_item[None, :], 0.0, -1e30).astype(F32)
    query_mask = jnp.repeat(block_mask, group_rows, axis=1)
    key_mask = jnp.repeat(block_mask.T, group_rows, axis=1)
    cross_mask = jnp.repeat(block_mask[:, group_count:], group_rows, axis=1)

    head_lanes = (
        jnp.arange(width, dtype=jnp.int32)[None, :] // head_size
        == jnp.arange(head_count, dtype=jnp.int32)[:, None]
    ).astype(F32)

    def grouped(values):
        return values.reshape(group_count, group_rows, values.shape[-1])

    def ungrouped(values):
        return values.reshape(local_rows, values.shape[-1])

    current = grouped(tokens.astype(F32))
    saved_layers = []
    full_downs = []
    for layer in range(layer_count):
        pair_bias, out_b, up_b, down_b = (full_biases[index][layer] for index in range(4))
        modulation = modulations[layer]
        shift_one, scale_one, gate_one, shift_two, scale_two, gate_two = jnp.split(
            of_groups(modulation), 6, axis=2
        )
        head_on = jnp.repeat(of_groups(head_mask[0, layer]), head_size, axis=2)[:, 0]
        channel_on = of_groups(channel_mask[0, layer])[:, 0]
        keep_tok = grouped(token_keep[:, layer].astype(F32)[:, None])
        normed_one, inverse_one = normalize(current)
        low_one = ungrouped((normed_one * (1.0 + scale_one) + shift_one).astype(BF))
        other_one = swap_bit(low_one, x_stage)
        bias_three = jnp.concatenate(
            [pair_bias[:width], jnp.zeros((width,), F32), pair_bias[width:]]
        )
        low_one = feed.tick(low_one)
        low_one = feed.tick(ordered(low_one))
        low_one = feed.tick(low_one)
        low_one = feed.until(gathered[3 * layer], low_one)
        qkv_low = project(low_one, qkv_tiles(layer), bias_three, BF, "project_qkv")
        qkv_low, other_one = lax.optimization_barrier((qkv_low, other_one))
        other_low = project(
            ordered(other_one), qkv_tiles(layer), bias_three, BF, "project_other"
        )
        other_low = feed.tick(other_low)
        mixed_low, mixed_wide, totals = attend(qkv_low, other_low, head_on, query_mask, head_count)
        totals = totals[:, :head_count].T
        other_totals = swap_bit(totals, x_stage)
        mixed_low = feed.tick(mixed_low)
        mixed_low = feed.tick(ordered(mixed_low))
        mixed_low = feed.tick(mixed_low)
        mixed_low = feed.until(gathered[3 * layer + 1], mixed_low)
        branch_one = grouped(project(mixed_low, out_tiles(layer), out_b, F32, "project_out"))
        after_attn = current + gate_one * branch_one
        normed_two, inverse_two = normalize(after_attn)
        low_two = ungrouped((normed_two * (1.0 + scale_two) + shift_two).astype(BF))
        low_two = feed.tick(ordered(low_two))
        hidden_pre, hidden_turned = project_up(low_two, up_tiles(layer), up_b, channel_on)
        hidden_turned = feed.tick(hidden_turned)
        hidden_turned = feed.tick(hidden_turned)
        hidden_turned = feed.until(gathered[3 * layer + 2], hidden_turned)
        full_down = place_chunks(*gathered[3 * layer + 2], place_table, (hidden_width, width))
        full_downs.append(full_down)
        branch_two = grouped(contract(hidden_turned, full_down, 0, 0) + down_b)
        saved_layers.append(
            dict(
                inputs=current,
                scale_one=scale_one,
                gate_one=gate_one,
                scale_two=scale_two,
                gate_two=gate_two,
                head_on=head_on,
                channel_on=channel_on,
                keep_tok=keep_tok,
                low_one=low_one,
                qkv_low=qkv_low,
                other_low=other_low,
                totals=totals,
                other_totals=other_totals,
                mixed_low=mixed_low,
                mixed_wide=mixed_wide,
                branch_one=branch_one,
                after_attn=after_attn,
                low_two=low_two,
                hidden_pre=hidden_pre,
                hidden_turned=hidden_turned,
                branch_two=branch_two,
            )
        )
        current = after_attn + keep_tok * gate_two * branch_two
    output = ungrouped(current).astype(BF)
    output = feed.finish(output)

    cond_rows = jnp.concatenate(
        [
            cond_every.reshape(seq_count, item_count, shard_rows),
            jnp.zeros((seq_count, 8 - item_count, shard_rows), BF),
        ],
        axis=1,
    ).reshape(seq_count * 8, shard_rows)
    cond_twice = jnp.concatenate([cond_rows, cond_rows], axis=0)

    def packet_flight(packet, wait, result):
        every = yield wait, lax.all_gather(packet, AXES, axis=0, tiled=True)
        grad_mod_weight = contract(cond_twice, every, 0, 0)
        sums = jnp.sum(every.astype(F32).reshape(device_count, *packet.shape), axis=0)

        def shard_of(row, start, columns):
            return lax.dynamic_slice_in_dim(row, start + flat_index * columns, columns, 0)

        grad_mod_bias = shard_of(jnp.sum(sums[:item_count], axis=0), 0, mod_bias.shape[1])
        bias_sum = sums[item_count:].reshape(-1)
        parts = []
        start = 0
        for bias in (qv_bias, out_bias, up_bias, down_bias):
            parts.append(shard_of(bias_sum, start, bias.shape[1]))
            start += device_count * bias.shape[1]
        grads = yield 1, (grad_mod_weight, *parts, grad_mod_bias)
        result.append(grads)

    grad_current = grouped(cotangent)
    layer_totals = [None] * layer_count
    for layer in reversed(range(layer_count)):
        saved = saved_layers[layer]
        kept_grad = grad_current * saved["keep_tok"]
        down_grad = ungrouped((kept_grad * saved["gate_two"]).astype(BF))
        grad_gate_two = jnp.sum(kept_grad * saved["branch_two"], axis=1)
        grad_down_bias = jnp.sum(down_grad.astype(F32), axis=0)
        down_rows, up_rows, out_rows, qkv_rows = [], [], [], []
        last = layer == 0
        scatter_chunks(saved["hidden_turned"], down_grad, (1, 1, 1, 2, 1, 1), down_rows)
        up_grad, grad_up_bias = hidden_back(
            down_grad, full_downs[layer], saved["hidden_pre"], saved["channel_on"], wide_tile(hidden_width) // 2
        )
        grad_up_bias = grad_up_bias[0]
        up_grad = feed.tick(feed.tick(up_grad))
        grad_after, out_grad, sums_two = project_norm_back(
            up_grad,
            up_tiles(layer),
            order,
            ungrouped(saved["after_attn"]),
            ungrouped(grad_current),
            saved["scale_two"][:, 0],
            ungrouped(saved["branch_one"]),
            saved["gate_one"][:, 0],
            "back_up",
        )
        grad_shift_two, grad_scale_two, grad_gate_one = (
            sums_two[part * group_count : (part + 1) * group_count] for part in range(3)
        )
        grad_out_bias = sums_two[3 * group_count]
        out_grad = feed.tick(feed.tick(out_grad))
        lefts, rights = (saved["low_two"], saved["mixed_low"]), (up_grad, out_grad)
        up_waits = (2, 0, 2, 2, 2, 2) if last else (2, 0, 2, 2, 2, 3)
        scatter_ordered(lefts, rights, up_waits, up_rows)
        grad_mixed = ungrouped(
            (
                grouped(project_back(out_grad, out_tiles(layer), order, 1, "back_out"))
                * saved["head_on"][:, None]
            ).astype(BF)
        )
        grad_mixed = feed.tick(grad_mixed)
        other_mixed = swap_bit(grad_mixed, x_stage)
        along = lax.dot_general(
            head_lanes,
            saved["mixed_wide"] * grad_mixed.astype(F32),
            (((1,), (1,)), ((), ())),
            precision=lax.Precision.HIGHEST,
            preferred_element_type=F32,
        )
        other_along = swap_bit(along, x_stage)
        grad_query, grad_pair = attend_back(
            saved["qkv_low"],
            saved["other_low"],
            grad_mixed,
            saved["totals"],
            along,
            key_mask,
            head_count,
        )
        grad_pair = feed.tick(grad_pair)
        grad_qkv = attend_back_other(
            saved["qkv_low"],
            saved["other_low"],
            other_mixed,
            saved["other_totals"],
            other_along,
            cross_mask,
            grad_query,
            grad_pair,
            head_count,
        )
        grad_qkv = feed.tick(grad_qkv)
        grad_qkv_bias = jnp.sum(grad_qkv.astype(F32), axis=0)
        qkv_waits = (1, 1, 1, 2) if last else (1, 0, 4, 2, 1, 2)
        scatter_ordered((saved["low_one"],), (grad_qkv,), qkv_waits, qkv_rows)
        if last:
            grad_qkv = feed.tick(feed.tick(grad_qkv))
        grad_inputs, sums_one = project_norm_back(
            grad_qkv,
            qkv_tiles(layer),
            order,
            ungrouped(saved["inputs"]),
            grad_after,
            saved["scale_one"][:, 0],
            None,
            None,
            "back_qkv",
        )
        grad_inputs = grouped(feed.tick(grad_inputs))
        grad_shift_one, grad_scale_one = (
            sums_one[part * group_count : (part + 1) * group_count] for part in range(2)
        )
        grad_groups = jnp.concatenate(
            [
                grad_shift_one,
                grad_scale_one,
                grad_gate_one,
                grad_shift_two,
                grad_scale_two,
                grad_gate_two,
            ],
            axis=1,
        )
        grad_slots = jnp.sum(jnp.where(group_is[:, :, None], grad_groups[:, None, :], 0.0), axis=0)
        mod_width = grad_slots.shape[1]
        bias_row = jnp.concatenate(
            [
                grad_qkv_bias[:width],
                grad_qkv_bias[2 * width :],
                grad_out_bias,
                grad_up_bias,
                grad_down_bias,
            ]
        )
        spare = jnp.zeros(((8 - item_count) * mod_width - bias_row.shape[0],), F32)
        packet = jnp.concatenate(
            [grad_slots, jnp.concatenate([bias_row, spare]).reshape(8 - item_count, mod_width)],
            axis=0,
        ).astype(BF)
        if last:
            grad_inputs, packet = feed.tick((grad_inputs, packet))
        shared_grads = []
        feed.start(packet_flight(packet, 3 if last else 7, shared_grads))
        grad_current = grad_inputs if last else feed.tick(grad_inputs)
        layer_totals[layer] = (
            qkv_rows,
            up_rows,
            up_rows,
            down_rows,
            shared_grads,
        )
    grad_current = feed.finish(grad_current)
    layer_totals = [
        (
            qkv[0],
            up[0][:, hidden_width:],
            up[0][:, :hidden_width],
            down[0],
            *shared[0],
        )
        for qkv, up, _, down, shared in layer_totals
    ]
    stacked = tuple(
        jnp.stack([layer_totals[layer][index] for layer in range(layer_count)])
        for index in range(10)
    )
    return (output, ungrouped(grad_current), *stacked)


def solution(mesh):
    rows = P(AXES, None)
    matrix = P(None, AXES, None)
    vector = P(None, AXES)
    return jax.shard_map(
        body,
        mesh=mesh,
        in_specs=(
            rows,
            matrix,
            matrix,
            matrix,
            matrix,
            matrix,
            vector,
            vector,
            vector,
            vector,
            vector,
            P("seq"),
            P("seq", None),
            P("seq", None, None, None),
            P("seq", None, None, None),
            rows,
            rows,
        ),
        out_specs=(
            rows,
            rows,
            matrix,
            matrix,
            matrix,
            matrix,
            matrix,
            vector,
            vector,
            vector,
            vector,
            vector,
        ),
        check_vma=False,
    )
```
